32 devices in a mesh: seq: 32 (over z, y, x, core), head: 1.
Axes of the slice: x: 2, y: 2, z: 4, core: 2. Of those that a mesh axis runs over, the one named last changes fastest.
Arguments:
- queries: bfloat16 [4096, 128], P('seq'), may hold values from -6 to 6
- key_rows: bfloat16 [4096, 128], P('seq'), may hold values from -0.01171875 to 0.01171875
- values: bfloat16 [4096, 5120], P('seq', 'head'), may hold values from -6 to 6
- gate_rows: bfloat16 [4096, 5120], P('seq', 'head'), may hold values from -6 to 6
- log_decay: float32 [4096, 80], P('seq', 'head'), may hold values from -0.69 to 0
- skip_gain: float32 [80], P('head'), may hold values from 0.3 to 4.2
- lam_index: int32 [4096], P('seq'), may hold values from 0 to 63
- segments: int32 [4096], P('seq'), may hold values from 0 to 127, never falling along the last dimension, each value on 1 to 64 neighbouring positions
- lam_table: float32 [64, 7, 80], P(None, None, 'head'), may hold values from 0.2 to 2
- norm_gain: float32 [5120], P('head'), may hold values from 0.25 to 1.75
- out_proj: bfloat16 [5120, 2560], P('head', 'seq'), may hold values from -0.078125 to 0.078125
Outputs:
- mixer_out: bfloat16 [4096, 2560], P(('seq', 'head'))
The draws below stay inside these ranges and needn't reach their ends.
Inputs may be any that keep to these rules, and one draw needn't show every extreme that they name: `segments`: stretch numbers never fall along the sequence; each stretch has 1 to 64 tokens.
All inputs are finite; a program needn't handle non-finite values.
Results may differ from the reference program's by a relative error of at most 0.012.
Values may be sent and summed in bfloat16 or wider, within the bound.
A program may use at most 128 MiB of HBM per device.

```python
import math
import jax
import jax.numpy as jnp
import numpy as np
from jax import lax

DM = 2560
HEAD_TOTAL = 80
HEAD_DIM = 64
STATE = 128
TOK_DEV = 128
CLASSES = 64
LOGS = 5
LEVELS = 7
DI = 5120
GROUP_COLS = 5120
TOKEN_TOTAL = 4096


def draw_log_decay(key, part):
    key_sequence = jax.random.split(jax.random.fold_in(key, 11), 7)
    fast_share = 0.35
    fast_heads = jax.random.bernoulli(key_sequence[0], fast_share, (HEAD_TOTAL,))
    fast_rate = jax.random.uniform(key_sequence[1], (HEAD_TOTAL,), jnp.float32, 1.0 / 50.0, 1.0 / 30.0)
    slow_total = jax.random.uniform(key_sequence[2], (HEAD_TOTAL,), jnp.float32, 0.05, 0.4)
    baseline_rate = jnp.where(fast_heads, fast_rate, slow_total / TOKEN_TOTAL)
    token_multiplier = jnp.exp(jax.random.uniform(key_sequence[3], (TOKEN_TOTAL, HEAD_TOTAL), jnp.float32, -math.log(2.0), math.log(2.0)))
    shard_multiplier = jnp.exp(jax.random.uniform(key_sequence[4], (TOKEN_TOTAL // TOK_DEV, HEAD_TOTAL), jnp.float32, -math.log(2.0), math.log(2.0)))
    shard_multiplier = jnp.repeat(shard_multiplier, TOK_DEV, axis=0)
    spike_positions = jax.random.randint(key_sequence[5], (2,), 0, TOKEN_TOTAL)
    spike_rows = jnp.any(jnp.arange(TOKEN_TOTAL, dtype=jnp.int32)[:, None] == spike_positions[None, :], axis=1)
    spike_loss = jnp.log(1.0 - jax.random.uniform(key_sequence[6], (TOKEN_TOTAL, HEAD_TOTAL), jnp.float32, 0.2, 0.45))
    final_result = -baseline_rate[None, :] * token_multiplier * shard_multiplier + jnp.where(spike_rows[:, None], spike_loss, 0.0)
    return jnp.maximum(final_result, -0.69).astype(jnp.float32)


def draw_skip_gain(key, part):
    base_gain = jnp.exp(jnp.linspace(math.log(0.5), math.log(2.5), HEAD_TOTAL))
    jitter = jax.random.uniform(jax.random.fold_in(key, 23), (HEAD_TOTAL,), jnp.float32, -0.3, 0.3)
    return (base_gain * jnp.exp(jitter)).astype(jnp.float32)


def with_ends(drawn, rng, least, top_value):
    index_at = [jax.random.randint(jax.random.fold_in(rng, axis), (), 0, length) for axis, length in enumerate(drawn.shape)]
    main_axis = drawn.shape.index(max(drawn.shape))
    beside = index_at[:main_axis] + [(index_at[main_axis] + 1) % drawn.shape[main_axis]] + index_at[main_axis + 1:]
    return drawn.at[tuple(index_at)].set(least).at[tuple(beside)].set(top_value)


def levels(rng, shape, pieces, least, top_value):
    level = 1.0
    for position, shards_of in pieces:
        steps = jax.random.uniform(jax.random.fold_in(jax.random.fold_in(rng, 6), position), (shards_of,), jnp.float32, least / len(pieces), top_value / len(pieces))
        level = level * jnp.repeat(jnp.exp(steps), shape[position] // shards_of).reshape((-1,) + (1,) * (len(shape) - 1 - position))
    return level


def length_profile(number_of, total, bound, lean):
    weights = [(1 << 20) // math.isqrt(standing ** lean) + 1 for standing in range(2, number_of + 1)]
    surplus, holding = total - bound - (number_of - 1), [1] * (number_of - 1)
    while surplus > 0:
        movable = [i for i in range(number_of - 1) if holding[i] < bound]
        whole, remaining = sum([weights[i] for i in movable]), surplus
        for i in movable:
            addition = min(bound - holding[i], max(1, remaining * weights[i] // whole), surplus)
            holding[i] = holding[i] + addition
            surplus = surplus - addition
    return np.array([bound] + holding)


def uneven(own_key, count, total, bound, lean):
    if count == 2:
        one = jax.random.randint(own_key, (), max(1, total - bound), min(bound, total - 1) + 1)
        return jnp.stack([one, total - one])
    sizes = jnp.asarray(length_profile(count, total, bound, lean), jnp.int32)
    twos = (count - 1) // 2
    giver, sink = sizes[1:1 + 2 * twos:2], sizes[2:2 + 2 * twos:2]
    room = jnp.minimum(giver - 1, bound - sink)
    passed = jax.random.randint(jax.random.fold_in(own_key, 1), (twos,), 0, 1 << 20) % (room + 1)
    sizes = sizes.at[1:1 + 2 * twos:2].set(giver - passed).at[2:2 + 2 * twos:2].set(sink + passed)
    return sizes[jax.random.permutation(jax.random.fold_in(own_key, 2), count)]


def centred(own_key, shape, deviation, reach, shards=(), kind=jnp.bfloat16):
    gain = levels(own_key, shape, shards, -0.22, 0.18) if shards else 1.0
    drawn = jax.random.normal(own_key, shape, jnp.float32) * deviation * gain
    return jnp.minimum(jnp.maximum(drawn, -reach), reach).astype(kind)


def setup_inputs(seed: int = 0) -> dict:
    key_list = jax.random.split(jax.random.key(seed), 12)
    return {
        "queries": centred(key_list[0], (TOKEN_TOTAL, STATE), 1.0, 6.0, ((0, 32),)),
        "key_rows": centred(key_list[1], (TOKEN_TOTAL, STATE), ((STATE * TOKEN_TOTAL // 2) ** -0.5), 0.01171875, ((0, 32),)),
        "values": centred(key_list[2], (TOKEN_TOTAL, DI), 1.0, 6.0, ((0, 32),)),
        "gate_rows": centred(key_list[3], (TOKEN_TOTAL, DI), 1.0, 6.0, ((0, 32),)),
        "log_decay": draw_log_decay(jax.random.fold_in(key_list[11], 71), 0),
        "skip_gain": draw_skip_gain(jax.random.fold_in(key_list[11], 71), 0),
        "lam_index": with_ends(jax.random.randint(key_list[6], (TOKEN_TOTAL,), 0, CLASSES), jax.random.fold_in(key_list[6], 1), 0, CLASSES - 1).astype(jnp.int32),
        "segments": jnp.searchsorted(jnp.cumsum(uneven(key_list[7], TOKEN_TOTAL // 32, TOKEN_TOTAL, 64, 1)), jnp.arange(TOKEN_TOTAL), side="right").astype(jnp.int32),
        "lam_table": jnp.clip(jnp.exp(jax.random.uniform(key_list[8], (CLASSES, LEVELS, HEAD_TOTAL), jnp.float32, math.log(0.2), math.log(2.0))), 0.2, 2.0),
        "norm_gain": jnp.clip(1.0 + 0.15 * jax.random.normal(key_list[9], (DI,), jnp.float32), 0.25, 1.75),
        "out_proj": centred(key_list[10], (DI, DM), DI ** -0.5, 0.078125, ((1, 32),)),
    }


epsilon = 1e-05
highest = lax.Precision.HIGHEST

def level_up(group_bf, bounds, level_pos, head_dim):
    pair_count = group_bf.shape[0] // 2
    width = 2 ** level_pos
    upper_start = (2 * jnp.arange(pair_count, dtype=jnp.int32) + 1) * width
    span = bounds[upper_start + width] - bounds[upper_start]
    pairs = group_bf.reshape(pair_count, 2, group_bf.shape[1], group_bf.shape[2]).astype(jnp.float32)
    factor = jnp.repeat(jnp.exp(span), head_dim, axis=1)[:, None, :]
    return (pairs[:, 1] + factor * pairs[:, 0]).astype(jnp.bfloat16)

def reference(queries, key_rows, values, gate_rows, log_decay, skip_gain, lam_index, segments, lam_table, norm_gain, out_proj):
    shard_count = TOKEN_TOTAL // TOK_DEV
    q_all = queries.reshape(shard_count, TOK_DEV, STATE)
    k_all = key_rows.reshape(shard_count, TOK_DEV, STATE)
    v_all = values.reshape(shard_count, TOK_DEV, DI)
    z_all = gate_rows.reshape(shard_count, TOK_DEV, DI)
    cum_all = jnp.cumsum(log_decay.reshape(shard_count, TOK_DEV, HEAD_TOTAL), axis=1)
    onehot = (lam_index[:, None] == jnp.arange(CLASSES, dtype=jnp.int32)[None, :]).astype(jnp.float32)
    level_wts = jnp.dot(onehot, lam_table.reshape(CLASSES, LEVELS * HEAD_TOTAL), precision=highest)
    level_wts = level_wts.reshape(shard_count, TOK_DEV, LEVELS, HEAD_TOTAL)
    seg_all = segments.reshape(shard_count, TOK_DEV)

    def end_state(args):
        k_blk, v_blk, c_blk = args
        decay_end = jnp.repeat(jnp.exp(c_blk[-1][None, :] - c_blk), HEAD_DIM, axis=1)
        decayed = (v_blk.astype(jnp.float32) * decay_end).astype(jnp.bfloat16)
        return jnp.dot(k_blk.T, decayed, preferred_element_type=jnp.float32).astype(jnp.bfloat16)
    end_states = lax.map(end_state, (k_all, v_all, cum_all))
    bounds = jnp.concatenate([jnp.zeros((1, HEAD_TOTAL), jnp.float32), jnp.cumsum(cum_all[:, -1, :], axis=0)], axis=0)
    group_levels = [end_states]
    for level_pos in range(LOGS - 1):
        group_levels.append(level_up(group_levels[-1], bounds, level_pos, HEAD_DIM))
    shard_ids = jnp.arange(shard_count, dtype=jnp.int32)
    positions = jnp.arange(TOK_DEV, dtype=jnp.int32)
    causal = positions[:, None] >= positions[None, :]

    def shard_out(args):
        shard_pos, q_blk, k_blk, v_blk, z_blk, c_blk, w_blk, s_blk = args
        here_bound = bounds[shard_pos]
        bucket_list = []
        for level_pos in range(LOGS):
            is_upper = jnp.bitwise_and(jnp.right_shift(shard_pos, level_pos), 1) == 1
            group_idx = jnp.right_shift(shard_pos, level_pos)
            start_row = jnp.left_shift(group_idx, level_pos)
            sibling = lax.dynamic_index_in_dim(group_levels[level_pos], jnp.maximum(group_idx - 1, 0), 0, keepdims=False)
            factor = jnp.repeat(jnp.exp(here_bound - bounds[start_row]), HEAD_DIM)[None, :]
            bucket_list.append(jnp.where(is_upper, factor * sibling.astype(jnp.float32), 0.0))
        buckets = jnp.stack(bucket_list)
        scores = jnp.dot(q_blk, k_blk.T, preferred_element_type=jnp.float32)
        c_heads = c_blk.T
        log_gaps = jnp.where(causal[None], c_heads[:, :, None] - c_heads[:, None, :], -jnp.inf)
        same_seg = s_blk[:, None] == s_blk[None, :]
        level_w = jnp.where(same_seg[None], w_blk[:, 0, :].T[:, :, None], w_blk[:, 1, :].T[:, :, None])
        weights_bf = (scores[None] * jnp.exp(log_gaps) * level_w).astype(jnp.bfloat16)
        v_heads = v_blk.reshape(TOK_DEV, HEAD_TOTAL, HEAD_DIM)
        local_out = jnp.einsum('htj,jhp->thp', weights_bf.astype(jnp.float32), v_heads.astype(jnp.float32), precision=highest)
        local_out = local_out.reshape(TOK_DEV, DI)
        level_reads = jnp.einsum('tn,lnc->tlc', q_blk.astype(jnp.float32), buckets, precision=highest)
        read_wts = jnp.repeat(w_blk[:, 2:, :], HEAD_DIM, axis=2)
        cross_out = lax.optimization_barrier(jnp.sum(level_reads * read_wts, axis=1)) * jnp.repeat(jnp.exp(c_blk), HEAD_DIM, axis=1)
        mixer_sum = local_out + cross_out + jnp.repeat(skip_gain, HEAD_DIM)[None, :] * v_blk.astype(jnp.float32)
        gated = mixer_sum * jax.nn.silu(z_blk.astype(jnp.float32))
        inv_rms = lax.rsqrt(lax.optimization_barrier(jnp.mean(gated * gated, axis=1, keepdims=True)) + epsilon)
        return (gated * inv_rms * norm_gain[None, :]).astype(jnp.bfloat16)
    hidden = lax.map(shard_out, (shard_ids, q_all, k_all, v_all, z_all, cum_all, level_wts, seg_all))
    hidden = hidden.reshape(TOKEN_TOTAL, DI)
    total_out = jnp.zeros((TOKEN_TOTAL, DM), jnp.float32)
    for group_pos in range(DI // GROUP_COLS):
        low_col = group_pos * GROUP_COLS
        partial_value = jnp.dot(hidden[:, low_col:low_col + GROUP_COLS], out_proj[low_col:low_col + GROUP_COLS], preferred_element_type=jnp.float32)
        total_out = total_out + lax.optimization_barrier(partial_value.astype(jnp.bfloat16)).astype(jnp.float32)
    return total_out.astype(jnp.bfloat16)
```

```python
import math

import jax
import jax.numpy as jnp
from jax import lax
from jax.experimental import pallas as pl
from jax.experimental.pallas import tpu as pltpu
from jax.sharding import PartitionSpec as P

epsilon = 1e-05
highest = lax.Precision.HIGHEST
f32 = jnp.float32
bf16 = jnp.bfloat16


def xor_permute(value, mask):
    pairs = [(source, source ^ mask) for source in range(lax.axis_size("seq"))]
    return lax.ppermute(value, "seq", pairs)


def widen(matrix, head_dim):
    return jnp.repeat(matrix, head_dim, axis=-1)


def pack_kernel(groups, q_ref, k_ref, x_ref, decay_ref, lam_ref, seg_ref, out_ref):
    tok, state_dim = q_ref.shape
    cg = x_ref.shape[1] // groups
    hg = decay_ref.shape[1] // groups
    t_pos = lax.broadcasted_iota(jnp.int32, (tok, tok), 0)
    j_pos = lax.broadcasted_iota(jnp.int32, (tok, tok), 1)
    ones = jnp.where(t_pos >= j_pos, 1.0, 0.0).astype(f32)
    cum = jnp.dot(ones, decay_ref[...], precision=highest, preferred_element_type=f32)
    first = cum.astype(bf16).astype(f32)
    second = (cum - first).astype(bf16).astype(f32)
    third = cum - first - second
    pad = out_ref.shape[2] - 2 * state_dim - cg - 3 * hg - 2
    tail = [lam_ref[...], seg_ref[...], jnp.zeros((tok, pad), f32)]
    for s in range(groups):
        out_ref[s, :, :state_dim] = q_ref[...]
        out_ref[s, :, state_dim : 2 * state_dim] = k_ref[...]
        out_ref[s, :, 2 * state_dim : 2 * state_dim + cg] = x_ref[:, s * cg : (s + 1) * cg]
        parts = [part[:, s * hg : (s + 1) * hg] for part in (first, second, third)]
        small = jnp.concatenate(parts + tail, axis=1)
        out_ref[s, :, 2 * state_dim + cg :] = small.astype(bf16)


def pack_call(queries, key_rows, values, log_decay, lam, seg, *, groups):
    tok, state_dim = queries.shape
    width = 2 * state_dim + values.shape[1] // groups + 3 * (log_decay.shape[1] // groups) + 2
    vmem = pl.BlockSpec(memory_space=pltpu.VMEM)
    return pl.pallas_call(
        lambda *refs: pack_kernel(groups, *refs),
        out_shape=jax.ShapeDtypeStruct((groups, tok, pl.cdiv(width + 1, 128) * 128), bf16),
        in_specs=[vmem] * 6,
        out_specs=vmem,
        name="pack",
        cost_estimate=pl.CostEstimate(
            flops=1 << 22, bytes_accessed=4 << 20, transcendentals=0
        ),
    )(queries, key_rows, values, log_decay, lam, seg)


def spread(scale, expand):
    high = scale.astype(bf16)
    low = (scale - high.astype(f32)).astype(bf16)
    return jnp.dot(high, expand, preferred_element_type=f32) + jnp.dot(
        low, expand, preferred_element_type=f32
    )


def state_kernel(bits, state_dim, packed_ref, scale_ref, up_ref, expand_ref, *outs):
    A = packed_ref.shape[0]
    expand = expand_ref[...]
    up_wide = spread(up_ref[...], expand)
    for s in range(A):
        decayed = packed_ref[s, :, 2 * state_dim : 2 * state_dim + expand.shape[1]].astype(f32) * spread(scale_ref[s], expand)
        keys = packed_ref[s, :, state_dim : 2 * state_dim]
        outs[0][s] = lax.dot_general(
            keys,
            decayed.astype(bf16),
            (((0,), (0,)), ((), ())),
            preferred_element_type=f32,
        ).astype(bf16)
    row = 0
    for b in range(bits):
        for g in range(A >> (b + 1)):
            low = outs[b][2 * g].astype(f32)
            high = outs[b][2 * g + 1].astype(f32)
            merged = (high + up_wide[row : row + 1] * low).astype(bf16)
            if b + 1 < bits:
                outs[b + 1][g] = merged
            else:
                outs[b + 1][...] = merged
            row += 1


def state_call(packed, end_scale, up_rows, expand, *, state_dim, bits):
    A = packed.shape[0]
    cg = expand.shape[1]
    shapes = [(A >> b, state_dim, cg) for b in range(bits)] + [(state_dim, cg)]
    vmem = pl.BlockSpec(memory_space=pltpu.VMEM)
    return pl.pallas_call(
        lambda *refs: state_kernel(bits, state_dim, *refs),
        out_shape=[jax.ShapeDtypeStruct(shape, bf16) for shape in shapes],
        in_specs=[vmem] * 4,
        out_specs=[vmem] * len(shapes),
        name="group_states",
        cost_estimate=pl.CostEstimate(
            flops=1 << 29, bytes_accessed=8 << 20, transcendentals=0
        ),
    )(packed, end_scale, up_rows, expand)


def local_kernel(
    state_dim, head_dim, bits, packed_ref, cum_ref, cum_t_ref, scale_ref, seg_ref,
    seg_t_ref, skip_ref, expand_ref, *rest
):
    states, out_ref = rest[:bits], rest[bits]
    tok, hg = cum_ref.shape[1:]
    cg = expand_ref.shape[1]
    q = packed_ref[0, :, :state_dim]
    keys = packed_ref[0, :, state_dim : 2 * state_dim]
    expand = expand_ref[...]
    scores = lax.dot_general(
        q, keys, (((1,), (1,)), ((), ())), preferred_element_type=f32
    )
    same = seg_ref[0] == seg_t_ref[0]
    t_pos = lax.broadcasted_iota(jnp.int32, (tok, tok), 0)
    j_pos = lax.broadcasted_iota(jnp.int32, (tok, tok), 1)
    causal = t_pos >= j_pos
    scales = scale_ref[0]
    cum = cum_ref[0]
    cum_t = cum_t_ref[0]
    x_wide = packed_ref[0, :, 2 * state_dim : 2 * state_dim + cg]
    acc = skip_ref[...] * x_wide.astype(f32)
    for b in range(bits):
        read = jnp.dot(q, states[b][0], preferred_element_type=f32)
        acc = acc + read * spread(scales[:, (2 + b) * hg : (3 + b) * hg], expand)
    out_ref[...] = acc

    def head_weights(h):
        gaps = jnp.where(causal, cum[:, h : h + 1] - cum_t[h : h + 1, :], -jnp.inf)
        level_w = jnp.where(same, scales[:, h : h + 1], scales[:, hg + h : hg + h + 1])
        return (scores * jnp.exp(gaps) * level_w).astype(bf16)

    per_tile = max(1, 128 // head_dim)
    for first in range(0, hg, per_tile):
        heads = range(first, min(first + per_tile, hg))
        low, high = first * head_dim, min((first + per_tile) * head_dim, cg)
        x_tile = x_wide[:, low:high]
        lane_head = lax.broadcasted_iota(jnp.int32, (tok, high - low), 1) // head_dim
        tile = None
        for h in heads:
            part = jnp.dot(head_weights(h), x_tile, preferred_element_type=f32)
            tile = part if tile is None else jnp.where(lane_head == h - first, part, tile)
        out_ref[:, low:high] += tile


def local_call(
    packed, cum, cum_t, scales, seg, level_states, skip, expand, *, state_dim, head_dim
):
    A, tok, width = packed.shape
    cg = expand.shape[1]
    hg = cum.shape[2]
    bits = len(level_states)

    def shard_spec(*dims):
        return pl.BlockSpec((1,) + dims, lambda s: (s, 0, 0))

    def sibling_spec(b):
        return pl.BlockSpec(
            (1, state_dim, cg), lambda s: (jnp.maximum(s // 2**b - 1, 0), 0, 0)
        )

    def whole_spec(shape):
        return pl.BlockSpec(shape, lambda s: (0, 0))

    return pl.pallas_call(
        lambda *refs: local_kernel(state_dim, head_dim, bits, *refs),
        grid=(A,),
        out_shape=jax.ShapeDtypeStruct((A * tok, cg), f32),
        in_specs=[
            shard_spec(tok, width),
            shard_spec(tok, hg),
            shard_spec(hg, tok),
            shard_spec(tok, scales.shape[2]),
            shard_spec(tok, 1),
            shard_spec(1, tok),
            whole_spec((1, cg)),
            whole_spec(expand.shape),
        ]
        + [sibling_spec(b) for b in range(bits)],
        out_specs=pl.BlockSpec((tok, cg), lambda s: (s, 0)),
        name="local_mix",
        cost_estimate=pl.CostEstimate(
            flops=1 << 32, bytes_accessed=12 << 20, transcendentals=1 << 21
        ),
    )(packed, cum, cum_t, scales, seg[:, :, None], seg[:, None, :], skip, expand, *level_states)


def gate_kernel(levels, packed_ref, mixed_ref, scale_ref, gates_ref, gain_ref, expand_ref, *rest):
    others, (hidden_ref, square_ref) = rest[:levels], rest[levels:]
    hg = expand_ref.shape[0]
    q = packed_ref[0]
    expand = expand_ref[...]
    scales = scale_ref[0]
    acc = mixed_ref[...]
    for level in range(levels):
        read = jnp.dot(q, others[level][...], preferred_element_type=f32)
        acc = acc + read * spread(scales[:, level * hg : (level + 1) * hg], expand)
    gate = gates_ref[0].astype(f32)
    gated = acc * (gate / (1.0 + jnp.exp(-gate)))
    square_ref[0] = jnp.sum(gated * gated, axis=1, keepdims=True)
    hidden_ref[...] = (gated * gain_ref[...]).astype(bf16)


def gate_call(packed, mixed, others, other_scales, gates, gain, expand, *, state_dim):
    A, tok, cg = gates.shape
    levels = len(others)
    scales = jnp.concatenate(other_scales, axis=2)

    def shard_spec(*dims):
        return pl.BlockSpec((1,) + dims, lambda s: (s, 0, 0))

    def whole_spec(shape):
        return pl.BlockSpec(shape, lambda s: (0, 0))

    rows_spec = pl.BlockSpec((tok, cg), lambda s: (s, 0))
    return pl.pallas_call(
        lambda *refs: gate_kernel(levels, *refs),
        grid=(A,),
        out_shape=[
            jax.ShapeDtypeStruct((A * tok, cg), bf16),
            jax.ShapeDtypeStruct((A, tok, 1), f32),
        ],
        in_specs=[
            shard_spec(tok, state_dim),
            rows_spec,
            shard_spec(tok, scales.shape[2]),
            shard_spec(tok, cg),
            whole_spec((1, cg)),
            whole_spec(expand.shape),
        ]
        + [whole_spec((state_dim, cg))] * levels,
        out_specs=[rows_spec, shard_spec(tok, 1)],
        name="gate_mix",
        cost_estimate=pl.CostEstimate(
            flops=1 << 30, bytes_accessed=8 << 20, transcendentals=1 << 20
        ),
    )(packed, mixed, scales, gates, gain, expand, *others)


MESH = pl.DeviceIdType.MESH
decay_floor = -0.69


def bit_of(pos, b):
    return lax.rem(lax.div(pos, 2**b), 2)


def flip(pos, mask):
    out = pos
    for b in range(mask.bit_length()):
        if (mask >> b) & 1:
            out = out + (1 - 2 * bit_of(pos, b)) * 2**b
    return out


def flip_traced(pos, step, bits):
    out = 0
    for b in range(bits):
        out = out + lax.rem(bit_of(pos, b) + bit_of(step, b), 2) * 2**b
    return out


def dot_f32(a, b, dims=(((1,), (0,)), ((), ())), precision=None):
    return lax.dot_general(a, b, dims, precision=precision, preferred_element_type=f32)


NT = (((1,), (1,)), ((), ()))
TN = (((0,), (0,)), ((), ()))


class Sizes:
    def __init__(self, tok, state, cg, hg, oc, A, Z, levels):
        self.tok, self.state, self.cg, self.hg, self.oc = tok, state, cg, hg, oc
        self.A, self.Z, self.levels = A, Z, levels
        self.a_bits = A.bit_length() - 1
        self.z_bits = Z.bit_length() - 1
        self.hr = pl.cdiv(hg, 16) * 16
        self.half = tok // 2
        self.head_dim = cg // hg


def mixer_kernel(
    sz, wt_ref, v_ref, g_ref, q_ref, k_ref, dec_ref, lam_ref, seg_ref, tab_ref, skip_ref, gain_ref,
    out_ref,
    wbuf, xbuf, gbuf, qkbuf, smsend, smbuf, pre, aft, lwbuf, acc, lev, pst, zsend, zrecv, tsend, trecv,
    hid, sqsend, sqrecv, expand, snd, rcv, keep,
    w_s, w_r, up_s, up_r, dn_s, dn_r, qk_s, qk_r, sm_s, sm_r, x_s, x_r, g_s, g_r,
    zs_s, zs_r, zt_s, zt_r, sq_s, sq_r, c_s, c_r,
):
    A, Z, tok, cg, hg, hr, oc = sz.A, sz.Z, sz.tok, sz.cg, sz.hg, sz.hr, sz.oc
    state, a_bits, z_bits, half, levels = sz.state, sz.a_bits, sz.z_bits, sz.half, sz.levels
    me = lax.axis_index("seq")
    p = lax.rem(me, A)
    z = lax.div(me, A)
    waits = []

    def dev(zz, pp):
        return {"seq": zz * A + pp}

    def cols(pos):
        return pl.ds(pl.multiple_of(pos * cg, cg), cg)

    def remote(src, dst, send, recv, device):
        return pltpu.make_async_remote_copy(
            src_ref=src, dst_ref=dst, send_sem=send, recv_sem=recv,
            device_id=device, device_id_type=MESH,
        )

    barrier = pltpu.get_barrier_semaphore()
    for d in range(1, A):
        pl.semaphore_signal(barrier, inc=1, device_id=dev(z, flip(p, d)), device_id_type=MESH)
    for dz in range(1, Z):
        pl.semaphore_signal(barrier, inc=1, device_id=dev(lax.rem(z + dz, Z), p), device_id_type=MESH)
    own_w = pltpu.make_async_copy(wt_ref.at[:, cols(p)], wbuf.at[z, p], w_r.at[0])
    own_x = pltpu.make_async_copy(v_ref.at[:, cols(p)], xbuf.at[p], x_r.at[0])
    own_g = pltpu.make_async_copy(g_ref.at[:, cols(p)], gbuf.at[p], g_r.at[0])
    own_w.start()
    own_x.start()
    own_g.start()
    qkbuf[p, 0] = q_ref[...]
    qkbuf[p, 1] = k_ref[...].astype(f32).T.astype(bf16)
    heads = dec_ref.shape[0]
    row_id = lax.broadcasted_iota(jnp.int32, (A * hr, heads), 0)
    head_id = lax.broadcasted_iota(jnp.int32, (A * hr, heads), 1)
    local_row = lax.rem(row_id, hr)
    place = (local_row < hg) & (lax.div(row_id, hr) * hg + local_row == head_id)
    placed = dot_f32(jnp.where(place, 1.0, 0.0).astype(f32), dec_ref[...], precision=highest)
    j_pos = lax.broadcasted_iota(jnp.int32, (tok, tok), 0)
    t_pos = lax.broadcasted_iota(jnp.int32, (tok, tok), 1)
    cum_all = dot_f32(placed, jnp.where(j_pos <= t_pos, 1.0, 0.0).astype(f32), precision=highest)
    for s in range(A):
        smsend[s, :hr] = cum_all[s * hr : (s + 1) * hr]
        smsend[s, hr : hr + 1] = lam_ref[...].astype(f32)
        smsend[s, hr + 1 : hr + 2] = seg_ref[...].astype(f32)
        smsend[s, hr + 2 : hr + 8] = jnp.zeros((6, tok), f32)
    smbuf[p] = smsend[p]
    pl.semaphore_wait(barrier, A - 1 + Z - 1)

    def start(copy):
        copy.start()
        waits.append(copy)
        return copy

    order = list(range(1, A))
    w_cp, qk_cp, sm_cp, x_cp, g_cp = {}, {}, {}, {}, {}
    for d in order:
        t = flip(p, d)
        w_cp[d] = start(remote(wt_ref.at[:, cols(t)], wbuf.at[z, p], w_s.at[d], w_r.at[d], dev(z, t)))
    for d in order:
        t = flip(p, d)
        sm_cp[d] = start(remote(smsend.at[t], smbuf.at[p], sm_s.at[d], sm_r.at[d], dev(z, t)))
        qk_cp[d] = start(remote(qkbuf.at[p], qkbuf.at[p], qk_s.at[d], qk_r.at[d], dev(z, t)))
    for d in order:
        t = flip(p, d)
        x_cp[d] = start(remote(v_ref.at[:, cols(t)], xbuf.at[p], x_s.at[d], x_r.at[d], dev(z, t)))

    pick_row = lax.broadcasted_iota(jnp.int32, (hr, heads), 0)
    pick_head = lax.broadcasted_iota(jnp.int32, (hr, heads), 1)
    pick = jnp.where((pick_row < hg) & (pick_row + p * hg == pick_head), 1.0, 0.0).astype(f32)
    table = jnp.concatenate(
        [dot_f32(pick, tab_ref[l], NT, precision=highest) for l in range(levels)], axis=0
    )
    e_row = lax.broadcasted_iota(jnp.int32, (2 * hr, cg), 0)
    e_col = lax.broadcasted_iota(jnp.int32, (2 * hr, cg), 1)
    expand[...] = jnp.where(lax.rem(e_row, hr) == lax.div(e_col, sz.head_dim), 1.0, 0.0).astype(bf16)

    def spread(rows):
        high = rows.astype(bf16)
        low = (rows - high.astype(f32)).astype(bf16)
        return dot_f32(jnp.concatenate([high, low], axis=0), expand[...], TN)

    def spread_row(column):
        return spread(jnp.broadcast_to(column, (hr, 8)))[:1]

    skip_rows = jnp.sum(pick * skip_ref[...], axis=1, keepdims=True)
    skip_wide = spread_row(skip_rows)
    gain = gain_ref[:, cols(p)]

    def up_copy(h, src, sem):
        return remote(src, src, up_s.at[sem], up_r.at[sem], dev(z + 1, p))

    def dn_copy(h, src, sem):
        return remote(src, src, dn_s.at[sem], dn_r.at[sem], dev(z - 1, p))

    def pieces(d):
        s = flip(p, d)
        return wbuf.at[z, s]

    for d in range(A):
        if d == 0:
            own_w.wait()
        else:
            w_cp[d].wait_recv()

        @pl.when(z + 1 < Z)
        def _():
            up_copy(0, pieces(d), d).start()

        @pl.when(z >= 1)
        def _():
            dn_copy(0, pieces(d), d).start()

    def hop(h):
        @pl.when(z - 1 - h >= 0)
        def _():
            zb = z - 1 - h
            if h == 0:
                for d in range(A):
                    up_copy(0, wbuf.at[zb, flip(p, d)], d).wait_recv()
            else:
                up_copy(h, wbuf.at[zb], A - 1 + h).wait_recv()

        @pl.when((z - 1 - h >= 0) & (z + 1 < Z))
        def _():
            up_copy(h + 1, wbuf.at[z - 1 - h], A + h).start()

        @pl.when(z + 1 + h < Z)
        def _():
            zb = z + 1 + h
            if h == 0:
                for d in range(A):
                    dn_copy(0, wbuf.at[zb, flip(p, d)], d).wait_recv()
            else:
                dn_copy(h, wbuf.at[zb], A - 1 + h).wait_recv()

        @pl.when((z + 1 + h < Z) & (z >= 1))
        def _():
            dn_copy(h + 1, wbuf.at[z + 1 + h], A + h).start()

    def hop_sends_done():
        @pl.when(z + 1 < Z)
        def _():
            for d in range(A):
                up_copy(0, wbuf.at[z, d], d).wait_send()

        @pl.when(z >= 1)
        def _():
            for d in range(A):
                dn_copy(0, wbuf.at[z, d], d).wait_send()

        for h in range(Z - 2):
            @pl.when((z - 1 - h >= 0) & (z + 1 < Z))
            def _():
                up_copy(h + 1, wbuf.at[z - 1 - h], A + h).wait_send()

            @pl.when((z + 1 + h < Z) & (z >= 1))
            def _():
                dn_copy(h + 1, wbuf.at[z + 1 + h], A + h).wait_send()

    for d in order:
        sm_cp[d].wait_recv()
    ends = [smbuf[s, :hr, tok - 1 : tok] for s in range(A)]
    running = jnp.zeros((hr, 1), f32)
    for s in range(A):
        pre[s] = jnp.broadcast_to(running, (hr, tok))
        running = running + ends[s]
    total = running
    running = jnp.zeros((hr, 1), f32)
    for s in reversed(range(A)):
        aft[s] = jnp.broadcast_to(running, (hr, tok))
        running = running + ends[s]

    for d in order:
        t = flip(p, d)
        g_cp[d] = start(remote(g_ref.at[:, cols(t)], gbuf.at[p], g_s.at[d], g_r.at[d], dev(z, t)))

    causal = j_pos >= t_pos
    class_id = lax.broadcasted_iota(jnp.int32, (tab_ref.shape[1], tok), 0).astype(f32)
    pst[...] = jnp.zeros(pst.shape, f32)

    def first_pass(s):
        c = smbuf[s, :hr]
        onehot = jnp.where(smbuf[s, hr : hr + 1] == class_id, 1.0, 0.0).astype(f32)
        lw = dot_f32(table, onehot, precision=highest)
        lwbuf[s] = lw
        seg_row = jnp.broadcast_to(smbuf[s, hr + 1 : hr + 2], (tok, tok))
        same = seg_row == seg_row.T
        scores = dot_f32(qkbuf[s, 0], qkbuf[s, 1])
        s_same = jnp.where(causal & same, scores, 0.0).astype(bf16)
        s_diff = jnp.where(causal & jnp.logical_not(same), scores, 0.0).astype(bf16)
        mid = c[:, half - 1 : half]
        x = xbuf[s].astype(f32)
        scaled = (x * spread(jnp.exp(mid - c))).astype(bf16)
        big = dot_f32(jnp.concatenate([s_same, s_diff, qkbuf[s, 1]], axis=0), scaled)
        later = jnp.exp(c - mid)
        acc[s] = (
            skip_wide * x
            + spread(later * lw[:hr]) * big[:tok]
            + spread(later * lw[hr : 2 * hr]) * big[tok : 2 * tok]
        )
        end = big[2 * tok :] * spread_row(jnp.exp(c[:, tok - 1 : tok] - mid))
        lev[0][s] = end.astype(bf16)
        pst[...] += end * spread_row(jnp.exp(aft[s, :, :1]))

    for d in range(A):
        if d == 0:
            own_x.wait()
        else:
            x_cp[d].wait_recv()
            qk_cp[d].wait_recv()
        first_pass(flip(p, d))
        if d == 1:
            hop(0)

    def z_copies(b, other):
        return (
            remote(zsend.at[b], zrecv.at[b], zs_s.at[b], zs_r.at[b], dev(other, p)),
            remote(tsend.at[b], trecv.at[b], zt_s.at[b], zt_r.at[b], dev(other, p)),
        )

    def z_send(b, value, tot):
        other = flip(z, 1 << b)
        zsend[b] = value.astype(bf16)
        tsend[b] = jnp.broadcast_to(tot, (hr, tok))
        if b + 1 < z_bits:
            for copy in z_copies(b, other):
                copy.start()
        else:
            @pl.when(bit_of(z, b) == 0)
            def _():
                for copy in z_copies(b, other):
                    copy.start()

    def z_wait(b):
        other = flip(z, 1 << b)
        if b + 1 < z_bits:
            for copy in z_copies(b, other):
                copy.wait()
        else:
            @pl.when(bit_of(z, b) == 0)
            def _():
                for copy in z_copies(b, other):
                    copy.wait_send()

            @pl.when(bit_of(z, b) == 1)
            def _():
                for copy in z_copies(b, other):
                    copy.wait_recv()

    z_send(0, pst[...], total)

    for b in range(a_bits - 1):
        for g in range(A >> (b + 1)):
            if g % 2 == 0:
                up_total = sum(ends[s] for s in range((2 * g + 1) << b, (2 * g + 2) << b))
                merged = lev[b][2 * g + 1].astype(f32) + spread_row(jnp.exp(up_total)) * lev[b][2 * g].astype(f32)
                lev[b + 1][g] = merged.astype(bf16)
            elif b + 2 < a_bits:
                up_total = sum(ends[s] for s in range((2 * g + 1) << b, (2 * g + 2) << b))
                merged = lev[b][2 * g + 1].astype(f32) + spread_row(jnp.exp(up_total)) * lev[b][2 * g].astype(f32)
                lev[b + 1][g] = merged.astype(bf16)
    for s in range(1, A):
        more = None
        for b in range(a_bits):
            if (s >> b) & 1:
                first = (s >> b) << b
                before = sum((ends[j] for j in range(first, s)), jnp.zeros((hr, 1), f32))
                scale = jnp.exp(smbuf[s, :hr] + before) * lwbuf[s, (2 + b) * hr : (3 + b) * hr]
                term = spread(scale) * dot_f32(qkbuf[s, 0], lev[b][(s >> b) - 1])
                more = term if more is None else more + term
        acc[s] += more

    z_prefix = jnp.zeros((hr, tok), f32)
    z_total = jnp.broadcast_to(total, (hr, tok))

    def z_pass(b, z_prefix):
        @pl.when(bit_of(z, b) == 1)
        def _():
            def body(s, carry):
                level = 2 + a_bits + b
                scale = jnp.exp(smbuf[s, :hr] + pre[s] + z_prefix) * lwbuf[s, level * hr : (level + 1) * hr]
                acc[s] += spread(scale) * dot_f32(qkbuf[s, 0], zrecv[b])
                return carry

            lax.fori_loop(0, A, body, 0)

    for b in range(z_bits):
        z_wait(b)
        is_up = bit_of(z, b) == 1
        if b + 1 < z_bits:
            t_other = trecv[b]
            mine, theirs = zsend[b].astype(f32), zrecv[b].astype(f32)
            upper = jnp.where(is_up, mine, theirs)
            lower = jnp.where(is_up, theirs, mine)
            factor = spread_row(jnp.exp(jnp.where(is_up, z_total, t_other)[:, :1]))
            z_send(b + 1, upper + factor * lower, (z_total + t_other)[:, :1])
        z_pass(b, z_prefix)
        if b + 1 < z_bits:
            z_prefix = z_prefix + jnp.where(is_up, t_other, 0.0)
            z_total = z_total + t_other
        if b == 0 and Z > 2:
            hop(1)

    own_g.wait()
    for d in order:
        g_cp[d].wait_recv()

    def gate_pass(s, carry):
        gate = gbuf[s].astype(f32)
        gated = acc[s] * (gate / (1.0 + jnp.exp(-gate)))
        square = gated * gated
        folded = square[:, :128]
        for first in range(128, cg, 128):
            folded = folded + square[:, first : first + 128]
        sqsend[s] = dot_f32(jnp.ones((8, 128), f32), folded, NT, precision=highest)
        hid[lax.div(s, 2), lax.rem(s, 2)] = (gated * gain).astype(bf16)
        return carry

    lax.fori_loop(0, A, gate_pass, 0)
    sq_cp = {}
    for d in order:
        t = flip(p, d)
        sq_cp[d] = start(remote(sqsend.at[t], sqrecv.at[p], sq_s.at[d], sq_r.at[d], dev(z, t)))
    sqrecv[p] = sqsend[p]

    bit0 = bit_of(p, 0)
    sequence = [list(range(a_bits)), [0] + list(range(1, a_bits))[::-1]]

    def block_of(k):
        out = 0
        for zz in range(Z):
            near = sorted(range(Z), key=lambda other: (abs(other - zz), other))
            out = jnp.where(z == zz, near[k], out)
        return out

    def unit(k, th):
        return 2 * k + th

    def stage_copy(t, u, b):
        return remote(
            snd[t].at[u], rcv[t].at[u], c_s.at[t, u], c_r.at[t, u], dev(z, flip(p, 1 << b))
        )

    def multiply(k):
        weights = wbuf[block_of(k)].reshape(Z * 0 + A * oc, cg)
        rows = A // 2 * tok
        rest = (A // 2, 2, half, A * oc)

        def product(bit):
            lhs = hid[:, bit].reshape(rows, cg)
            return dot_f32(lhs, weights, NT).reshape(rest)

        theirs = product(1 - bit0)
        for th in range(2):
            u = unit(k, th)
            snd[0][u] = theirs[:, th].astype(bf16).reshape(snd[0].shape[1:])
            stage_copy(0, u, 0).start()
        mine = product(bit0)
        for th in range(2):
            u = unit(k, th)
            keep[0][u] = mine[:, th].reshape(keep[0].shape[1:])

    def pick_half(ref, u, left, b, bit):
        axis = left.index(b)
        index = (u,) + (slice(None),) * axis + (bit,)
        return ref[index]

    def fold(t, k):
        for th in range(2):
            u = unit(k, th)
            seq = sequence[th]
            left = [b for b in range(a_bits)[::-1] if b not in seq[: t + 1]]
            stage_copy(t, u, seq[t]).wait_recv()
            b = seq[t + 1]
            bit = bit_of(p, b)
            out = pick_half(keep[t], u, left, b, 1 - bit) + pick_half(rcv[t], u, left, b, 1 - bit).astype(f32)
            snd[t + 1][u] = out.astype(bf16)
            stage_copy(t + 1, u, b).start()
            keep[t + 1][u] = pick_half(keep[t], u, left, b, bit) + pick_half(rcv[t], u, left, b, bit).astype(f32)

    def finish(k, inv):
        t = a_bits - 1
        for th in range(2):
            u = unit(k, th)
            stage_copy(t, u, sequence[th][t]).wait_recv()
            value = keep[t][u] + rcv[t][u].astype(f32)
            scale = jnp.concatenate([inv[th * half : (th + 1) * half]] * (A * oc // 128), axis=1)
            first = pl.multiple_of(block_of(k) * (A * oc), 128)
            out_ref[th * half : (th + 1) * half, pl.ds(first, A * oc)] = (value * scale).astype(out_ref.dtype)

    steps = []
    for k in range(Z):
        steps.append((k, 0, k))
        for t in range(a_bits):
            steps.append((k + t + 1, 1 + t, k))
    inv = None
    for _, kind, k in sorted(steps):
        if kind == 0:
            if k == Z - 1 and Z > 1:
                hop(Z - 2)
            multiply(k)
        elif kind < a_bits:
            fold(kind - 1, k)
        else:
            if inv is None:
                for d in order:
                    sq_cp[d].wait_recv()
                gathered = jnp.concatenate([sqrecv[s, :1] for s in range(A)], axis=0)
                sums = dot_f32(gathered, jnp.ones((A, 128), f32), TN, precision=highest)
                inv = lax.rsqrt(sums / (A * cg) + epsilon)
            finish(k, inv)

    for copy in waits:
        copy.wait_send()
    hop_sends_done()
    for k in range(Z):
        for th in range(2):
            for t in range(a_bits):
                stage_copy(t, unit(k, th), sequence[th][t]).wait_send()


def mixer_call(sz, wt, values, gates, queries, keys, decay_t, lam, seg, table, skip, gain):
    A, Z, tok, cg, hr, oc = sz.A, sz.Z, sz.tok, sz.cg, sz.hr, sz.oc
    a_bits, z_bits, half, state = sz.a_bits, sz.z_bits, sz.half, sz.state
    hbm = pl.BlockSpec(memory_space=pl.ANY)
    vmem = pl.BlockSpec(memory_space=pltpu.VMEM)
    units = 2 * Z
    left = [(2,) * (a_bits - 1 - t) + (half, A * oc) for t in range(a_bits)]
    dma = pltpu.SemaphoreType.DMA
    scratch = [
        pltpu.VMEM((Z, A, oc, cg), bf16),
        pltpu.VMEM((A, tok, cg), bf16),
        pltpu.VMEM((A, tok, cg), bf16),
        pltpu.VMEM((A, 2, tok, state), bf16),
        pltpu.VMEM((A, hr + 8, tok), f32),
        pltpu.VMEM((A, hr + 8, tok), f32),
        pltpu.VMEM((A, hr, tok), f32),
        pltpu.VMEM((A, hr, tok), f32),
        pltpu.VMEM((A, sz.levels * hr, tok), f32),
        pltpu.VMEM((A, tok, cg), f32),
        [pltpu.VMEM((A >> b, state, cg), bf16) for b in range(a_bits)],
        pltpu.VMEM((state, cg), f32),
        pltpu.VMEM((z_bits, state, cg), bf16),
        pltpu.VMEM((z_bits, state, cg), bf16),
        pltpu.VMEM((z_bits, hr, tok), f32),
        pltpu.VMEM((z_bits, hr, tok), f32),
        pltpu.VMEM((A // 2, 2, tok, cg), bf16),
        pltpu.VMEM((A, 8, tok), f32),
        pltpu.VMEM((A, 8, tok), f32),
        pltpu.VMEM((2 * hr, cg), bf16),
        [pltpu.VMEM((units,) + shape, bf16) for shape in left],
        [pltpu.VMEM((units,) + shape, bf16) for shape in left],
        [pltpu.VMEM((units,) + shape, f32) for shape in left],
        dma((A,)), dma((A,)),
        dma((A + Z,)), dma((A + Z,)), dma((A + Z,)), dma((A + Z,)),
        dma((A,)), dma((A,)), dma((A,)), dma((A,)), dma((A,)), dma((A,)), dma((A,)), dma((A,)),
        dma((z_bits,)), dma((z_bits,)), dma((z_bits,)), dma((z_bits,)),
        dma((A,)), dma((A,)),
        dma((a_bits, units)), dma((a_bits, units)),
    ]
    return pl.pallas_call(
        lambda *refs: mixer_kernel(sz, *refs),
        out_shape=jax.ShapeDtypeStruct((tok, Z * A * oc), bf16),
        in_specs=[hbm] * 3 + [vmem] * 8,
        out_specs=vmem,
        scratch_shapes=scratch,
        name="mixer",
        cost_estimate=pl.CostEstimate(flops=1 << 32, bytes_accessed=32 << 20, transcendentals=1 << 21),
        compiler_params=pltpu.CompilerParams(
            collective_id=0, has_side_effects=True, vmem_limit_bytes=56 << 20
        ),
    )(wt, values, gates, queries, keys, decay_t, lam, seg, table, skip, gain)


def sizes_for(queries, values, log_decay, lam_table, out_proj):
    tok, state = queries.shape
    heads = log_decay.shape[1]
    count = lax.axis_size("seq")
    A = math.gcd(math.gcd(heads, 8), count)
    Z = count // A
    cg = values.shape[1] // A
    oc = out_proj.shape[1]
    fits = lax.axis_size("head") == 1 and A > 1 and Z > 1 and Z & (Z - 1) == 0
    fits = fits and cg % 128 == 0 and oc % 16 == 0 and (A * oc) % 128 == 0
    fits = fits and tok == 128 and state == 128 and -decay_floor * tok / 2 < 60
    if not fits:
        return None
    return Sizes(tok, state, cg, heads // A, oc, A, Z, lam_table.shape[1])


def split_device(
    queries,
    key_rows,
    values,
    gate_rows,
    log_decay,
    skip_gain,
    lam_index,
    segments,
    lam_table,
    norm_gain,
    out_proj,
):
    tok, state_dim = queries.shape
    head_count = log_decay.shape[1]
    cols = values.shape[1]
    head_dim = cols // head_count
    classes, level_count = lam_table.shape[:2]
    dev_count = lax.axis_size("seq")
    inner_total = cols * lax.axis_size("head")
    A = math.gcd(math.gcd(head_count, 8), dev_count)
    Z = dev_count // A
    a_bits = A.bit_length() - 1
    z_bits = Z.bit_length() - 1
    hg = head_count // A
    cg = hg * head_dim
    rows = A * tok
    out_cols = out_proj.shape[1]
    groups = [[z * A + i for i in range(A)] for z in range(Z)]
    me = lax.axis_index("seq")
    in_pos = lax.rem(me, A)
    z_pos = lax.div(me, A)

    def exchange(blocks):
        return lax.all_to_all(
            blocks, "seq", 0, 0, tiled=True, axis_index_groups=groups
        )

    def my_heads(array, width, axis):
        return lax.dynamic_slice_in_dim(array, in_pos * width, width, axis)

    w_blocks = out_proj.T.reshape(out_cols, A, cg).swapaxes(0, 1)
    w_block = exchange(w_blocks).reshape(A * out_cols, cg)

    packed = pack_call(
        queries,
        key_rows,
        values,
        log_decay,
        lam_index.astype(f32)[:, None],
        segments.astype(f32)[:, None],
        groups=A,
    )
    packed = exchange(packed)
    small = packed[:, :, 2 * state_dim + cg :].astype(f32)

    def shift(block, step):
        pairs = [(p, (p + step * A) % dev_count) for p in range(dev_count)]
        return lax.ppermute(block, "seq", pairs)

    w_ring = [(0, w_block)]
    above = below = w_block
    if Z > 1:
        above = shift(w_block, 1)
        w_ring.append((1, above))
    if Z > 2:
        below = shift(w_block, -1)
        w_ring.append((-1, below))

    cum = small[:, :, :hg] + small[:, :, hg : 2 * hg] + small[:, :, 2 * hg : 3 * hg]
    lam = small[:, :, 3 * hg].reshape(rows).astype(jnp.int32)
    seg = small[:, :, 3 * hg + 1]
    span = cum[:, -1, :]
    onehot = (lam[:, None] == jnp.arange(classes, dtype=jnp.int32)[None, :]).astype(f32)
    table = my_heads(lam_table, hg, 2).reshape(classes, level_count * hg)
    lw = jnp.dot(onehot, table, precision=highest).reshape(A, tok, level_count * hg)
    expand = (
        jnp.arange(hg, dtype=jnp.int32)[:, None]
        == jnp.arange(cg, dtype=jnp.int32)[None, :] // head_dim
    ).astype(bf16)

    total = span
    prefix = jnp.zeros((A, hg), f32)
    prefixes = []
    up_factors = []
    for b in range(a_bits):
        wide = 2**b
        low_total, up_total = total[0::2], total[1::2]
        is_up = (jnp.arange(A, dtype=jnp.int32) // wide % 2 == 1)[:, None]
        prefixes.append(jnp.where(is_up, prefix, -jnp.inf))
        up_factors.append(jnp.exp(up_total))
        prefix = prefix + jnp.where(is_up, jnp.repeat(low_total, 2 * wide, axis=0), 0.0)
        total = low_total + up_total
    total = total[0]

    def level_scale(before, level):
        weight = lw[:, :, (2 + level) * hg : (3 + level) * hg]
        return jnp.exp(cum + before[:, None, :]) * weight

    end_scale = jnp.exp(span[:, None, :] - cum)
    up_rows = jnp.concatenate(up_factors, axis=0)
    *level_states, state = state_call(
        packed, end_scale, up_rows, expand, state_dim=state_dim, bits=a_bits
    )
    gate_blocks = gate_rows.reshape(tok, A, cg).swapaxes(0, 1)
    gate_blocks, state, total = lax.optimization_barrier((gate_blocks, state, total))
    gates = exchange(gate_blocks)
    local_scales = [lw[:, :, : 2 * hg]]
    local_scales += [level_scale(before, b) for b, before in enumerate(prefixes)]
    local_scales = jnp.concatenate(local_scales, axis=2)

    others, other_scales = [], []
    for zb in range(z_bits):
        other = xor_permute(state, A << zb)
        other_total = xor_permute(total[None, :], A << zb)[0]
        is_up = jnp.bitwise_and(jnp.right_shift(z_pos, zb), 1) == 1
        others.append(other)
        before = jnp.where(is_up, prefix, -jnp.inf)
        other_scales.append(level_scale(before, a_bits + zb))
        if zb + 1 < z_bits:
            up_state = jnp.where(is_up, state, other).astype(f32)
            low_state = jnp.where(is_up, other, state).astype(f32)
            factor = widen(jnp.exp(jnp.where(is_up, total, other_total)), head_dim)
            state = (up_state + factor[None, :] * low_state).astype(bf16)
            prefix = prefix + jnp.where(is_up, other_total, 0.0)[None, :]
            total = total + other_total

    for distance in range(2, Z // 2 + 1):
        above, others = lax.optimization_barrier((above, others))
        above = shift(above, 1)
        w_ring.append((distance, above))
        if 2 * distance < Z:
            below = shift(below, -1)
            w_ring.append((-distance, below))

    skip = widen(my_heads(skip_gain, hg, 0), head_dim)[None, :]
    mixed = local_call(
        packed, cum, cum.swapaxes(1, 2), local_scales, seg, level_states, skip, expand,
        state_dim=state_dim, head_dim=head_dim,
    )
    gain = my_heads(norm_gain, cg, 0)[None, :]
    hidden, squares = gate_call(
        packed, mixed, others, other_scales, gates, gain, expand, state_dim=state_dim
    )

    def reduce_group(part, order, narrow):
        left = list(range(a_bits))[::-1]
        part = part.reshape((2,) * a_bits + part.shape[1:])
        for b in order:
            axis = left.index(b)
            left.remove(b)
            bit = jnp.bitwise_and(jnp.right_shift(in_pos, b), 1)
            mine = lax.dynamic_index_in_dim(part, bit, axis, keepdims=False)
            theirs = lax.dynamic_index_in_dim(part, 1 - bit, axis, keepdims=False)
            part = mine + xor_permute(theirs.astype(narrow), 2**b).astype(f32)
        return part

    bits = list(range(a_bits))
    flipped = bits[:1] + bits[1:][::-1]
    square_sum = reduce_group(squares.reshape(A, tok), bits, f32)
    square_sum = lax.psum(square_sum, "head")
    inv_rms = lax.rsqrt(square_sum / inner_total + epsilon)[:, None]
    block_cols = A * out_cols
    out = jnp.zeros((tok, Z * block_cols), bf16)
    for step, (distance, w_part) in enumerate(w_ring):
        part = lax.dot_general(
            hidden, w_part, (((1,), (1,)), ((), ())), preferred_element_type=f32
        )
        part = reduce_group(
            part.reshape(A, tok, block_cols), flipped if step % 2 else bits, bf16
        )
        block = lax.rem(z_pos - distance + Z, Z)
        out = lax.dynamic_update_slice_in_dim(
            out, (part * inv_rms).astype(bf16), block * block_cols, 1
        )
    return lax.psum_scatter(out, "head", scatter_dimension=0, tiled=True)


def per_device(
    queries,
    key_rows,
    values,
    gate_rows,
    log_decay,
    skip_gain,
    lam_index,
    segments,
    lam_table,
    norm_gain,
    out_proj,
):
    sz = sizes_for(queries, values, log_decay, lam_table, out_proj)
    if sz is None:
        return split_device(
            queries, key_rows, values, gate_rows, log_decay, skip_gain,
            lam_index, segments, lam_table, norm_gain, out_proj,
        )
    return mixer_call(
        sz,
        out_proj.T,
        values,
        gate_rows,
        queries,
        key_rows,
        log_decay.T,
        lam_index[None, :],
        segments[None, :],
        lam_table.transpose(1, 0, 2),
        skip_gain[None, :],
        norm_gain[None, :],
    )


def solution(mesh):
    return jax.shard_map(
        per_device,
        mesh=mesh,
        in_specs=(
            P("seq", None),
            P("seq", None),
            P("seq", "head"),
            P("seq", "head"),
            P("seq", "head"),
            P("head"),
            P("seq"),
            P("seq"),
            P(None, None, "head"),
            P("head"),
            P("head", "seq"),
        ),
        out_specs=P(("seq", "head"), None),
        check_vma=False,
    )
```

```python
import math

import jax
import jax.numpy as jnp
from jax import lax
from jax.experimental import pallas as pl
from jax.experimental.pallas import tpu as pltpu
from jax.sharding import PartitionSpec as P

epsilon = 1e-05
highest = lax.Precision.HIGHEST
f32 = jnp.float32
bf16 = jnp.bfloat16


def xor_permute(value, mask):
    pairs = [(source, source ^ mask) for source in range(lax.axis_size("seq"))]
    return lax.ppermute(value, "seq", pairs)


def widen(matrix, head_dim):
    return jnp.repeat(matrix, head_dim, axis=-1)


def pack_kernel(groups, q_ref, k_ref, x_ref, decay_ref, lam_ref, seg_ref, out_ref):
    tok, state_dim = q_ref.shape
    cg = x_ref.shape[1] // groups
    hg = decay_ref.shape[1] // groups
    t_pos = lax.broadcasted_iota(jnp.int32, (tok, tok), 0)
    j_pos = lax.broadcasted_iota(jnp.int32, (tok, tok), 1)
    ones = jnp.where(t_pos >= j_pos, 1.0, 0.0).astype(f32)
    cum = jnp.dot(ones, decay_ref[...], precision=highest, preferred_element_type=f32)
    first = cum.astype(bf16).astype(f32)
    second = (cum - first).astype(bf16).astype(f32)
    third = cum - first - second
    pad = out_ref.shape[2] - 2 * state_dim - cg - 3 * hg - 2
    tail = [lam_ref[...], seg_ref[...], jnp.zeros((tok, pad), f32)]
    for s in range(groups):
        out_ref[s, :, :state_dim] = q_ref[...]
        out_ref[s, :, state_dim : 2 * state_dim] = k_ref[...]
        out_ref[s, :, 2 * state_dim : 2 * state_dim + cg] = x_ref[:, s * cg : (s + 1) * cg]
        parts = [part[:, s * hg : (s + 1) * hg] for part in (first, second, third)]
        small = jnp.concatenate(parts + tail, axis=1)
        out_ref[s, :, 2 * state_dim + cg :] = small.astype(bf16)


def pack_call(queries, key_rows, values, log_decay, lam, seg, *, groups):
    tok, state_dim = queries.shape
    width = 2 * state_dim + values.shape[1] // groups + 3 * (log_decay.shape[1] // groups) + 2
    vmem = pl.BlockSpec(memory_space=pltpu.VMEM)
    return pl.pallas_call(
        lambda *refs: pack_kernel(groups, *refs),
        out_shape=jax.ShapeDtypeStruct((groups, tok, pl.cdiv(width + 1, 128) * 128), bf16),
        in_specs=[vmem] * 6,
        out_specs=vmem,
        name="pack",
        cost_estimate=pl.CostEstimate(
            flops=1 << 22, bytes_accessed=4 << 20, transcendentals=0
        ),
    )(queries, key_rows, values, log_decay, lam, seg)


def spread(scale, expand):
    high = scale.astype(bf16)
    low = (scale - high.astype(f32)).astype(bf16)
    return jnp.dot(high, expand, preferred_element_type=f32) + jnp.dot(
        low, expand, preferred_element_type=f32
    )


def state_kernel(bits, state_dim, packed_ref, scale_ref, up_ref, expand_ref, *outs):
    A = packed_ref.shape[0]
    expand = expand_ref[...]
    up_wide = spread(up_ref[...], expand)
    for s in range(A):
        decayed = packed_ref[s, :, 2 * state_dim : 2 * state_dim + expand.shape[1]].astype(f32) * spread(scale_ref[s], expand)
        keys = packed_ref[s, :, state_dim : 2 * state_dim]
        outs[0][s] = lax.dot_general(
            keys,
            decayed.astype(bf16),
            (((0,), (0,)), ((), ())),
            preferred_element_type=f32,
        ).astype(bf16)
    row = 0
    for b in range(bits):
        for g in range(A >> (b + 1)):
            low = outs[b][2 * g].astype(f32)
            high = outs[b][2 * g + 1].astype(f32)
            merged = (high + up_wide[row : row + 1] * low).astype(bf16)
            if b + 1 < bits:
                outs[b + 1][g] = merged
            else:
                outs[b + 1][...] = merged
            row += 1


def state_call(packed, end_scale, up_rows, expand, *, state_dim, bits):
    A = packed.shape[0]
    cg = expand.shape[1]
    shapes = [(A >> b, state_dim, cg) for b in range(bits)] + [(state_dim, cg)]
    vmem = pl.BlockSpec(memory_space=pltpu.VMEM)
    return pl.pallas_call(
        lambda *refs: state_kernel(bits, state_dim, *refs),
        out_shape=[jax.ShapeDtypeStruct(shape, bf16) for shape in shapes],
        in_specs=[vmem] * 4,
        out_specs=[vmem] * len(shapes),
        name="group_states",
        cost_estimate=pl.CostEstimate(
            flops=1 << 29, bytes_accessed=8 << 20, transcendentals=0
        ),
    )(packed, end_scale, up_rows, expand)


def local_kernel(
    state_dim, head_dim, bits, packed_ref, cum_ref, cum_t_ref, scale_ref, seg_ref,
    seg_t_ref, skip_ref, expand_ref, *rest
):
    states, out_ref = rest[:bits], rest[bits]
    tok, hg = cum_ref.shape[1:]
    cg = expand_ref.shape[1]
    q = packed_ref[0, :, :state_dim]
    keys = packed_ref[0, :, state_dim : 2 * state_dim]
    expand = expand_ref[...]
    scores = lax.dot_general(
        q, keys, (((1,), (1,)), ((), ())), preferred_element_type=f32
    )
    same = seg_ref[0] == seg_t_ref[0]
    t_pos = lax.broadcasted_iota(jnp.int32, (tok, tok), 0)
    j_pos = lax.broadcasted_iota(jnp.int32, (tok, tok), 1)
    causal = t_pos >= j_pos
    scales = scale_ref[0]
    cum = cum_ref[0]
    cum_t = cum_t_ref[0]
    x_wide = packed_ref[0, :, 2 * state_dim : 2 * state_dim + cg]
    acc = skip_ref[...] * x_wide.astype(f32)
    for b in range(bits):
        read = jnp.dot(q, states[b][0], preferred_element_type=f32)
        acc = acc + read * spread(scales[:, (2 + b) * hg : (3 + b) * hg], expand)
    out_ref[...] = acc

    def head_weights(h):
        gaps = jnp.where(causal, cum[:, h : h + 1] - cum_t[h : h + 1, :], -jnp.inf)
        level_w = jnp.where(same, scales[:, h : h + 1], scales[:, hg + h : hg + h + 1])
        return (scores * jnp.exp(gaps) * level_w).astype(bf16)

    per_tile = max(1, 128 // head_dim)
    for first in range(0, hg, per_tile):
        heads = range(first, min(first + per_tile, hg))
        low, high = first * head_dim, min((first + per_tile) * head_dim, cg)
        x_tile = x_wide[:, low:high]
        lane_head = lax.broadcasted_iota(jnp.int32, (tok, high - low), 1) // head_dim
        tile = None
        for h in heads:
            part = jnp.dot(head_weights(h), x_tile, preferred_element_type=f32)
            tile = part if tile is None else jnp.where(lane_head == h - first, part, tile)
        out_ref[:, low:high] += tile


def local_call(
    packed, cum, cum_t, scales, seg, level_states, skip, expand, *, state_dim, head_dim
):
    A, tok, width = packed.shape
    cg = expand.shape[1]
    hg = cum.shape[2]
    bits = len(level_states)

    def shard_spec(*dims):
        return pl.BlockSpec((1,) + dims, lambda s: (s, 0, 0))

    def sibling_spec(b):
        return pl.BlockSpec(
            (1, state_dim, cg), lambda s: (jnp.maximum(s // 2**b - 1, 0), 0, 0)
        )

    def whole_spec(shape):
        return pl.BlockSpec(shape, lambda s: (0, 0))

    return pl.pallas_call(
        lambda *refs: local_kernel(state_dim, head_dim, bits, *refs),
        grid=(A,),
        out_shape=jax.ShapeDtypeStruct((A * tok, cg), f32),
        in_specs=[
            shard_spec(tok, width),
            shard_spec(tok, hg),
            shard_spec(hg, tok),
            shard_spec(tok, scales.shape[2]),
            shard_spec(tok, 1),
            shard_spec(1, tok),
            whole_spec((1, cg)),
            whole_spec(expand.shape),
        ]
        + [sibling_spec(b) for b in range(bits)],
        out_specs=pl.BlockSpec((tok, cg), lambda s: (s, 0)),
        name="local_mix",
        cost_estimate=pl.CostEstimate(
            flops=1 << 32, bytes_accessed=12 << 20, transcendentals=1 << 21
        ),
    )(packed, cum, cum_t, scales, seg[:, :, None], seg[:, None, :], skip, expand, *level_states)


def gate_kernel(levels, packed_ref, mixed_ref, scale_ref, gates_ref, gain_ref, expand_ref, *rest):
    others, (hidden_ref, square_ref) = rest[:levels], rest[levels:]
    hg = expand_ref.shape[0]
    q = packed_ref[0]
    expand = expand_ref[...]
    scales = scale_ref[0]
    acc = mixed_ref[...]
    for level in range(levels):
        read = jnp.dot(q, others[level][...], preferred_element_type=f32)
        acc = acc + read * spread(scales[:, level * hg : (level + 1) * hg], expand)
    gate = gates_ref[0].astype(f32)
    gated = acc * (gate / (1.0 + jnp.exp(-gate)))
    square_ref[0] = jnp.sum(gated * gated, axis=1, keepdims=True)
    hidden_ref[...] = (gated * gain_ref[...]).astype(bf16)


def gate_call(packed, mixed, others, other_scales, gates, gain, expand, *, state_dim):
    A, tok, cg = gates.shape
    levels = len(others)
    scales = jnp.concatenate(other_scales, axis=2)

    def shard_spec(*dims):
        return pl.BlockSpec((1,) + dims, lambda s: (s, 0, 0))

    def whole_spec(shape):
        return pl.BlockSpec(shape, lambda s: (0, 0))

    rows_spec = pl.BlockSpec((tok, cg), lambda s: (s, 0))
    return pl.pallas_call(
        lambda *refs: gate_kernel(levels, *refs),
        grid=(A,),
        out_shape=[
            jax.ShapeDtypeStruct((A * tok, cg), bf16),
            jax.ShapeDtypeStruct((A, tok, 1), f32),
        ],
        in_specs=[
            shard_spec(tok, state_dim),
            rows_spec,
            shard_spec(tok, scales.shape[2]),
            shard_spec(tok, cg),
            whole_spec((1, cg)),
            whole_spec(expand.shape),
        ]
        + [whole_spec((state_dim, cg))] * levels,
        out_specs=[rows_spec, shard_spec(tok, 1)],
        name="gate_mix",
        cost_estimate=pl.CostEstimate(
            flops=1 << 30, bytes_accessed=8 << 20, transcendentals=1 << 20
        ),
    )(packed, mixed, scales, gates, gain, expand, *others)


MESH = pl.DeviceIdType.MESH
decay_floor = -0.69


def bit_of(pos, b):
    return lax.rem(lax.div(pos, 2**b), 2)


def flip(pos, mask):
    out = pos
    for b in range(mask.bit_length()):
        if (mask >> b) & 1:
            out = out + (1 - 2 * bit_of(pos, b)) * 2**b
    return out


def flip_traced(pos, step, bits):
    out = 0
    for b in range(bits):
        out = out + lax.rem(bit_of(pos, b) + bit_of(step, b), 2) * 2**b
    return out


def dot_f32(a, b, dims=(((1,), (0,)), ((), ())), precision=None):
    return lax.dot_general(a, b, dims, precision=precision, preferred_element_type=f32)


NT = (((1,), (1,)), ((), ()))
TN = (((0,), (0,)), ((), ()))


class Sizes:
    def __init__(self, tok, state, cg, hg, oc, A, Z, levels):
        self.tok, self.state, self.cg, self.hg, self.oc = tok, state, cg, hg, oc
        self.A, self.Z, self.levels = A, Z, levels
        self.a_bits = A.bit_length() - 1
        self.z_bits = Z.bit_length() - 1
        self.hr = pl.cdiv(hg, 16) * 16
        self.half = tok // 2
        self.head_dim = cg // hg


def plane_partners(Z):
    pairs = {(a, a + 1) for a in range(Z - 1)}
    for b in range(Z.bit_length() - 1):
        for last in range(2**b - 1, Z, 2 ** (b + 1)):
            pairs |= {(last, last + step) for step in range(1, 2**b + 1)}
    pairs |= {(b, a) for a, b in pairs}
    return [sorted(b for a, b in pairs if a == zz) for zz in range(Z)]


def mixer_kernel(
    sz, wt_ref, v_ref, g_ref, q_in, k_in, dec_in, lam_in, seg_in, tab_in, skip_in, gain_in,
    out_ref,
    q_ref, k_ref, dec_ref, lam_ref, seg_ref, tab_ref, skip_ref, gain_ref,
    wbuf, xbuf, gbuf, qkbuf, smsend, smbuf, pre, aft, lwbuf, acc, lev, pst, zsend, zrecv, tsend, trecv,
    hid, sqsend, sqrecv, folds, expand, snd, rcv, keep,
    w_s, w_r, up_s, up_r, dn_s, dn_r, qk_s, qk_r, sm_s, sm_r, x_s, x_r, g_s, g_r,
    zs_s, zs_r, zt_s, zt_r, sq_s, sq_r, c_s, c_r, in_r,
):
    A, Z, tok, cg, hg, hr, oc = sz.A, sz.Z, sz.tok, sz.cg, sz.hg, sz.hr, sz.oc
    state, a_bits, z_bits, half, levels = sz.state, sz.a_bits, sz.z_bits, sz.half, sz.levels
    me = lax.axis_index("seq")
    p = lax.rem(me, A)
    z = lax.div(me, A)
    waits = []

    def dev(zz, pp):
        return {"seq": zz * A + pp}

    def cols(pos):
        return pl.ds(pl.multiple_of(pos * cg, cg), cg)

    def remote(src, dst, send, recv, device):
        return pltpu.make_async_remote_copy(
            src_ref=src, dst_ref=dst, send_sem=send, recv_sem=recv,
            device_id=device, device_id_type=MESH,
        )

    barrier = pltpu.get_barrier_semaphore()
    for d in range(1, A):
        pl.semaphore_signal(barrier, inc=1, device_id=dev(z, flip(p, d)), device_id_type=MESH)
    meets = plane_partners(Z)
    for zz in range(Z):
        @pl.when(z == zz)
        def _():
            for other in meets[zz]:
                pl.semaphore_signal(barrier, inc=1, device_id=dev(other, p), device_id_type=MESH)


    def piece(zz, pos):
        return wbuf.at[zz, pl.ds(pl.multiple_of(pos * oc, 16), oc)]

    own_w = pltpu.make_async_copy(wt_ref.at[:, cols(p)], piece(z, p), w_r.at[0])
    own_x = pltpu.make_async_copy(v_ref.at[:, cols(p)], xbuf.at[p], x_r.at[0])
    own_g = pltpu.make_async_copy(g_ref.at[:, cols(p)], gbuf.at[p], g_r.at[0, 0])
    own_w.start()
    own_x.start()
    own_g.start()
    small_in = [
        pltpu.make_async_copy(src, dst, in_r.at[n])
        for n, (src, dst) in enumerate([
            (k_in, k_ref), (q_in, q_ref), (dec_in, dec_ref), (lam_in, lam_ref), (seg_in, seg_ref),
            (tab_in, tab_ref), (skip_in, skip_ref), (gain_in, gain_ref),
        ])
    ]
    for copy in small_in:
        copy.start()
    for copy in small_in[:2]:
        copy.wait()
    qkbuf[p, 0] = q_ref[...]
    qkbuf[p, 1] = k_ref[...].astype(f32).T.astype(bf16)
    expected = A - 1
    for zz in range(Z):
        expected = expected + jnp.where(z == zz, len(meets[zz]), 0)
    pl.semaphore_wait(barrier, expected)

    def start(copy):
        copy.start()
        waits.append(copy)
        return copy

    def up_copy(src, h, pos, dst=None):
        return remote(src, src if dst is None else dst, up_s.at[h, pos], up_r.at[h, pos], dev(z + 1, p))

    def dn_copy(src, h, pos, dst=None):
        return remote(src, src if dst is None else dst, dn_s.at[h, pos], dn_r.at[h, pos], dev(z - 1, p))

    def send_own(src, pos):
        @pl.when(z + 1 < Z)
        def _():
            up_copy(src, 0, pos, piece(z, pos)).start()

        @pl.when(z >= 1)
        def _():
            dn_copy(src, 0, pos, piece(z, pos)).start()

    order = list(range(1, A))
    relayed = [d for d in order if d % 2 == 0]
    direct = [1] + relayed
    w_cp, qk_cp, sm_cp, x_cp, g_cp = {}, {}, {}, {}, {}
    send_own(wt_ref.at[:, cols(p)], p)
    for d in order:
        t = flip(p, d)
        w_cp[d] = start(remote(wt_ref.at[:, cols(t)], piece(z, p), w_s.at[d], w_r.at[d], dev(z, t)))

    for copy in small_in[2:]:
        copy.wait()

    heads = dec_ref.shape[0]
    row_id = lax.broadcasted_iota(jnp.int32, (A * hr, heads), 0)
    head_id = lax.broadcasted_iota(jnp.int32, (A * hr, heads), 1)
    local_row = lax.rem(row_id, hr)
    place = (local_row < hg) & (lax.div(row_id, hr) * hg + local_row == head_id)
    placed = dot_f32(jnp.where(place, 1.0, 0.0).astype(f32), dec_ref[...], precision=highest)
    j_pos = lax.broadcasted_iota(jnp.int32, (tok, tok), 0)
    t_pos = lax.broadcasted_iota(jnp.int32, (tok, tok), 1)
    cum_all = dot_f32(placed, jnp.where(j_pos <= t_pos, 1.0, 0.0).astype(f32), precision=highest)
    for s in range(A):
        smsend[s, :hr] = cum_all[s * hr : (s + 1) * hr]
        smsend[s, hr : hr + 1] = lam_ref[...].astype(f32)
        smsend[s, hr + 1 : hr + 2] = seg_ref[...].astype(f32)
        smsend[s, hr + 2 : hr + 8] = jnp.zeros((6, tok), f32)
    smbuf[p] = smsend[p]
    for d in order:
        t = flip(p, d)
        sm_cp[d] = start(remote(smsend.at[t], smbuf.at[p], sm_s.at[d], sm_r.at[d], dev(z, t)))
    for d in direct:
        qk_cp[d] = start(remote(qkbuf.at[p], qkbuf.at[p], qk_s.at[d], qk_r.at[d], dev(z, flip(p, d))))
    for d in order:
        t = flip(p, d)
        x_cp[d] = start(remote(v_ref.at[:, cols(t)], xbuf.at[p], x_s.at[d], x_r.at[d], dev(z, t)))
    rows_of = [pl.ds(th * half, half) for th in range(2)]
    for th in range(2):
        for d in order:
            t = flip(p, d)
            g_cp[th, d] = start(
                remote(g_ref.at[rows_of[th], cols(t)], gbuf.at[p, rows_of[th]], g_s.at[th, d], g_r.at[th, d], dev(z, t))
            )

    pick_row = lax.broadcasted_iota(jnp.int32, (hr, heads), 0)
    pick_head = lax.broadcasted_iota(jnp.int32, (hr, heads), 1)
    pick = jnp.where((pick_row < hg) & (pick_row + p * hg == pick_head), 1.0, 0.0).astype(f32)
    table = jnp.concatenate(
        [dot_f32(pick, tab_ref[l], NT, precision=highest) for l in range(levels)], axis=0
    )
    e_row = lax.broadcasted_iota(jnp.int32, (2 * hr, cg), 0)
    e_col = lax.broadcasted_iota(jnp.int32, (2 * hr, cg), 1)
    expand[...] = jnp.where(lax.rem(e_row, hr) == lax.div(e_col, sz.head_dim), 1.0, 0.0).astype(bf16)

    def spread(rows):
        high = rows.astype(bf16)
        low = (rows - high.astype(f32)).astype(bf16)
        return dot_f32(jnp.concatenate([high, low], axis=0), expand[...], TN)

    def spread_row(column):
        return spread(jnp.broadcast_to(column, (hr, 8)))[:1]

    skip_rows = jnp.sum(pick * skip_ref[...], axis=1, keepdims=True)
    skip_wide = spread_row(skip_rows)
    gain = gain_ref[:, cols(p)]

    for d in order:
        w_cp[d].wait_recv()
        send_own(piece(z, flip(p, d)), flip(p, d))

    def hop(h, positions):
        for pos in positions:
            @pl.when(z - 1 - h >= 0)
            def _():
                up_copy(piece(z - 1 - h, pos), h, pos).wait_recv()

            if h + 2 < Z:
                @pl.when((z - 1 - h >= 0) & (z + 1 < Z))
                def _():
                    up_copy(piece(z - 1 - h, pos), h + 1, pos).start()

            @pl.when(z + 1 + h < Z)
            def _():
                dn_copy(piece(z + 1 + h, pos), h, pos).wait_recv()

            if h + 2 < Z:
                @pl.when((z + 1 + h < Z) & (z >= 1))
                def _():
                    dn_copy(piece(z + 1 + h, pos), h + 1, pos).start()

    def hop_sends_done():
        for h in range(Z - 1):
            for pos in range(A):
                @pl.when((z - h >= 0) & (z + 1 < Z))
                def _():
                    up_copy(piece(z - h, pos), h, pos).wait_send()

                @pl.when((z + h < Z) & (z >= 1))
                def _():
                    dn_copy(piece(z + h, pos), h, pos).wait_send()

    for d in order:
        sm_cp[d].wait_recv()
    ends = [smbuf[s, :hr, tok - 1 : tok] for s in range(A)]
    running = jnp.zeros((hr, 1), f32)
    for s in range(A):
        pre[s] = jnp.broadcast_to(running, (hr, tok))
        running = running + ends[s]
    total = running
    running = jnp.zeros((hr, 1), f32)
    for s in reversed(range(A)):
        aft[s] = jnp.broadcast_to(running, (hr, tok))
        running = running + ends[s]

    for d in relayed:
        qk_cp[d].wait_recv()
        there = qkbuf.at[flip(p, d)]
        qk_cp[d + 1] = start(remote(there, there, qk_s.at[d + 1], qk_r.at[d + 1], dev(z, flip(p, 1))))
    early, middle, late = list(range(A))[: A - 3], list(range(A))[A - 3 : A - 2], list(range(A))[A - 2 :]
    hop(0, early)

    causal = j_pos >= t_pos
    class_id = lax.broadcasted_iota(jnp.int32, (tab_ref.shape[1], tok), 0).astype(f32)
    pst[...] = jnp.zeros(pst.shape, f32)

    def first_pass(s):
        c = smbuf[s, :hr]
        onehot = jnp.where(smbuf[s, hr : hr + 1] == class_id, 1.0, 0.0).astype(f32)
        lw = dot_f32(table, onehot, precision=highest)
        lwbuf[s] = lw
        seg_row = jnp.broadcast_to(smbuf[s, hr + 1 : hr + 2], (tok, tok))
        same = seg_row == seg_row.T
        scores = dot_f32(qkbuf[s, 0], qkbuf[s, 1])
        s_same = jnp.where(causal & same, scores, 0.0).astype(bf16)
        s_diff = jnp.where(causal & jnp.logical_not(same), scores, 0.0).astype(bf16)
        mid = c[:, half - 1 : half]
        x = xbuf[s].astype(f32)
        scaled = (x * spread(jnp.exp(mid - c))).astype(bf16)
        big = dot_f32(jnp.concatenate([s_same, s_diff, qkbuf[s, 1]], axis=0), scaled)
        later = jnp.exp(c - mid)
        acc[s] = (
            skip_wide * x
            + spread(later * lw[:hr]) * big[:tok]
            + spread(later * lw[hr : 2 * hr]) * big[tok : 2 * tok]
        )
        end = big[2 * tok :] * spread_row(jnp.exp(c[:, tok - 1 : tok] - mid))
        lev[0][s] = end.astype(bf16)
        pst[...] += end * spread_row(jnp.exp(aft[s, :, :1]))

    for d in range(A):
        if d == 0:
            own_x.wait()
        else:
            x_cp[d].wait_recv()
            if d not in relayed:
                qk_cp[d].wait_recv()
        first_pass(flip(p, d))

    def z_copies(b, step):
        there = dev(z + step, p)
        return (
            remote(zsend.at[b], zrecv.at[b], zs_s.at[b, step], zs_r.at[b], there),
            remote(tsend.at[b], trecv.at[b], zt_s.at[b, step], zt_r.at[b], there),
        )

    def is_last(b):
        return lax.rem(z, 2 ** (b + 1)) == 2**b - 1

    def z_send(b):
        for step in range(2**b, 0, -1):
            for copy in z_copies(b, step):
                copy.start()

    def z_sent(b):
        @pl.when(is_last(b))
        def _():
            for step in range(2**b, 0, -1):
                for copy in z_copies(b, step):
                    copy.wait_send()

    def z_wait(b):
        @pl.when(bit_of(z, b) == 1)
        def _():
            for copy in z_copies(b, 1):
                copy.wait_recv()

    total_wide = jnp.broadcast_to(total, (hr, tok))

    @pl.when(is_last(0))
    def _():
        zsend[0] = pst[...].astype(bf16)
        tsend[0] = total_wide
        z_send(0)

    hop(0, middle)

    for b in range(a_bits - 1):
        for g in range(A >> (b + 1)):
            if g % 2 == 0:
                up_total = sum(ends[s] for s in range((2 * g + 1) << b, (2 * g + 2) << b))
                merged = lev[b][2 * g + 1].astype(f32) + spread_row(jnp.exp(up_total)) * lev[b][2 * g].astype(f32)
                lev[b + 1][g] = merged.astype(bf16)
            elif b + 2 < a_bits:
                up_total = sum(ends[s] for s in range((2 * g + 1) << b, (2 * g + 2) << b))
                merged = lev[b][2 * g + 1].astype(f32) + spread_row(jnp.exp(up_total)) * lev[b][2 * g].astype(f32)
                lev[b + 1][g] = merged.astype(bf16)
    for s in range(1, A):
        more = None
        for b in range(a_bits):
            if (s >> b) & 1:
                first = (s >> b) << b
                before = sum((ends[j] for j in range(first, s)), jnp.zeros((hr, 1), f32))
                scale = jnp.exp(smbuf[s, :hr] + before) * lwbuf[s, (2 + b) * hr : (3 + b) * hr]
                term = spread(scale) * dot_f32(qkbuf[s, 0], lev[b][(s >> b) - 1])
                more = term if more is None else more + term
        acc[s] += more

    for b in range(z_bits - 1):
        z_wait(b)

        @pl.when(lax.rem(z, 2 ** (b + 1)) == 2 ** (b + 1) - 1)
        def _():
            mine = pst[...] if b == 0 else zsend[b].astype(f32)
            mine_total = total_wide if b == 0 else tsend[b]
            joined = mine + spread_row(jnp.exp(mine_total[:, :1])) * zrecv[b].astype(f32)
            zsend[b + 1] = joined.astype(bf16)
            tsend[b + 1] = mine_total + trecv[b]

        @pl.when(is_last(b + 1))
        def _():
            z_send(b + 1)

    hop(0, late)
    if Z > 2:
        hop(1, early)

    z_prefix = jnp.zeros((hr, tok), f32)

    def z_pass(b, z_prefix):
        @pl.when(bit_of(z, b) == 1)
        def _():
            def body(s, carry):
                level = 2 + a_bits + b
                scale = jnp.exp(smbuf[s, :hr] + pre[s] + z_prefix) * lwbuf[s, level * hr : (level + 1) * hr]
                acc[s] += spread(scale) * dot_f32(qkbuf[s, 0], zrecv[b])
                return carry

            lax.fori_loop(0, A, body, 0)

    for b in range(z_bits):
        if b > 0:
            z_wait(b)
        z_pass(b, z_prefix)
        if b + 1 < z_bits:
            z_prefix = z_prefix + jnp.where(bit_of(z, b) == 1, trecv[b], 0.0)
        if b == 0 and Z > 2:
            hop(1, middle)

    def gate_pass(th):
        def body(s, carry):
            gate = gbuf[s, rows_of[th]].astype(f32)
            half_gate = 0.5 * gate
            gated = acc[s, rows_of[th]] * (half_gate + half_gate * jnp.tanh(half_gate))
            square = gated * gated
            folded = square[:, :128]
            for first in range(128, cg, 128):
                folded = folded + square[:, first : first + 128]
            folds[s, rows_of[th]] = folded
            hid[lax.div(s, 2), lax.rem(s, 2), rows_of[th]] = (gated * gain).astype(bf16)
            return carry

        if th == 0:
            own_g.wait()
        for d in order:
            g_cp[th, d].wait_recv()
        lax.fori_loop(0, A, body, 0, unroll=2)

    sq_cp = {}

    def send_squares():
        for s in range(A):
            sqsend[s] = dot_f32(jnp.ones((8, 128), f32), folds[s], NT, precision=highest)
        for d in order:
            t = flip(p, d)
            sq_cp[d] = start(remote(sqsend.at[t], sqrecv.at[p], sq_s.at[d], sq_r.at[d], dev(z, t)))
        sqrecv[p] = sqsend[p]

    bit0 = bit_of(p, 0)
    sequence = [list(range(a_bits)), [0] + list(range(1, a_bits))[::-1]]
    parts = projection_parts(sz)

    def block_of(k):
        out = 0
        for zz in range(Z):
            near = sorted(range(Z), key=lambda other: (abs(other - zz), other))
            out = jnp.where(z == zz, near[k], out)
        return out

    def path(i, th):
        return sequence[(i + th) % 2]

    def stage_copy(t, i, th):
        b = path(i, th)[t]
        return remote(
            snd[i][t].at[th], rcv[i][t].at[th], c_s.at[t, 2 * i + th], c_r.at[t, 2 * i + th],
            dev(z, flip(p, 1 << b)),
        )

    def multiply(i, th):
        k, first, width = parts[i]
        weights = wbuf[block_of(k), first : first + width]
        rows = A // 2 * half
        lhs = jnp.concatenate(
            [hid[:, bit, rows_of[th]].reshape(rows, cg) for bit in (1 - bit0, bit0)], axis=0
        )
        product = dot_f32(lhs, weights, NT)
        shape = snd[i][0].shape[1:]
        snd[i][0][th] = product[:rows].astype(bf16).reshape(shape)
        stage_copy(0, i, th).start()
        keep[i][0][th] = product[rows:].reshape(shape)

    def pick_half(ref, th, left, b, bit):
        axis = left.index(b)
        return ref[(th,) + (slice(None),) * axis + (bit,)]

    def fold(t, i, th):
        seq = path(i, th)
        left = [b for b in range(a_bits)[::-1] if b not in seq[: t + 1]]
        stage_copy(t, i, th).wait_recv()
        b = seq[t + 1]
        bit = bit_of(p, b)
        kept, got = keep[i][t], rcv[i][t]
        out = pick_half(kept, th, left, b, 1 - bit) + pick_half(got, th, left, b, 1 - bit).astype(f32)
        snd[i][t + 1][th] = out.astype(bf16)
        stage_copy(t + 1, i, th).start()
        keep[i][t + 1][th] = pick_half(kept, th, left, b, bit) + pick_half(got, th, left, b, bit).astype(f32)

    inverse = {}

    def finish(i, th):
        if not inverse:
            for d in order:
                sq_cp[d].wait_recv()
            gathered = jnp.concatenate([sqrecv[s, :1] for s in range(A)], axis=0)
            sums = dot_f32(gathered, jnp.ones((A, 128), f32), TN, precision=highest)
            inverse[0] = lax.rsqrt(sums / (A * cg) + epsilon)
        t = a_bits - 1
        k, first, width = parts[i]
        stage_copy(t, i, th).wait_recv()
        value = keep[i][t][th] + rcv[i][t][th].astype(f32)
        scale = jnp.concatenate([inverse[0][th * half : (th + 1) * half]] * (width // 128), axis=1)
        column = pl.multiple_of(block_of(k) * (A * oc) + first, 128)
        out_ref[rows_of[th], pl.ds(column, width)] = (value * scale).astype(out_ref.dtype)

    last = parts[-1][0]
    here = [i for i in range(len(parts)) if parts[i][0] < last]
    done = {}

    def run(i, th, upto):
        for stage in range(done.get((i, th), -1) + 1, upto + 1):
            if stage == 0:
                multiply(i, th)
            elif stage < a_bits:
                fold(stage - 1, i, th)
            else:
                finish(i, th)
            done[i, th] = stage

    own_w.wait()
    gate_pass(0)
    run(0, 0, 0)
    run(1, 0, 0)
    run(0, 0, 1)
    gate_pass(1)
    run(0, 1, 0)
    run(1, 0, 1)
    run(1, 1, 0)
    run(0, 1, 1)
    send_squares()
    if Z > 2:
        hop(1, late)
    fresh = [(1, 1)]
    for i in here[2:]:
        for th in range(2):
            run(i, th, 0)
            run(*fresh.pop(), 1)
            fresh.append((i, th))
    run(*fresh.pop(), 1)
    units = [(i, th) for i in here for th in range(2)]
    for stage in range(2, a_bits):
        for unit in units:
            run(*unit, stage)
    for unit in units[:2]:
        run(*unit, a_bits)
    seen = 0
    ending = [i for i in range(len(parts)) if i not in here]
    for i in ending:
        need = pl.cdiv(parts[i][1] + parts[i][2], oc)
        hop(Z - 2, range(seen, need))
        seen = need
        run(i, 0, 0)
        run(i, 1, 0)
        run(i, 0, 1)
        run(i, 1, 1)
    units += [(i, th) for i in ending for th in range(2)]
    for stage in range(2, a_bits + 1):
        for unit in units:
            run(*unit, max(done[unit], stage))

    for copy in waits:
        copy.wait_send()
    hop_sends_done()
    for b in range(z_bits):
        z_sent(b)
    for i in range(len(parts)):
        for th in range(2):
            for t in range(a_bits):
                stage_copy(t, i, th).wait_send()


def projection_parts(sz):
    width = sz.A * sz.oc
    parts = [(k, 0, width) for k in range(sz.Z - 1)]
    first = pl.cdiv(width // 128, 2) * 128
    parts.append((sz.Z - 1, 0, first))
    if first < width:
        parts.append((sz.Z - 1, first, width - first))
    return parts


def mixer_call(sz, wt, values, gates, queries, keys, decay_t, lam, seg, table, skip, gain):
    A, Z, tok, cg, hr, oc = sz.A, sz.Z, sz.tok, sz.cg, sz.hr, sz.oc
    a_bits, z_bits, half, state = sz.a_bits, sz.z_bits, sz.half, sz.state
    hbm = pl.BlockSpec(memory_space=pl.ANY)
    vmem = pl.BlockSpec(memory_space=pltpu.VMEM)
    parts = projection_parts(sz)

    def stages(kind):
        return [
            [pltpu.VMEM((2,) + (2,) * (a_bits - 1 - t) + (half, width), kind) for t in range(a_bits)]
            for _, _, width in parts
        ]

    dma = pltpu.SemaphoreType.DMA
    smalls = [queries, keys, decay_t, lam, seg, table, skip, gain]
    scratch = [pltpu.VMEM(a.shape, a.dtype) for a in smalls] + [
        pltpu.VMEM((Z, A * oc, cg), bf16),
        pltpu.VMEM((A, tok, cg), bf16),
        pltpu.VMEM((A, tok, cg), bf16),
        pltpu.VMEM((A, 2, tok, state), bf16),
        pltpu.VMEM((A, hr + 8, tok), f32),
        pltpu.VMEM((A, hr + 8, tok), f32),
        pltpu.VMEM((A, hr, tok), f32),
        pltpu.VMEM((A, hr, tok), f32),
        pltpu.VMEM((A, sz.levels * hr, tok), f32),
        pltpu.VMEM((A, tok, cg), f32),
        [pltpu.VMEM((A >> b, state, cg), bf16) for b in range(a_bits)],
        pltpu.VMEM((state, cg), f32),
        pltpu.VMEM((z_bits, state, cg), bf16),
        pltpu.VMEM((z_bits, state, cg), bf16),
        pltpu.VMEM((z_bits, hr, tok), f32),
        pltpu.VMEM((z_bits, hr, tok), f32),
        pltpu.VMEM((A // 2, 2, tok, cg), bf16),
        pltpu.VMEM((A, 8, tok), f32),
        pltpu.VMEM((A, 8, tok), f32),
        pltpu.VMEM((A, tok, 128), f32),
        pltpu.VMEM((2 * hr, cg), bf16),
        stages(bf16),
        stages(bf16),
        stages(f32),
        dma((A,)), dma((A,)),
        dma((Z, A)), dma((Z, A)), dma((Z, A)), dma((Z, A)),
        dma((A,)), dma((A,)), dma((A,)), dma((A,)), dma((A,)), dma((A,)), dma((2, A)), dma((2, A)),
        dma((z_bits, Z)), dma((z_bits,)), dma((z_bits, Z)), dma((z_bits,)),
        dma((A,)), dma((A,)),
        dma((a_bits, 2 * len(parts))), dma((a_bits, 2 * len(parts))),
        dma((len(smalls),)),
    ]
    return pl.pallas_call(
        lambda *refs: mixer_kernel(sz, *refs),
        out_shape=jax.ShapeDtypeStruct((tok, Z * A * oc), bf16),
        in_specs=[hbm] * 11,
        out_specs=vmem,
        scratch_shapes=scratch,
        name="mixer",
        cost_estimate=pl.CostEstimate(flops=1 << 32, bytes_accessed=32 << 20, transcendentals=1 << 21),
        compiler_params=pltpu.CompilerParams(
            collective_id=0, has_side_effects=True, vmem_limit_bytes=56 << 20
        ),
    )(wt, values, gates, queries, keys, decay_t, lam, seg, table, skip, gain)


def sizes_for(queries, values, log_decay, lam_table, out_proj):
    tok, state = queries.shape
    heads = log_decay.shape[1]
    count = lax.axis_size("seq")
    A = math.gcd(math.gcd(heads, 8), count)
    Z = count // A
    cg = values.shape[1] // A
    oc = out_proj.shape[1]
    fits = lax.axis_size("head") == 1 and A > 1 and Z > 1 and Z & (Z - 1) == 0
    fits = fits and cg % 128 == 0 and oc % 16 == 0 and (A * oc) % 128 == 0
    fits = fits and tok == 128 and state == 128 and -decay_floor * tok / 2 < 60
    if not fits:
        return None
    return Sizes(tok, state, cg, heads // A, oc, A, Z, lam_table.shape[1])


def split_device(
    queries,
    key_rows,
    values,
    gate_rows,
    log_decay,
    skip_gain,
    lam_index,
    segments,
    lam_table,
    norm_gain,
    out_proj,
):
    tok, state_dim = queries.shape
    head_count = log_decay.shape[1]
    cols = values.shape[1]
    head_dim = cols // head_count
    classes, level_count = lam_table.shape[:2]
    dev_count = lax.axis_size("seq")
    inner_total = cols * lax.axis_size("head")
    A = math.gcd(math.gcd(head_count, 8), dev_count)
    Z = dev_count // A
    a_bits = A.bit_length() - 1
    z_bits = Z.bit_length() - 1
    hg = head_count // A
    cg = hg * head_dim
    rows = A * tok
    out_cols = out_proj.shape[1]
    groups = [[z * A + i for i in range(A)] for z in range(Z)]
    me = lax.axis_index("seq")
    in_pos = lax.rem(me, A)
    z_pos = lax.div(me, A)

    def exchange(blocks):
        return lax.all_to_all(
            blocks, "seq", 0, 0, tiled=True, axis_index_groups=groups
        )

    def my_heads(array, width, axis):
        return lax.dynamic_slice_in_dim(array, in_pos * width, width, axis)

    w_blocks = out_proj.T.reshape(out_cols, A, cg).swapaxes(0, 1)
    w_block = exchange(w_blocks).reshape(A * out_cols, cg)

    packed = pack_call(
        queries,
        key_rows,
        values,
        log_decay,
        lam_index.astype(f32)[:, None],
        segments.astype(f32)[:, None],
        groups=A,
    )
    packed = exchange(packed)
    small = packed[:, :, 2 * state_dim + cg :].astype(f32)

    def shift(block, step):
        pairs = [(p, (p + step * A) % dev_count) for p in range(dev_count)]
        return lax.ppermute(block, "seq", pairs)

    w_ring = [(0, w_block)]
    above = below = w_block
    if Z > 1:
        above = shift(w_block, 1)
        w_ring.append((1, above))
    if Z > 2:
        below = shift(w_block, -1)
        w_ring.append((-1, below))

    cum = small[:, :, :hg] + small[:, :, hg : 2 * hg] + small[:, :, 2 * hg : 3 * hg]
    lam = small[:, :, 3 * hg].reshape(rows).astype(jnp.int32)
    seg = small[:, :, 3 * hg + 1]
    span = cum[:, -1, :]
    onehot = (lam[:, None] == jnp.arange(classes, dtype=jnp.int32)[None, :]).astype(f32)
    table = my_heads(lam_table, hg, 2).reshape(classes, level_count * hg)
    lw = jnp.dot(onehot, table, precision=highest).reshape(A, tok, level_count * hg)
    expand = (
        jnp.arange(hg, dtype=jnp.int32)[:, None]
        == jnp.arange(cg, dtype=jnp.int32)[None, :] // head_dim
    ).astype(bf16)

    total = span
    prefix = jnp.zeros((A, hg), f32)
    prefixes = []
    up_factors = []
    for b in range(a_bits):
        wide = 2**b
        low_total, up_total = total[0::2], total[1::2]
        is_up = (jnp.arange(A, dtype=jnp.int32) // wide % 2 == 1)[:, None]
        prefixes.append(jnp.where(is_up, prefix, -jnp.inf))
        up_factors.append(jnp.exp(up_total))
        prefix = prefix + jnp.where(is_up, jnp.repeat(low_total, 2 * wide, axis=0), 0.0)
        total = low_total + up_total
    total = total[0]

    def level_scale(before, level):
        weight = lw[:, :, (2 + level) * hg : (3 + level) * hg]
        return jnp.exp(cum + before[:, None, :]) * weight

    end_scale = jnp.exp(span[:, None, :] - cum)
    up_rows = jnp.concatenate(up_factors, axis=0)
    *level_states, state = state_call(
        packed, end_scale, up_rows, expand, state_dim=state_dim, bits=a_bits
    )
    gate_blocks = gate_rows.reshape(tok, A, cg).swapaxes(0, 1)
    gate_blocks, state, total = lax.optimization_barrier((gate_blocks, state, total))
    gates = exchange(gate_blocks)
    local_scales = [lw[:, :, : 2 * hg]]
    local_scales += [level_scale(before, b) for b, before in enumerate(prefixes)]
    local_scales = jnp.concatenate(local_scales, axis=2)

    others, other_scales = [], []
    for zb in range(z_bits):
        other = xor_permute(state, A << zb)
        other_total = xor_permute(total[None, :], A << zb)[0]
        is_up = jnp.bitwise_and(jnp.right_shift(z_pos, zb), 1) == 1
        others.append(other)
        before = jnp.where(is_up, prefix, -jnp.inf)
        other_scales.append(level_scale(before, a_bits + zb))
        if zb + 1 < z_bits:
            up_state = jnp.where(is_up, state, other).astype(f32)
            low_state = jnp.where(is_up, other, state).astype(f32)
            factor = widen(jnp.exp(jnp.where(is_up, total, other_total)), head_dim)
            state = (up_state + factor[None, :] * low_state).astype(bf16)
            prefix = prefix + jnp.where(is_up, other_total, 0.0)[None, :]
            total = total + other_total

    for distance in range(2, Z // 2 + 1):
        above, others = lax.optimization_barrier((above, others))
        above = shift(above, 1)
        w_ring.append((distance, above))
        if 2 * distance < Z:
            below = shift(below, -1)
            w_ring.append((-distance, below))

    skip = widen(my_heads(skip_gain, hg, 0), head_dim)[None, :]
    mixed = local_call(
        packed, cum, cum.swapaxes(1, 2), local_scales, seg, level_states, skip, expand,
        state_dim=state_dim, head_dim=head_dim,
    )
    gain = my_heads(norm_gain, cg, 0)[None, :]
    hidden, squares = gate_call(
        packed, mixed, others, other_scales, gates, gain, expand, state_dim=state_dim
    )

    def reduce_group(part, order, narrow):
        left = list(range(a_bits))[::-1]
        part = part.reshape((2,) * a_bits + part.shape[1:])
        for b in order:
            axis = left.index(b)
            left.remove(b)
            bit = jnp.bitwise_and(jnp.right_shift(in_pos, b), 1)
            mine = lax.dynamic_index_in_dim(part, bit, axis, keepdims=False)
            theirs = lax.dynamic_index_in_dim(part, 1 - bit, axis, keepdims=False)
            part = mine + xor_permute(theirs.astype(narrow), 2**b).astype(f32)
        return part

    bits = list(range(a_bits))
    flipped = bits[:1] + bits[1:][::-1]
    square_sum = reduce_group(squares.reshape(A, tok), bits, f32)
    square_sum = lax.psum(square_sum, "head")
    inv_rms = lax.rsqrt(square_sum / inner_total + epsilon)[:, None]
    block_cols = A * out_cols
    out = jnp.zeros((tok, Z * block_cols), bf16)
    for step, (distance, w_part) in enumerate(w_ring):
        part = lax.dot_general(
            hidden, w_part, (((1,), (1,)), ((), ())), preferred_element_type=f32
        )
        part = reduce_group(
            part.reshape(A, tok, block_cols), flipped if step % 2 else bits, bf16
        )
        block = lax.rem(z_pos - distance + Z, Z)
        out = lax.dynamic_update_slice_in_dim(
            out, (part * inv_rms).astype(bf16), block * block_cols, 1
        )
    return lax.psum_scatter(out, "head", scatter_dimension=0, tiled=True)


def per_device(
    queries,
    key_rows,
    values,
    gate_rows,
    log_decay,
    skip_gain,
    lam_index,
    segments,
    lam_table,
    norm_gain,
    out_proj,
):
    sz = sizes_for(queries, values, log_decay, lam_table, out_proj)
    if sz is None:
        return split_device(
            queries, key_rows, values, gate_rows, log_decay, skip_gain,
            lam_index, segments, lam_table, norm_gain, out_proj,
        )
    return mixer_call(
        sz,
        out_proj.T,
        values,
        gate_rows,
        queries,
        key_rows,
        log_decay.T,
        lam_index[None, :],
        segments[None, :],
        lam_table.transpose(1, 0, 2),
        skip_gain[None, :],
        norm_gain[None, :],
    )


def solution(mesh):
    return jax.shard_map(
        per_device,
        mesh=mesh,
        in_specs=(
            P("seq", None),
            P("seq", None),
            P("seq", "head"),
            P("seq", "head"),
            P("seq", "head"),
            P("head"),
            P("seq"),
            P("seq"),
            P(None, None, "head"),
            P("head"),
            P("head", "seq"),
        ),
        out_specs=P(("seq", "head"), None),
        check_vma=False,
    )
```

```python
import math

import jax
import jax.numpy as jnp
from jax import lax
from jax.experimental import pallas as pl
from jax.experimental.pallas import tpu as pltpu
from jax.sharding import PartitionSpec as P

epsilon = 1e-05
highest = lax.Precision.HIGHEST
f32 = jnp.float32
bf16 = jnp.bfloat16


def xor_permute(value, mask):
    pairs = [(source, source ^ mask) for source in range(lax.axis_size("seq"))]
    return lax.ppermute(value, "seq", pairs)


def widen(matrix, head_dim):
    return jnp.repeat(matrix, head_dim, axis=-1)


def pack_kernel(groups, q_ref, k_ref, x_ref, decay_ref, lam_ref, seg_ref, out_ref):
    tok, state_dim = q_ref.shape
    cg = x_ref.shape[1] // groups
    hg = decay_ref.shape[1] // groups
    t_pos = lax.broadcasted_iota(jnp.int32, (tok, tok), 0)
    j_pos = lax.broadcasted_iota(jnp.int32, (tok, tok), 1)
    ones = jnp.where(t_pos >= j_pos, 1.0, 0.0).astype(f32)
    cum = jnp.dot(ones, decay_ref[...], precision=highest, preferred_element_type=f32)
    first = cum.astype(bf16).astype(f32)
    second = (cum - first).astype(bf16).astype(f32)
    third = cum - first - second
    pad = out_ref.shape[2] - 2 * state_dim - cg - 3 * hg - 2
    tail = [lam_ref[...], seg_ref[...], jnp.zeros((tok, pad), f32)]
    for s in range(groups):
        out_ref[s, :, :state_dim] = q_ref[...]
        out_ref[s, :, state_dim : 2 * state_dim] = k_ref[...]
        out_ref[s, :, 2 * state_dim : 2 * state_dim + cg] = x_ref[:, s * cg : (s + 1) * cg]
        parts = [part[:, s * hg : (s + 1) * hg] for part in (first, second, third)]
        small = jnp.concatenate(parts + tail, axis=1)
        out_ref[s, :, 2 * state_dim + cg :] = small.astype(bf16)


def pack_call(queries, key_rows, values, log_decay, lam, seg, *, groups):
    tok, state_dim = queries.shape
    width = 2 * state_dim + values.shape[1] // groups + 3 * (log_decay.shape[1] // groups) + 2
    vmem = pl.BlockSpec(memory_space=pltpu.VMEM)
    return pl.pallas_call(
        lambda *refs: pack_kernel(groups, *refs),
        out_shape=jax.ShapeDtypeStruct((groups, tok, pl.cdiv(width + 1, 128) * 128), bf16),
        in_specs=[vmem] * 6,
        out_specs=vmem,
        name="pack",
        cost_estimate=pl.CostEstimate(
            flops=1 << 22, bytes_accessed=4 << 20, transcendentals=0
        ),
    )(queries, key_rows, values, log_decay, lam, seg)


def spread(scale, expand):
    high = scale.astype(bf16)
    low = (scale - high.astype(f32)).astype(bf16)
    return jnp.dot(high, expand, preferred_element_type=f32) + jnp.dot(
        low, expand, preferred_element_type=f32
    )


def state_kernel(bits, state_dim, packed_ref, scale_ref, up_ref, expand_ref, *outs):
    A = packed_ref.shape[0]
    expand = expand_ref[...]
    up_wide = spread(up_ref[...], expand)
    for s in range(A):
        decayed = packed_ref[s, :, 2 * state_dim : 2 * state_dim + expand.shape[1]].astype(f32) * spread(scale_ref[s], expand)
        keys = packed_ref[s, :, state_dim : 2 * state_dim]
        outs[0][s] = lax.dot_general(
            keys,
            decayed.astype(bf16),
            (((0,), (0,)), ((), ())),
            preferred_element_type=f32,
        ).astype(bf16)
    row = 0
    for b in range(bits):
        for g in range(A >> (b + 1)):
            low = outs[b][2 * g].astype(f32)
            high = outs[b][2 * g + 1].astype(f32)
            merged = (high + up_wide[row : row + 1] * low).astype(bf16)
            if b + 1 < bits:
                outs[b + 1][g] = merged
            else:
                outs[b + 1][...] = merged
            row += 1


def state_call(packed, end_scale, up_rows, expand, *, state_dim, bits):
    A = packed.shape[0]
    cg = expand.shape[1]
    shapes = [(A >> b, state_dim, cg) for b in range(bits)] + [(state_dim, cg)]
    vmem = pl.BlockSpec(memory_space=pltpu.VMEM)
    return pl.pallas_call(
        lambda *refs: state_kernel(bits, state_dim, *refs),
        out_shape=[jax.ShapeDtypeStruct(shape, bf16) for shape in shapes],
        in_specs=[vmem] * 4,
        out_specs=[vmem] * len(shapes),
        name="group_states",
        cost_estimate=pl.CostEstimate(
            flops=1 << 29, bytes_accessed=8 << 20, transcendentals=0
        ),
    )(packed, end_scale, up_rows, expand)


def local_kernel(
    state_dim, head_dim, bits, packed_ref, cum_ref, cum_t_ref, scale_ref, seg_ref,
    seg_t_ref, skip_ref, expand_ref, *rest
):
    states, out_ref = rest[:bits], rest[bits]
    tok, hg = cum_ref.shape[1:]
    cg = expand_ref.shape[1]
    q = packed_ref[0, :, :state_dim]
    keys = packed_ref[0, :, state_dim : 2 * state_dim]
    expand = expand_ref[...]
    scores = lax.dot_general(
        q, keys, (((1,), (1,)), ((), ())), preferred_element_type=f32
    )
    same = seg_ref[0] == seg_t_ref[0]
    t_pos = lax.broadcasted_iota(jnp.int32, (tok, tok), 0)
    j_pos = lax.broadcasted_iota(jnp.int32, (tok, tok), 1)
    causal = t_pos >= j_pos
    scales = scale_ref[0]
    cum = cum_ref[0]
    cum_t = cum_t_ref[0]
    x_wide = packed_ref[0, :, 2 * state_dim : 2 * state_dim + cg]
    acc = skip_ref[...] * x_wide.astype(f32)
    for b in range(bits):
        read = jnp.dot(q, states[b][0], preferred_element_type=f32)
        acc = acc + read * spread(scales[:, (2 + b) * hg : (3 + b) * hg], expand)
    out_ref[...] = acc

    def head_weights(h):
        gaps = jnp.where(causal, cum[:, h : h + 1] - cum_t[h : h + 1, :], -jnp.inf)
        level_w = jnp.where(same, scales[:, h : h + 1], scales[:, hg + h : hg + h + 1])
        return (scores * jnp.exp(gaps) * level_w).astype(bf16)

    per_tile = max(1, 128 // head_dim)
    for first in range(0, hg, per_tile):
        heads = range(first, min(first + per_tile, hg))
        low, high = first * head_dim, min((first + per_tile) * head_dim, cg)
        x_tile = x_wide[:, low:high]
        lane_head = lax.broadcasted_iota(jnp.int32, (tok, high - low), 1) // head_dim
        tile = None
        for h in heads:
            part = jnp.dot(head_weights(h), x_tile, preferred_element_type=f32)
            tile = part if tile is None else jnp.where(lane_head == h - first, part, tile)
        out_ref[:, low:high] += tile


def local_call(
    packed, cum, cum_t, scales, seg, level_states, skip, expand, *, state_dim, head_dim
):
    A, tok, width = packed.shape
    cg = expand.shape[1]
    hg = cum.shape[2]
    bits = len(level_states)

    def shard_spec(*dims):
        return pl.BlockSpec((1,) + dims, lambda s: (s, 0, 0))

    def sibling_spec(b):
        return pl.BlockSpec(
            (1, state_dim, cg), lambda s: (jnp.maximum(s // 2**b - 1, 0), 0, 0)
        )

    def whole_spec(shape):
        return pl.BlockSpec(shape, lambda s: (0, 0))

    return pl.pallas_call(
        lambda *refs: local_kernel(state_dim, head_dim, bits, *refs),
        grid=(A,),
        out_shape=jax.ShapeDtypeStruct((A * tok, cg), f32),
        in_specs=[
            shard_spec(tok, width),
            shard_spec(tok, hg),
            shard_spec(hg, tok),
            shard_spec(tok, scales.shape[2]),
            shard_spec(tok, 1),
            shard_spec(1, tok),
            whole_spec((1, cg)),
            whole_spec(expand.shape),
        ]
        + [sibling_spec(b) for b in range(bits)],
        out_specs=pl.BlockSpec((tok, cg), lambda s: (s, 0)),
        name="local_mix",
        cost_estimate=pl.CostEstimate(
            flops=1 << 32, bytes_accessed=12 << 20, transcendentals=1 << 21
        ),
    )(packed, cum, cum_t, scales, seg[:, :, None], seg[:, None, :], skip, expand, *level_states)


def gate_kernel(levels, packed_ref, mixed_ref, scale_ref, gates_ref, gain_ref, expand_ref, *rest):
    others, (hidden_ref, square_ref) = rest[:levels], rest[levels:]
    hg = expand_ref.shape[0]
    q = packed_ref[0]
    expand = expand_ref[...]
    scales = scale_ref[0]
    acc = mixed_ref[...]
    for level in range(levels):
        read = jnp.dot(q, others[level][...], preferred_element_type=f32)
        acc = acc + read * spread(scales[:, level * hg : (level + 1) * hg], expand)
    gate = gates_ref[0].astype(f32)
    gated = acc * (gate / (1.0 + jnp.exp(-gate)))
    square_ref[0] = jnp.sum(gated * gated, axis=1, keepdims=True)
    hidden_ref[...] = (gated * gain_ref[...]).astype(bf16)


def gate_call(packed, mixed, others, other_scales, gates, gain, expand, *, state_dim):
    A, tok, cg = gates.shape
    levels = len(others)
    scales = jnp.concatenate(other_scales, axis=2)

    def shard_spec(*dims):
        return pl.BlockSpec((1,) + dims, lambda s: (s, 0, 0))

    def whole_spec(shape):
        return pl.BlockSpec(shape, lambda s: (0, 0))

    rows_spec = pl.BlockSpec((tok, cg), lambda s: (s, 0))
    return pl.pallas_call(
        lambda *refs: gate_kernel(levels, *refs),
        grid=(A,),
        out_shape=[
            jax.ShapeDtypeStruct((A * tok, cg), bf16),
            jax.ShapeDtypeStruct((A, tok, 1), f32),
        ],
        in_specs=[
            shard_spec(tok, state_dim),
            rows_spec,
            shard_spec(tok, scales.shape[2]),
            shard_spec(tok, cg),
            whole_spec((1, cg)),
            whole_spec(expand.shape),
        ]
        + [whole_spec((state_dim, cg))] * levels,
        out_specs=[rows_spec, shard_spec(tok, 1)],
        name="gate_mix",
        cost_estimate=pl.CostEstimate(
            flops=1 << 30, bytes_accessed=8 << 20, transcendentals=1 << 20
        ),
    )(packed, mixed, scales, gates, gain, expand, *others)


MESH = pl.DeviceIdType.MESH
decay_floor = -0.69


def bit_of(pos, b):
    return lax.rem(lax.div(pos, 2**b), 2)


def flip(pos, mask):
    out = pos
    for b in range(mask.bit_length()):
        if (mask >> b) & 1:
            out = out + (1 - 2 * bit_of(pos, b)) * 2**b
    return out


def flip_traced(pos, step, bits):
    out = 0
    for b in range(bits):
        out = out + lax.rem(bit_of(pos, b) + bit_of(step, b), 2) * 2**b
    return out


def dot_f32(a, b, dims=(((1,), (0,)), ((), ())), precision=None):
    return lax.dot_general(a, b, dims, precision=precision, preferred_element_type=f32)


NT = (((1,), (1,)), ((), ()))
TN = (((0,), (0,)), ((), ()))


class Sizes:
    def __init__(self, tok, state, cg, hg, oc, A, Z, levels):
        self.tok, self.state, self.cg, self.hg, self.oc = tok, state, cg, hg, oc
        self.A, self.Z, self.levels = A, Z, levels
        self.a_bits = A.bit_length() - 1
        self.z_bits = Z.bit_length() - 1
        self.hr = pl.cdiv(hg, 16) * 16
        self.half = tok // 2
        self.head_dim = cg // hg


def plane_partners(Z):
    pairs = {(a, a + 1) for a in range(Z - 1)}
    for b in range(Z.bit_length() - 1):
        for last in range(2**b - 1, Z, 2 ** (b + 1)):
            pairs |= {(last, last + step) for step in range(1, 2**b + 1)}
    pairs |= {(b, a) for a, b in pairs}
    return [sorted(b for a, b in pairs if a == zz) for zz in range(Z)]


def mixer_kernel(
    sz, wt_ref, v_ref, g_ref, q_in, k_in, dec_in, lam_in, seg_in, tab_in, skip_in, gain_in,
    out_ref,
    q_ref, k_ref, dec_ref, lam_ref, seg_ref, tab_ref, skip_ref, gain_ref,
    wbuf, xbuf, gbuf, qkbuf, smsend, smbuf, pre, aft, lwbuf, acc, lev, pst, zsend, zrecv, tsend, trecv,
    hid, sqsend, sqrecv, folds, expand, snd, rcv, keep,
    w_s, w_r, up_s, up_r, dn_s, dn_r, qk_s, qk_r, sm_s, sm_r, x_s, x_r, g_s, g_r,
    zs_s, zs_r, zt_s, zt_r, sq_s, sq_r, c_s, c_r, in_r,
):
    A, Z, tok, cg, hg, hr, oc = sz.A, sz.Z, sz.tok, sz.cg, sz.hg, sz.hr, sz.oc
    state, a_bits, z_bits, half, levels = sz.state, sz.a_bits, sz.z_bits, sz.half, sz.levels
    me = lax.axis_index("seq")
    p = lax.rem(me, A)
    z = lax.div(me, A)
    waits = []

    def dev(zz, pp):
        return {"seq": zz * A + pp}

    def cols(pos):
        return pl.ds(pl.multiple_of(pos * cg, cg), cg)

    def remote(src, dst, send, recv, device):
        return pltpu.make_async_remote_copy(
            src_ref=src, dst_ref=dst, send_sem=send, recv_sem=recv,
            device_id=device, device_id_type=MESH,
        )

    barrier = pltpu.get_barrier_semaphore()
    for d in range(1, A):
        pl.semaphore_signal(barrier, inc=1, device_id=dev(z, flip(p, d)), device_id_type=MESH)
    meets = plane_partners(Z)
    for zz in range(Z):
        @pl.when(z == zz)
        def _():
            for other in meets[zz]:
                pl.semaphore_signal(barrier, inc=1, device_id=dev(other, p), device_id_type=MESH)


    def piece(zz, pos):
        return wbuf.at[zz, pl.ds(pl.multiple_of(pos * oc, 16), oc)]

    own_w = pltpu.make_async_copy(wt_ref.at[:, cols(p)], piece(z, p), w_r.at[0])
    own_x = pltpu.make_async_copy(v_ref.at[:, cols(p)], xbuf.at[p], x_r.at[0])
    own_g = pltpu.make_async_copy(g_ref.at[:, cols(p)], gbuf.at[p], g_r.at[0, 0])
    own_w.start()
    own_x.start()
    own_g.start()
    small_in = [
        pltpu.make_async_copy(src, dst, in_r.at[n])
        for n, (src, dst) in enumerate([
            (k_in, k_ref), (q_in, q_ref), (dec_in, dec_ref), (lam_in, lam_ref), (seg_in, seg_ref),
            (tab_in, tab_ref), (skip_in, skip_ref), (gain_in, gain_ref),
        ])
    ]
    for copy in small_in:
        copy.start()
    for copy in small_in[:2]:
        copy.wait()
    qkbuf[p, 0] = q_ref[...]
    qkbuf[p, 1] = k_ref[...].astype(f32).T.astype(bf16)
    expected = A - 1
    for zz in range(Z):
        expected = expected + jnp.where(z == zz, len(meets[zz]), 0)
    pl.semaphore_wait(barrier, expected)

    def start(copy):
        copy.start()
        waits.append(copy)
        return copy

    def up_copy(src, h, pos, dst=None):
        return remote(src, src if dst is None else dst, up_s.at[h, pos], up_r.at[h, pos], dev(z + 1, p))

    def dn_copy(src, h, pos, dst=None):
        return remote(src, src if dst is None else dst, dn_s.at[h, pos], dn_r.at[h, pos], dev(z - 1, p))

    def send_own(src, pos):
        @pl.when(z + 1 < Z)
        def _():
            up_copy(src, 0, pos, piece(z, pos)).start()

        @pl.when(z >= 1)
        def _():
            dn_copy(src, 0, pos, piece(z, pos)).start()

    order = list(range(1, A))
    relayed = [d for d in order if d % 2 == 0]
    direct = [1] + relayed
    w_cp, qk_cp, sm_cp, x_cp, g_cp = {}, {}, {}, {}, {}
    send_own(wt_ref.at[:, cols(p)], p)
    for d in order:
        t = flip(p, d)
        w_cp[d] = start(remote(wt_ref.at[:, cols(t)], piece(z, p), w_s.at[d], w_r.at[d], dev(z, t)))

    for copy in small_in[2:]:
        copy.wait()

    heads = dec_ref.shape[0]
    row_id = lax.broadcasted_iota(jnp.int32, (A * hr, heads), 0)
    head_id = lax.broadcasted_iota(jnp.int32, (A * hr, heads), 1)
    local_row = lax.rem(row_id, hr)
    place = (local_row < hg) & (lax.div(row_id, hr) * hg + local_row == head_id)
    placed = dot_f32(jnp.where(place, 1.0, 0.0).astype(f32), dec_ref[...], precision=highest)
    j_pos = lax.broadcasted_iota(jnp.int32, (tok, tok), 0)
    t_pos = lax.broadcasted_iota(jnp.int32, (tok, tok), 1)
    cum_all = dot_f32(placed, jnp.where(j_pos <= t_pos, 1.0, 0.0).astype(f32), precision=highest)
    for s in range(A):
        smsend[s, :hr] = cum_all[s * hr : (s + 1) * hr]
        smsend[s, hr : hr + 1] = lam_ref[...].astype(f32)
        smsend[s, hr + 1 : hr + 2] = seg_ref[...].astype(f32)
        smsend[s, hr + 2 : hr + 8] = jnp.zeros((6, tok), f32)
    smbuf[p] = smsend[p]
    for d in order:
        t = flip(p, d)
        sm_cp[d] = start(remote(smsend.at[t], smbuf.at[p], sm_s.at[d], sm_r.at[d], dev(z, t)))
    for d in direct:
        qk_cp[d] = start(remote(qkbuf.at[p], qkbuf.at[p], qk_s.at[d], qk_r.at[d], dev(z, flip(p, d))))
    for d in order:
        t = flip(p, d)
        x_cp[d] = start(remote(v_ref.at[:, cols(t)], xbuf.at[p], x_s.at[d], x_r.at[d], dev(z, t)))
    rows_of = [pl.ds(th * half, half) for th in range(2)]
    for th in range(2):
        for d in order:
            t = flip(p, d)
            g_cp[th, d] = start(
                remote(g_ref.at[rows_of[th], cols(t)], gbuf.at[p, rows_of[th]], g_s.at[th, d], g_r.at[th, d], dev(z, t))
            )

    pick_row = lax.broadcasted_iota(jnp.int32, (hr, heads), 0)
    pick_head = lax.broadcasted_iota(jnp.int32, (hr, heads), 1)
    pick = jnp.where((pick_row < hg) & (pick_row + p * hg == pick_head), 1.0, 0.0).astype(f32)
    table = jnp.concatenate(
        [dot_f32(pick, tab_ref[l], NT, precision=highest) for l in range(levels)], axis=0
    )
    e_row = lax.broadcasted_iota(jnp.int32, (2 * hr, cg), 0)
    e_col = lax.broadcasted_iota(jnp.int32, (2 * hr, cg), 1)
    expand[...] = jnp.where(lax.rem(e_row, hr) == lax.div(e_col, sz.head_dim), 1.0, 0.0).astype(bf16)

    def spread(rows):
        high = rows.astype(bf16)
        low = (rows - high.astype(f32)).astype(bf16)
        return dot_f32(jnp.concatenate([high, low], axis=0), expand[...], TN)

    def spread_row(column):
        return spread(jnp.broadcast_to(column, (hr, 8)))[:1]

    skip_rows = jnp.sum(pick * skip_ref[...], axis=1, keepdims=True)
    skip_wide = spread_row(skip_rows)
    gain = gain_ref[:, cols(p)]

    for d in order:
        w_cp[d].wait_recv()
        send_own(piece(z, flip(p, d)), flip(p, d))

    def hop(h, positions):
        for pos in positions:
            @pl.when(z - 1 - h >= 0)
            def _():
                up_copy(piece(z - 1 - h, pos), h, pos).wait_recv()

            if h + 2 < Z:
                @pl.when((z - 1 - h >= 0) & (z + 1 < Z))
                def _():
                    up_copy(piece(z - 1 - h, pos), h + 1, pos).start()

            @pl.when(z + 1 + h < Z)
            def _():
                dn_copy(piece(z + 1 + h, pos), h, pos).wait_recv()

            if h + 2 < Z:
                @pl.when((z + 1 + h < Z) & (z >= 1))
                def _():
                    dn_copy(piece(z + 1 + h, pos), h + 1, pos).start()

    def hop_sends_done():
        for h in range(Z - 1):
            for pos in range(A):
                @pl.when((z - h >= 0) & (z + 1 < Z))
                def _():
                    up_copy(piece(z - h, pos), h, pos).wait_send()

                @pl.when((z + h < Z) & (z >= 1))
                def _():
                    dn_copy(piece(z + h, pos), h, pos).wait_send()

    for d in order:
        sm_cp[d].wait_recv()
    ends = [smbuf[s, :hr, tok - 1 : tok] for s in range(A)]
    running = jnp.zeros((hr, 1), f32)
    for s in range(A):
        pre[s] = jnp.broadcast_to(running, (hr, tok))
        running = running + ends[s]
    total = running
    running = jnp.zeros((hr, 1), f32)
    for s in reversed(range(A)):
        aft[s] = jnp.broadcast_to(running, (hr, tok))
        running = running + ends[s]

    for d in relayed:
        qk_cp[d].wait_recv()
        there = qkbuf.at[flip(p, d)]
        qk_cp[d + 1] = start(remote(there, there, qk_s.at[d + 1], qk_r.at[d + 1], dev(z, flip(p, 1))))
    early, middle, late = list(range(A))[: A - 3], list(range(A))[A - 3 : A - 2], list(range(A))[A - 2 :]
    hop(0, early)

    causal = j_pos >= t_pos
    class_id = lax.broadcasted_iota(jnp.int32, (tab_ref.shape[1], tok), 0).astype(f32)
    pst[...] = jnp.zeros(pst.shape, f32)

    def first_pass(s):
        c = smbuf[s, :hr]
        onehot = jnp.where(smbuf[s, hr : hr + 1] == class_id, 1.0, 0.0).astype(f32)
        lw = dot_f32(table, onehot, precision=highest)
        lwbuf[s] = lw
        seg_row = jnp.broadcast_to(smbuf[s, hr + 1 : hr + 2], (tok, tok))
        same = seg_row == seg_row.T
        scores = dot_f32(qkbuf[s, 0], qkbuf[s, 1])
        s_same = jnp.where(causal & same, scores, 0.0).astype(bf16)
        s_diff = jnp.where(causal & jnp.logical_not(same), scores, 0.0).astype(bf16)
        mid = c[:, half - 1 : half]
        x = xbuf[s].astype(f32)
        scaled = (x * spread(jnp.exp(mid - c))).astype(bf16)
        big = dot_f32(jnp.concatenate([s_same, s_diff, qkbuf[s, 1]], axis=0), scaled)
        later = jnp.exp(c - mid)
        acc[s] = (
            skip_wide * x
            + spread(later * lw[:hr]) * big[:tok]
            + spread(later * lw[hr : 2 * hr]) * big[tok : 2 * tok]
        )
        end = big[2 * tok :] * spread_row(jnp.exp(c[:, tok - 1 : tok] - mid))
        lev[0][s] = end.astype(bf16)
        pst[...] += end * spread_row(jnp.exp(aft[s, :, :1]))

    for d in range(A):
        if d == 0:
            own_x.wait()
        else:
            x_cp[d].wait_recv()
            if d not in relayed:
                qk_cp[d].wait_recv()
        first_pass(flip(p, d))

    def z_copies(b, step):
        there = dev(z + step, p)
        return (
            remote(zsend.at[b], zrecv.at[b], zs_s.at[b, step], zs_r.at[b], there),
            remote(tsend.at[b], trecv.at[b], zt_s.at[b, step], zt_r.at[b], there),
        )

    def is_last(b):
        return lax.rem(z, 2 ** (b + 1)) == 2**b - 1

    def z_send(b):
        for step in range(2**b, 0, -1):
            for copy in z_copies(b, step):
                copy.start()

    def z_sent(b):
        @pl.when(is_last(b))
        def _():
            for step in range(2**b, 0, -1):
                for copy in z_copies(b, step):
                    copy.wait_send()

    def z_wait(b):
        @pl.when(bit_of(z, b) == 1)
        def _():
            for copy in z_copies(b, 1):
                copy.wait_recv()

    total_wide = jnp.broadcast_to(total, (hr, tok))

    @pl.when(is_last(0))
    def _():
        zsend[0] = pst[...].astype(bf16)
        tsend[0] = total_wide
        z_send(0)

    hop(0, middle)

    for b in range(a_bits - 1):
        for g in range(A >> (b + 1)):
            if g % 2 == 0:
                up_total = sum(ends[s] for s in range((2 * g + 1) << b, (2 * g + 2) << b))
                merged = lev[b][2 * g + 1].astype(f32) + spread_row(jnp.exp(up_total)) * lev[b][2 * g].astype(f32)
                lev[b + 1][g] = merged.astype(bf16)
            elif b + 2 < a_bits:
                up_total = sum(ends[s] for s in range((2 * g + 1) << b, (2 * g + 2) << b))
                merged = lev[b][2 * g + 1].astype(f32) + spread_row(jnp.exp(up_total)) * lev[b][2 * g].astype(f32)
                lev[b + 1][g] = merged.astype(bf16)
    for s in range(1, A):
        more = None
        for b in range(a_bits):
            if (s >> b) & 1:
                first = (s >> b) << b
                before = sum((ends[j] for j in range(first, s)), jnp.zeros((hr, 1), f32))
                scale = jnp.exp(smbuf[s, :hr] + before) * lwbuf[s, (2 + b) * hr : (3 + b) * hr]
                term = spread(scale) * dot_f32(qkbuf[s, 0], lev[b][(s >> b) - 1])
                more = term if more is None else more + term
        acc[s] += more

    for b in range(z_bits - 1):
        z_wait(b)

        @pl.when(lax.rem(z, 2 ** (b + 1)) == 2 ** (b + 1) - 1)
        def _():
            mine = pst[...] if b == 0 else zsend[b].astype(f32)
            mine_total = total_wide if b == 0 else tsend[b]
            joined = mine + spread_row(jnp.exp(mine_total[:, :1])) * zrecv[b].astype(f32)
            zsend[b + 1] = joined.astype(bf16)
            tsend[b + 1] = mine_total + trecv[b]

        @pl.when(is_last(b + 1))
        def _():
            z_send(b + 1)

    hop(0, late)
    if Z > 2:
        hop(1, early)

    z_prefix = jnp.zeros((hr, tok), f32)

    def z_pass(b, z_prefix):
        @pl.when(bit_of(z, b) == 1)
        def _():
            def body(s, carry):
                level = 2 + a_bits + b
                scale = jnp.exp(smbuf[s, :hr] + pre[s] + z_prefix) * lwbuf[s, level * hr : (level + 1) * hr]
                acc[s] += spread(scale) * dot_f32(qkbuf[s, 0], zrecv[b])
                return carry

            lax.fori_loop(0, A, body, 0, unroll=8)

    for b in range(z_bits):
        if b > 0:
            z_wait(b)
        z_pass(b, z_prefix)
        if b + 1 < z_bits:
            z_prefix = z_prefix + jnp.where(bit_of(z, b) == 1, trecv[b], 0.0)
        if b == 0 and Z > 2:
            hop(1, middle)

    def gate_pass(th):
        def body(s, carry):
            gate = gbuf[s, rows_of[th]].astype(f32)
            half_gate = 0.5 * gate
            gated = acc[s, rows_of[th]] * (half_gate + half_gate * jnp.tanh(half_gate))
            square = gated * gated
            folded = square[:, :128]
            for first in range(128, cg, 128):
                folded = folded + square[:, first : first + 128]
            folds[s, rows_of[th]] = folded
            hid[lax.div(s, 2), lax.rem(s, 2), rows_of[th]] = (gated * gain).astype(bf16)
            return carry

        if th == 0:
            own_g.wait()
        for d in order:
            g_cp[th, d].wait_recv()
        lax.fori_loop(0, A, body, 0, unroll=2)

    sq_cp = {}

    def send_squares():
        for s in range(A):
            sqsend[s] = dot_f32(jnp.ones((8, 128), f32), folds[s], NT, precision=highest)
        for d in order:
            t = flip(p, d)
            sq_cp[d] = start(remote(sqsend.at[t], sqrecv.at[p], sq_s.at[d], sq_r.at[d], dev(z, t)))
        sqrecv[p] = sqsend[p]

    bit0 = bit_of(p, 0)
    sequence = [list(range(a_bits)), [0] + list(range(1, a_bits))[::-1]]
    parts = projection_parts(sz)

    def block_of(k):
        out = 0
        for zz in range(Z):
            near = sorted(range(Z), key=lambda other: (abs(other - zz), other))
            out = jnp.where(z == zz, near[k], out)
        return out

    def path(i, th):
        return sequence[(i + th) % 2]

    def stage_copy(t, i, th):
        b = path(i, th)[t]
        return remote(
            snd[i][t].at[th], rcv[i][t].at[th], c_s.at[t, 2 * i + th], c_r.at[t, 2 * i + th],
            dev(z, flip(p, 1 << b)),
        )

    def multiply(i, th):
        k, first, width = parts[i]
        weights = wbuf[block_of(k), first : first + width]
        rows = A // 2 * half
        lhs = jnp.concatenate(
            [hid[:, bit, rows_of[th]].reshape(rows, cg) for bit in (1 - bit0, bit0)], axis=0
        )
        product = dot_f32(lhs, weights, NT)
        shape = snd[i][0].shape[1:]
        snd[i][0][th] = product[:rows].astype(bf16).reshape(shape)
        stage_copy(0, i, th).start()
        keep[i][0][th] = product[rows:].reshape(shape)

    def pick_half(ref, th, left, b, bit):
        axis = left.index(b)
        return ref[(th,) + (slice(None),) * axis + (bit,)]

    def fold(t, i, th):
        seq = path(i, th)
        left = [b for b in range(a_bits)[::-1] if b not in seq[: t + 1]]
        stage_copy(t, i, th).wait_recv()
        b = seq[t + 1]
        bit = bit_of(p, b)
        kept, got = keep[i][t], rcv[i][t]
        out = pick_half(kept, th, left, b, 1 - bit) + pick_half(got, th, left, b, 1 - bit).astype(f32)
        snd[i][t + 1][th] = out.astype(bf16)
        stage_copy(t + 1, i, th).start()
        keep[i][t + 1][th] = pick_half(kept, th, left, b, bit) + pick_half(got, th, left, b, bit).astype(f32)

    inverse = {}

    def finish(i, th):
        if not inverse:
            for d in order:
                sq_cp[d].wait_recv()
            gathered = jnp.concatenate([sqrecv[s, :1] for s in range(A)], axis=0)
            sums = dot_f32(gathered, jnp.ones((A, 128), f32), TN, precision=highest)
            inverse[0] = lax.rsqrt(sums / (A * cg) + epsilon)
        t = a_bits - 1
        k, first, width = parts[i]
        stage_copy(t, i, th).wait_recv()
        value = keep[i][t][th] + rcv[i][t][th].astype(f32)
        scale = jnp.concatenate([inverse[0][th * half : (th + 1) * half]] * (width // 128), axis=1)
        column = pl.multiple_of(block_of(k) * (A * oc) + first, 128)
        out_ref[rows_of[th], pl.ds(column, width)] = (value * scale).astype(out_ref.dtype)

    last = parts[-1][0]
    here = [i for i in range(len(parts)) if parts[i][0] < last]
    done = {}

    def run(i, th, upto):
        for stage in range(done.get((i, th), -1) + 1, upto + 1):
            if stage == 0:
                multiply(i, th)
            elif stage < a_bits:
                fold(stage - 1, i, th)
            else:
                finish(i, th)
            done[i, th] = stage

    own_w.wait()
    gate_pass(0)
    run(0, 0, 0)
    run(1, 0, 0)
    run(0, 0, 1)
    gate_pass(1)
    run(0, 1, 0)
    run(1, 0, 1)
    run(1, 1, 0)
    run(0, 1, 1)
    send_squares()
    if Z > 2:
        hop(1, late)
    fresh = [(1, 1)]
    for i in here[2:]:
        for th in range(2):
            run(i, th, 0)
            run(*fresh.pop(), 1)
            fresh.append((i, th))
    run(*fresh.pop(), 1)
    units = [(i, th) for i in here for th in range(2)]
    ending = [i for i in range(len(parts)) if i not in here]
    seen = 0

    def close(count):
        for stage in range(2, a_bits):
            for unit in units[:count]:
                if done[unit] < stage:
                    run(*unit, stage)

    for n, i in enumerate(ending):
        close(2 + 2 * n)
        need = pl.cdiv(parts[i][1] + parts[i][2], oc)
        hop(Z - 2, range(seen, need))
        seen = need
        run(i, 0, 0)
        run(i, 1, 0)
        run(i, 0, 1)
        run(i, 1, 1)
    units += [(i, th) for i in ending for th in range(2)]
    for stage in range(2, a_bits + 1):
        for unit in units:
            run(*unit, max(done[unit], stage))

    for copy in waits:
        copy.wait_send()
    hop_sends_done()
    for b in range(z_bits):
        z_sent(b)
    for i in range(len(parts)):
        for th in range(2):
            for t in range(a_bits):
                stage_copy(t, i, th).wait_send()


def projection_parts(sz):
    width = sz.A * sz.oc
    parts = [(k, 0, width) for k in range(sz.Z - 1)]
    first = pl.cdiv(width // 128, 2) * 128
    parts.append((sz.Z - 1, 0, first))
    if first < width:
        parts.append((sz.Z - 1, first, width - first))
    return parts


def mixer_call(sz, wt, values, gates, queries, keys, decay_t, lam, seg, table, skip, gain):
    A, Z, tok, cg, hr, oc = sz.A, sz.Z, sz.tok, sz.cg, sz.hr, sz.oc
    a_bits, z_bits, half, state = sz.a_bits, sz.z_bits, sz.half, sz.state
    hbm = pl.BlockSpec(memory_space=pl.ANY)
    vmem = pl.BlockSpec(memory_space=pltpu.VMEM)
    parts = projection_parts(sz)

    def stages(kind):
        return [
            [pltpu.VMEM((2,) + (2,) * (a_bits - 1 - t) + (half, width), kind) for t in range(a_bits)]
            for _, _, width in parts
        ]

    dma = pltpu.SemaphoreType.DMA
    smalls = [queries, keys, decay_t, lam, seg, table, skip, gain]
    scratch = [pltpu.VMEM(a.shape, a.dtype) for a in smalls] + [
        pltpu.VMEM((Z, A * oc, cg), bf16),
        pltpu.VMEM((A, tok, cg), bf16),
        pltpu.VMEM((A, tok, cg), bf16),
        pltpu.VMEM((A, 2, tok, state), bf16),
        pltpu.VMEM((A, hr + 8, tok), f32),
        pltpu.VMEM((A, hr + 8, tok), f32),
        pltpu.VMEM((A, hr, tok), f32),
        pltpu.VMEM((A, hr, tok), f32),
        pltpu.VMEM((A, sz.levels * hr, tok), f32),
        pltpu.VMEM((A, tok, cg), f32),
        [pltpu.VMEM((A >> b, state, cg), bf16) for b in range(a_bits)],
        pltpu.VMEM((state, cg), f32),
        pltpu.VMEM((z_bits, state, cg), bf16),
        pltpu.VMEM((z_bits, state, cg), bf16),
        pltpu.VMEM((z_bits, hr, tok), f32),
        pltpu.VMEM((z_bits, hr, tok), f32),
        pltpu.VMEM((A // 2, 2, tok, cg), bf16),
        pltpu.VMEM((A, 8, tok), f32),
        pltpu.VMEM((A, 8, tok), f32),
        pltpu.VMEM((A, tok, 128), f32),
        pltpu.VMEM((2 * hr, cg), bf16),
        stages(bf16),
        stages(bf16),
        stages(f32),
        dma((A,)), dma((A,)),
        dma((Z, A)), dma((Z, A)), dma((Z, A)), dma((Z, A)),
        dma((A,)), dma((A,)), dma((A,)), dma((A,)), dma((A,)), dma((A,)), dma((2, A)), dma((2, A)),
        dma((z_bits, Z)), dma((z_bits,)), dma((z_bits, Z)), dma((z_bits,)),
        dma((A,)), dma((A,)),
        dma((a_bits, 2 * len(parts))), dma((a_bits, 2 * len(parts))),
        dma((len(smalls),)),
    ]
    return pl.pallas_call(
        lambda *refs: mixer_kernel(sz, *refs),
        out_shape=jax.ShapeDtypeStruct((tok, Z * A * oc), bf16),
        in_specs=[hbm] * 11,
        out_specs=vmem,
        scratch_shapes=scratch,
        name="mixer",
        cost_estimate=pl.CostEstimate(flops=1 << 32, bytes_accessed=32 << 20, transcendentals=1 << 21),
        compiler_params=pltpu.CompilerParams(
            collective_id=0, has_side_effects=True, vmem_limit_bytes=56 << 20
        ),
    )(wt, values, gates, queries, keys, decay_t, lam, seg, table, skip, gain)


def sizes_for(queries, values, log_decay, lam_table, out_proj):
    tok, state = queries.shape
    heads = log_decay.shape[1]
    count = lax.axis_size("seq")
    A = math.gcd(math.gcd(heads, 8), count)
    Z = count // A
    cg = values.shape[1] // A
    oc = out_proj.shape[1]
    fits = lax.axis_size("head") == 1 and A > 1 and Z > 1 and Z & (Z - 1) == 0
    fits = fits and cg % 128 == 0 and oc % 16 == 0 and (A * oc) % 128 == 0
    fits = fits and tok == 128 and state == 128 and -decay_floor * tok / 2 < 60
    if not fits:
        return None
    return Sizes(tok, state, cg, heads // A, oc, A, Z, lam_table.shape[1])


def split_device(
    queries,
    key_rows,
    values,
    gate_rows,
    log_decay,
    skip_gain,
    lam_index,
    segments,
    lam_table,
    norm_gain,
    out_proj,
):
    tok, state_dim = queries.shape
    head_count = log_decay.shape[1]
    cols = values.shape[1]
    head_dim = cols // head_count
    classes, level_count = lam_table.shape[:2]
    dev_count = lax.axis_size("seq")
    inner_total = cols * lax.axis_size("head")
    A = math.gcd(math.gcd(head_count, 8), dev_count)
    Z = dev_count // A
    a_bits = A.bit_length() - 1
    z_bits = Z.bit_length() - 1
    hg = head_count // A
    cg = hg * head_dim
    rows = A * tok
    out_cols = out_proj.shape[1]
    groups = [[z * A + i for i in range(A)] for z in range(Z)]
    me = lax.axis_index("seq")
    in_pos = lax.rem(me, A)
    z_pos = lax.div(me, A)

    def exchange(blocks):
        return lax.all_to_all(
            blocks, "seq", 0, 0, tiled=True, axis_index_groups=groups
        )

    def my_heads(array, width, axis):
        return lax.dynamic_slice_in_dim(array, in_pos * width, width, axis)

    w_blocks = out_proj.T.reshape(out_cols, A, cg).swapaxes(0, 1)
    w_block = exchange(w_blocks).reshape(A * out_cols, cg)

    packed = pack_call(
        queries,
        key_rows,
        values,
        log_decay,
        lam_index.astype(f32)[:, None],
        segments.astype(f32)[:, None],
        groups=A,
    )
    packed = exchange(packed)
    small = packed[:, :, 2 * state_dim + cg :].astype(f32)

    def shift(block, step):
        pairs = [(p, (p + step * A) % dev_count) for p in range(dev_count)]
        return lax.ppermute(block, "seq", pairs)

    w_ring = [(0, w_block)]
    above = below = w_block
    if Z > 1:
        above = shift(w_block, 1)
        w_ring.append((1, above))
    if Z > 2:
        below = shift(w_block, -1)
        w_ring.append((-1, below))

    cum = small[:, :, :hg] + small[:, :, hg : 2 * hg] + small[:, :, 2 * hg : 3 * hg]
    lam = small[:, :, 3 * hg].reshape(rows).astype(jnp.int32)
    seg = small[:, :, 3 * hg + 1]
    span = cum[:, -1, :]
    onehot = (lam[:, None] == jnp.arange(classes, dtype=jnp.int32)[None, :]).astype(f32)
    table = my_heads(lam_table, hg, 2).reshape(classes, level_count * hg)
    lw = jnp.dot(onehot, table, precision=highest).reshape(A, tok, level_count * hg)
    expand = (
        jnp.arange(hg, dtype=jnp.int32)[:, None]
        == jnp.arange(cg, dtype=jnp.int32)[None, :] // head_dim
    ).astype(bf16)

    total = span
    prefix = jnp.zeros((A, hg), f32)
    prefixes = []
    up_factors = []
    for b in range(a_bits):
        wide = 2**b
        low_total, up_total = total[0::2], total[1::2]
        is_up = (jnp.arange(A, dtype=jnp.int32) // wide % 2 == 1)[:, None]
        prefixes.append(jnp.where(is_up, prefix, -jnp.inf))
        up_factors.append(jnp.exp(up_total))
        prefix = prefix + jnp.where(is_up, jnp.repeat(low_total, 2 * wide, axis=0), 0.0)
        total = low_total + up_total
    total = total[0]

    def level_scale(before, level):
        weight = lw[:, :, (2 + level) * hg : (3 + level) * hg]
        return jnp.exp(cum + before[:, None, :]) * weight

    end_scale = jnp.exp(span[:, None, :] - cum)
    up_rows = jnp.concatenate(up_factors, axis=0)
    *level_states, state = state_call(
        packed, end_scale, up_rows, expand, state_dim=state_dim, bits=a_bits
    )
    gate_blocks = gate_rows.reshape(tok, A, cg).swapaxes(0, 1)
    gate_blocks, state, total = lax.optimization_barrier((gate_blocks, state, total))
    gates = exchange(gate_blocks)
    local_scales = [lw[:, :, : 2 * hg]]
    local_scales += [level_scale(before, b) for b, before in enumerate(prefixes)]
    local_scales = jnp.concatenate(local_scales, axis=2)

    others, other_scales = [], []
    for zb in range(z_bits):
        other = xor_permute(state, A << zb)
        other_total = xor_permute(total[None, :], A << zb)[0]
        is_up = jnp.bitwise_and(jnp.right_shift(z_pos, zb), 1) == 1
        others.append(other)
        before = jnp.where(is_up, prefix, -jnp.inf)
        other_scales.append(level_scale(before, a_bits + zb))
        if zb + 1 < z_bits:
            up_state = jnp.where(is_up, state, other).astype(f32)
            low_state = jnp.where(is_up, other, state).astype(f32)
            factor = widen(jnp.exp(jnp.where(is_up, total, other_total)), head_dim)
            state = (up_state + factor[None, :] * low_state).astype(bf16)
            prefix = prefix + jnp.where(is_up, other_total, 0.0)[None, :]
            total = total + other_total

    for distance in range(2, Z // 2 + 1):
        above, others = lax.optimization_barrier((above, others))
        above = shift(above, 1)
        w_ring.append((distance, above))
        if 2 * distance < Z:
            below = shift(below, -1)
            w_ring.append((-distance, below))

    skip = widen(my_heads(skip_gain, hg, 0), head_dim)[None, :]
    mixed = local_call(
        packed, cum, cum.swapaxes(1, 2), local_scales, seg, level_states, skip, expand,
        state_dim=state_dim, head_dim=head_dim,
    )
    gain = my_heads(norm_gain, cg, 0)[None, :]
    hidden, squares = gate_call(
        packed, mixed, others, other_scales, gates, gain, expand, state_dim=state_dim
    )

    def reduce_group(part, order, narrow):
        left = list(range(a_bits))[::-1]
        part = part.reshape((2,) * a_bits + part.shape[1:])
        for b in order:
            axis = left.index(b)
            left.remove(b)
            bit = jnp.bitwise_and(jnp.right_shift(in_pos, b), 1)
            mine = lax.dynamic_index_in_dim(part, bit, axis, keepdims=False)
            theirs = lax.dynamic_index_in_dim(part, 1 - bit, axis, keepdims=False)
            part = mine + xor_permute(theirs.astype(narrow), 2**b).astype(f32)
        return part

    bits = list(range(a_bits))
    flipped = bits[:1] + bits[1:][::-1]
    square_sum = reduce_group(squares.reshape(A, tok), bits, f32)
    square_sum = lax.psum(square_sum, "head")
    inv_rms = lax.rsqrt(square_sum / inner_total + epsilon)[:, None]
    block_cols = A * out_cols
    out = jnp.zeros((tok, Z * block_cols), bf16)
    for step, (distance, w_part) in enumerate(w_ring):
        part = lax.dot_general(
            hidden, w_part, (((1,), (1,)), ((), ())), preferred_element_type=f32
        )
        part = reduce_group(
            part.reshape(A, tok, block_cols), flipped if step % 2 else bits, bf16
        )
        block = lax.rem(z_pos - distance + Z, Z)
        out = lax.dynamic_update_slice_in_dim(
            out, (part * inv_rms).astype(bf16), block * block_cols, 1
        )
    return lax.psum_scatter(out, "head", scatter_dimension=0, tiled=True)


def per_device(
    queries,
    key_rows,
    values,
    gate_rows,
    log_decay,
    skip_gain,
    lam_index,
    segments,
    lam_table,
    norm_gain,
    out_proj,
):
    sz = sizes_for(queries, values, log_decay, lam_table, out_proj)
    if sz is None:
        return split_device(
            queries, key_rows, values, gate_rows, log_decay, skip_gain,
            lam_index, segments, lam_table, norm_gain, out_proj,
        )
    return mixer_call(
        sz,
        out_proj.T,
        values,
        gate_rows,
        queries,
        key_rows,
        log_decay.T,
        lam_index[None, :],
        segments[None, :],
        lam_table.transpose(1, 0, 2),
        skip_gain[None, :],
        norm_gain[None, :],
    )


def solution(mesh):
    return jax.shard_map(
        per_device,
        mesh=mesh,
        in_specs=(
            P("seq", None),
            P("seq", None),
            P("seq", "head"),
            P("seq", "head"),
            P("seq", "head"),
            P("head"),
            P("seq"),
            P("seq"),
            P(None, None, "head"),
            P("head"),
            P("head", "seq"),
        ),
        out_specs=P(("seq", "head"), None),
        check_vma=False,
    )
```

```python
import math

import jax
import jax.numpy as jnp
from jax import lax
from jax.experimental import pallas as pl
from jax.experimental.pallas import tpu as pltpu
from jax.sharding import PartitionSpec as P

epsilon = 1e-05
highest = lax.Precision.HIGHEST
f32 = jnp.float32
bf16 = jnp.bfloat16


def xor_permute(value, mask):
    pairs = [(source, source ^ mask) for source in range(lax.axis_size("seq"))]
    return lax.ppermute(value, "seq", pairs)


def widen(matrix, head_dim):
    return jnp.repeat(matrix, head_dim, axis=-1)


def pack_kernel(groups, q_ref, k_ref, x_ref, decay_ref, lam_ref, seg_ref, out_ref):
    tok, state_dim = q_ref.shape
    cg = x_ref.shape[1] // groups
    hg = decay_ref.shape[1] // groups
    t_pos = lax.broadcasted_iota(jnp.int32, (tok, tok), 0)
    j_pos = lax.broadcasted_iota(jnp.int32, (tok, tok), 1)
    ones = jnp.where(t_pos >= j_pos, 1.0, 0.0).astype(f32)
    cum = jnp.dot(ones, decay_ref[...], precision=highest, preferred_element_type=f32)
    first = cum.astype(bf16).astype(f32)
    second = (cum - first).astype(bf16).astype(f32)
    third = cum - first - second
    pad = out_ref.shape[2] - 2 * state_dim - cg - 3 * hg - 2
    tail = [lam_ref[...], seg_ref[...], jnp.zeros((tok, pad), f32)]
    for s in range(groups):
        out_ref[s, :, :state_dim] = q_ref[...]
        out_ref[s, :, state_dim : 2 * state_dim] = k_ref[...]
        out_ref[s, :, 2 * state_dim : 2 * state_dim + cg] = x_ref[:, s * cg : (s + 1) * cg]
        parts = [part[:, s * hg : (s + 1) * hg] for part in (first, second, third)]
        small = jnp.concatenate(parts + tail, axis=1)
        out_ref[s, :, 2 * state_dim + cg :] = small.astype(bf16)


def pack_call(queries, key_rows, values, log_decay, lam, seg, *, groups):
    tok, state_dim = queries.shape
    width = 2 * state_dim + values.shape[1] // groups + 3 * (log_decay.shape[1] // groups) + 2
    vmem = pl.BlockSpec(memory_space=pltpu.VMEM)
    return pl.pallas_call(
        lambda *refs: pack_kernel(groups, *refs),
        out_shape=jax.ShapeDtypeStruct((groups, tok, pl.cdiv(width + 1, 128) * 128), bf16),
        in_specs=[vmem] * 6,
        out_specs=vmem,
        name="pack",
        cost_estimate=pl.CostEstimate(
            flops=1 << 22, bytes_accessed=4 << 20, transcendentals=0
        ),
    )(queries, key_rows, values, log_decay, lam, seg)


def spread(scale, expand):
    high = scale.astype(bf16)
    low = (scale - high.astype(f32)).astype(bf16)
    return jnp.dot(high, expand, preferred_element_type=f32) + jnp.dot(
        low, expand, preferred_element_type=f32
    )


def state_kernel(bits, state_dim, packed_ref, scale_ref, up_ref, expand_ref, *outs):
    A = packed_ref.shape[0]
    expand = expand_ref[...]
    up_wide = spread(up_ref[...], expand)
    for s in range(A):
        decayed = packed_ref[s, :, 2 * state_dim : 2 * state_dim + expand.shape[1]].astype(f32) * spread(scale_ref[s], expand)
        keys = packed_ref[s, :, state_dim : 2 * state_dim]
        outs[0][s] = lax.dot_general(
            keys,
            decayed.astype(bf16),
            (((0,), (0,)), ((), ())),
            preferred_element_type=f32,
        ).astype(bf16)
    row = 0
    for b in range(bits):
        for g in range(A >> (b + 1)):
            low = outs[b][2 * g].astype(f32)
            high = outs[b][2 * g + 1].astype(f32)
            merged = (high + up_wide[row : row + 1] * low).astype(bf16)
            if b + 1 < bits:
                outs[b + 1][g] = merged
            else:
                outs[b + 1][...] = merged
            row += 1


def state_call(packed, end_scale, up_rows, expand, *, state_dim, bits):
    A = packed.shape[0]
    cg = expand.shape[1]
    shapes = [(A >> b, state_dim, cg) for b in range(bits)] + [(state_dim, cg)]
    vmem = pl.BlockSpec(memory_space=pltpu.VMEM)
    return pl.pallas_call(
        lambda *refs: state_kernel(bits, state_dim, *refs),
        out_shape=[jax.ShapeDtypeStruct(shape, bf16) for shape in shapes],
        in_specs=[vmem] * 4,
        out_specs=[vmem] * len(shapes),
        name="group_states",
        cost_estimate=pl.CostEstimate(
            flops=1 << 29, bytes_accessed=8 << 20, transcendentals=0
        ),
    )(packed, end_scale, up_rows, expand)


def local_kernel(
    state_dim, head_dim, bits, packed_ref, cum_ref, cum_t_ref, scale_ref, seg_ref,
    seg_t_ref, skip_ref, expand_ref, *rest
):
    states, out_ref = rest[:bits], rest[bits]
    tok, hg = cum_ref.shape[1:]
    cg = expand_ref.shape[1]
    q = packed_ref[0, :, :state_dim]
    keys = packed_ref[0, :, state_dim : 2 * state_dim]
    expand = expand_ref[...]
    scores = lax.dot_general(
        q, keys, (((1,), (1,)), ((), ())), preferred_element_type=f32
    )
    same = seg_ref[0] == seg_t_ref[0]
    t_pos = lax.broadcasted_iota(jnp.int32, (tok, tok), 0)
    j_pos = lax.broadcasted_iota(jnp.int32, (tok, tok), 1)
    causal = t_pos >= j_pos
    scales = scale_ref[0]
    cum = cum_ref[0]
    cum_t = cum_t_ref[0]
    x_wide = packed_ref[0, :, 2 * state_dim : 2 * state_dim + cg]
    acc = skip_ref[...] * x_wide.astype(f32)
    for b in range(bits):
        read = jnp.dot(q, states[b][0], preferred_element_type=f32)
        acc = acc + read * spread(scales[:, (2 + b) * hg : (3 + b) * hg], expand)
    out_ref[...] = acc

    def head_weights(h):
        gaps = jnp.where(causal, cum[:, h : h + 1] - cum_t[h : h + 1, :], -jnp.inf)
        level_w = jnp.where(same, scales[:, h : h + 1], scales[:, hg + h : hg + h + 1])
        return (scores * jnp.exp(gaps) * level_w).astype(bf16)

    per_tile = max(1, 128 // head_dim)
    for first in range(0, hg, per_tile):
        heads = range(first, min(first + per_tile, hg))
        low, high = first * head_dim, min((first + per_tile) * head_dim, cg)
        x_tile = x_wide[:, low:high]
        lane_head = lax.broadcasted_iota(jnp.int32, (tok, high - low), 1) // head_dim
        tile = None
        for h in heads:
            part = jnp.dot(head_weights(h), x_tile, preferred_element_type=f32)
            tile = part if tile is None else jnp.where(lane_head == h - first, part, tile)
        out_ref[:, low:high] += tile


def local_call(
    packed, cum, cum_t, scales, seg, level_states, skip, expand, *, state_dim, head_dim
):
    A, tok, width = packed.shape
    cg = expand.shape[1]
    hg = cum.shape[2]
    bits = len(level_states)

    def shard_spec(*dims):
        return pl.BlockSpec((1,) + dims, lambda s: (s, 0, 0))

    def sibling_spec(b):
        return pl.BlockSpec(
            (1, state_dim, cg), lambda s: (jnp.maximum(s // 2**b - 1, 0), 0, 0)
        )

    def whole_spec(shape):
        return pl.BlockSpec(shape, lambda s: (0, 0))

    return pl.pallas_call(
        lambda *refs: local_kernel(state_dim, head_dim, bits, *refs),
        grid=(A,),
        out_shape=jax.ShapeDtypeStruct((A * tok, cg), f32),
        in_specs=[
            shard_spec(tok, width),
            shard_spec(tok, hg),
            shard_spec(hg, tok),
            shard_spec(tok, scales.shape[2]),
            shard_spec(tok, 1),
            shard_spec(1, tok),
            whole_spec((1, cg)),
            whole_spec(expand.shape),
        ]
        + [sibling_spec(b) for b in range(bits)],
        out_specs=pl.BlockSpec((tok, cg), lambda s: (s, 0)),
        name="local_mix",
        cost_estimate=pl.CostEstimate(
            flops=1 << 32, bytes_accessed=12 << 20, transcendentals=1 << 21
        ),
    )(packed, cum, cum_t, scales, seg[:, :, None], seg[:, None, :], skip, expand, *level_states)


def gate_kernel(levels, packed_ref, mixed_ref, scale_ref, gates_ref, gain_ref, expand_ref, *rest):
    others, (hidden_ref, square_ref) = rest[:levels], rest[levels:]
    hg = expand_ref.shape[0]
    q = packed_ref[0]
    expand = expand_ref[...]
    scales = scale_ref[0]
    acc = mixed_ref[...]
    for level in range(levels):
        read = jnp.dot(q, others[level][...], preferred_element_type=f32)
        acc = acc + read * spread(scales[:, level * hg : (level + 1) * hg], expand)
    gate = gates_ref[0].astype(f32)
    gated = acc * (gate / (1.0 + jnp.exp(-gate)))
    square_ref[0] = jnp.sum(gated * gated, axis=1, keepdims=True)
    hidden_ref[...] = (gated * gain_ref[...]).astype(bf16)


def gate_call(packed, mixed, others, other_scales, gates, gain, expand, *, state_dim):
    A, tok, cg = gates.shape
    levels = len(others)
    scales = jnp.concatenate(other_scales, axis=2)

    def shard_spec(*dims):
        return pl.BlockSpec((1,) + dims, lambda s: (s, 0, 0))

    def whole_spec(shape):
        return pl.BlockSpec(shape, lambda s: (0, 0))

    rows_spec = pl.BlockSpec((tok, cg), lambda s: (s, 0))
    return pl.pallas_call(
        lambda *refs: gate_kernel(levels, *refs),
        grid=(A,),
        out_shape=[
            jax.ShapeDtypeStruct((A * tok, cg), bf16),
            jax.ShapeDtypeStruct((A, tok, 1), f32),
        ],
        in_specs=[
            shard_spec(tok, state_dim),
            rows_spec,
            shard_spec(tok, scales.shape[2]),
            shard_spec(tok, cg),
            whole_spec((1, cg)),
            whole_spec(expand.shape),
        ]
        + [whole_spec((state_dim, cg))] * levels,
        out_specs=[rows_spec, shard_spec(tok, 1)],
        name="gate_mix",
        cost_estimate=pl.CostEstimate(
            flops=1 << 30, bytes_accessed=8 << 20, transcendentals=1 << 20
        ),
    )(packed, mixed, scales, gates, gain, expand, *others)


MESH = pl.DeviceIdType.MESH
decay_floor = -0.69


def bit_of(pos, b):
    return lax.rem(lax.div(pos, 2**b), 2)


def flip(pos, mask):
    out = pos
    for b in range(mask.bit_length()):
        if (mask >> b) & 1:
            out = out + (1 - 2 * bit_of(pos, b)) * 2**b
    return out


def flip_traced(pos, step, bits):
    out = 0
    for b in range(bits):
        out = out + lax.rem(bit_of(pos, b) + bit_of(step, b), 2) * 2**b
    return out


def dot_f32(a, b, dims=(((1,), (0,)), ((), ())), precision=None):
    return lax.dot_general(a, b, dims, precision=precision, preferred_element_type=f32)


NT = (((1,), (1,)), ((), ()))
TN = (((0,), (0,)), ((), ()))


class Sizes:
    def __init__(self, tok, state, cg, hg, oc, A, Z, levels):
        self.tok, self.state, self.cg, self.hg, self.oc = tok, state, cg, hg, oc
        self.A, self.Z, self.levels = A, Z, levels
        self.a_bits = A.bit_length() - 1
        self.z_bits = Z.bit_length() - 1
        self.hr = pl.cdiv(hg, 16) * 16
        self.half = tok // 2
        self.head_dim = cg // hg


def plane_partners(Z):
    pairs = {(a, a + 1) for a in range(Z - 1)}
    for b in range(Z.bit_length() - 1):
        for last in range(2**b - 1, Z, 2 ** (b + 1)):
            pairs |= {(last, last + step) for step in range(1, 2**b + 1)}
    pairs |= {(b, a) for a, b in pairs}
    return [sorted(b for a, b in pairs if a == zz) for zz in range(Z)]


def mixer_kernel(
    sz, wt_ref, v_ref, g_ref, q_in, k_in, dec_in, lam_in, seg_in, tab_in, skip_in, gain_in,
    out_ref,
    q_ref, k_ref, dec_ref, lam_ref, seg_ref, tab_ref, skip_ref, gain_ref,
    wbuf, xbuf, gbuf, qkbuf, smsend, smbuf, pre, aft, lwbuf, acc, lev, pst, zsend, zrecv, tsend, trecv,
    hid, sqsend, sqrecv, folds, scaled, expand, snd, rcv, keep,
    w_s, w_r, up_s, up_r, dn_s, dn_r, qk_s, qk_r, sm_s, sm_r, x_s, x_r, g_s, g_r,
    zs_s, zs_r, zt_s, zt_r, sq_s, sq_r, c_s, c_r, in_r,
):
    A, Z, tok, cg, hg, hr, oc = sz.A, sz.Z, sz.tok, sz.cg, sz.hg, sz.hr, sz.oc
    state, a_bits, z_bits, half, levels = sz.state, sz.a_bits, sz.z_bits, sz.half, sz.levels
    me = lax.axis_index("seq")
    p = lax.rem(me, A)
    z = lax.div(me, A)
    waits = []

    def dev(zz, pp):
        return {"seq": zz * A + pp}

    def cols(pos):
        return pl.ds(pl.multiple_of(pos * cg, cg), cg)

    def remote(src, dst, send, recv, device):
        return pltpu.make_async_remote_copy(
            src_ref=src, dst_ref=dst, send_sem=send, recv_sem=recv,
            device_id=device, device_id_type=MESH,
        )

    barrier = pltpu.get_barrier_semaphore()
    for d in range(1, A):
        pl.semaphore_signal(barrier, inc=1, device_id=dev(z, flip(p, d)), device_id_type=MESH)
    meets = plane_partners(Z)
    for zz in range(Z):
        @pl.when(z == zz)
        def _():
            for other in meets[zz]:
                pl.semaphore_signal(barrier, inc=1, device_id=dev(other, p), device_id_type=MESH)


    def piece(zz, pos):
        return wbuf.at[zz, pl.ds(pl.multiple_of(pos * oc, 16), oc)]

    own_w = pltpu.make_async_copy(wt_ref.at[:, cols(p)], piece(z, p), w_r.at[0])
    own_x = pltpu.make_async_copy(v_ref.at[:, cols(p)], xbuf.at[p], x_r.at[0])
    own_g = pltpu.make_async_copy(g_ref.at[:, cols(p)], gbuf.at[p], g_r.at[0, 0])
    own_w.start()
    own_x.start()
    own_g.start()
    small_in = [
        pltpu.make_async_copy(src, dst, in_r.at[n])
        for n, (src, dst) in enumerate([
            (k_in, k_ref), (q_in, q_ref), (dec_in, dec_ref), (lam_in, lam_ref), (seg_in, seg_ref),
            (tab_in, tab_ref), (skip_in, skip_ref), (gain_in, gain_ref),
        ])
    ]
    for copy in small_in:
        copy.start()
    for copy in small_in[:2]:
        copy.wait()
    qkbuf[p, 0] = q_ref[...]
    qkbuf[p, 1] = k_ref[...].astype(f32).T.astype(bf16)
    expected = A - 1
    for zz in range(Z):
        expected = expected + jnp.where(z == zz, len(meets[zz]), 0)
    pl.semaphore_wait(barrier, expected)

    def start(copy):
        copy.start()
        waits.append(copy)
        return copy

    def up_copy(src, h, pos, dst=None):
        return remote(src, src if dst is None else dst, up_s.at[h, pos], up_r.at[h, pos], dev(z + 1, p))

    def dn_copy(src, h, pos, dst=None):
        return remote(src, src if dst is None else dst, dn_s.at[h, pos], dn_r.at[h, pos], dev(z - 1, p))

    def send_own(src, pos):
        @pl.when(z + 1 < Z)
        def _():
            up_copy(src, 0, pos, piece(z, pos)).start()

        @pl.when(z >= 1)
        def _():
            dn_copy(src, 0, pos, piece(z, pos)).start()

    order = list(range(1, A))
    relayed = [d for d in order if d % 2 == 0]
    direct = [1] + relayed
    w_cp, qk_cp, sm_cp, x_cp, g_cp = {}, {}, {}, {}, {}
    send_own(wt_ref.at[:, cols(p)], p)
    for d in order:
        t = flip(p, d)
        w_cp[d] = start(remote(wt_ref.at[:, cols(t)], piece(z, p), w_s.at[d], w_r.at[d], dev(z, t)))

    for copy in small_in[2:]:
        copy.wait()

    heads = dec_ref.shape[0]
    row_id = lax.broadcasted_iota(jnp.int32, (A * hr, heads), 0)
    head_id = lax.broadcasted_iota(jnp.int32, (A * hr, heads), 1)
    local_row = lax.rem(row_id, hr)
    place = (local_row < hg) & (lax.div(row_id, hr) * hg + local_row == head_id)
    placed = dot_f32(jnp.where(place, 1.0, 0.0).astype(f32), dec_ref[...], precision=highest)
    j_pos = lax.broadcasted_iota(jnp.int32, (tok, tok), 0)
    t_pos = lax.broadcasted_iota(jnp.int32, (tok, tok), 1)
    cum_all = dot_f32(placed, jnp.where(j_pos <= t_pos, 1.0, 0.0).astype(f32), precision=highest)
    for s in range(A):
        smsend[s, :hr] = cum_all[s * hr : (s + 1) * hr]
        smsend[s, hr : hr + 1] = lam_ref[...].astype(f32)
        smsend[s, hr + 1 : hr + 2] = seg_ref[...].astype(f32)
        smsend[s, hr + 2 : hr + 8] = jnp.zeros((6, tok), f32)
    smbuf[p] = smsend[p]
    for d in order:
        t = flip(p, d)
        sm_cp[d] = start(remote(smsend.at[t], smbuf.at[p], sm_s.at[d], sm_r.at[d], dev(z, t)))
    for d in direct:
        qk_cp[d] = start(remote(qkbuf.at[p], qkbuf.at[p], qk_s.at[d], qk_r.at[d], dev(z, flip(p, d))))
    for d in order:
        t = flip(p, d)
        x_cp[d] = start(remote(v_ref.at[:, cols(t)], xbuf.at[p], x_s.at[d], x_r.at[d], dev(z, t)))
    rows_of = [pl.ds(th * half, half) for th in range(2)]
    for th in range(2):
        for d in order:
            t = flip(p, d)
            g_cp[th, d] = start(
                remote(g_ref.at[rows_of[th], cols(t)], gbuf.at[p, rows_of[th]], g_s.at[th, d], g_r.at[th, d], dev(z, t))
            )

    pick_row = lax.broadcasted_iota(jnp.int32, (hr, heads), 0)
    pick_head = lax.broadcasted_iota(jnp.int32, (hr, heads), 1)
    pick = jnp.where((pick_row < hg) & (pick_row + p * hg == pick_head), 1.0, 0.0).astype(f32)
    table = jnp.concatenate(
        [dot_f32(pick, tab_ref[l], NT, precision=highest) for l in range(levels)], axis=0
    )
    e_row = lax.broadcasted_iota(jnp.int32, (2 * hr, cg), 0)
    e_col = lax.broadcasted_iota(jnp.int32, (2 * hr, cg), 1)
    expand[...] = jnp.where(lax.rem(e_row, hr) == lax.div(e_col, sz.head_dim), 1.0, 0.0).astype(bf16)

    def spread(rows):
        high = rows.astype(bf16)
        low = (rows - high.astype(f32)).astype(bf16)
        return dot_f32(jnp.concatenate([high, low], axis=0), expand[...], TN)

    def spread_row(column):
        return spread(jnp.broadcast_to(column, (hr, 8)))[:1]

    skip_rows = jnp.sum(pick * skip_ref[...], axis=1, keepdims=True)
    skip_wide = spread_row(skip_rows)
    gain = gain_ref[:, cols(p)]

    for d in order:
        w_cp[d].wait_recv()
        send_own(piece(z, flip(p, d)), flip(p, d))

    def hop(h, positions):
        for pos in positions:
            @pl.when(z - 1 - h >= 0)
            def _():
                up_copy(piece(z - 1 - h, pos), h, pos).wait_recv()

            if h + 2 < Z:
                @pl.when((z - 1 - h >= 0) & (z + 1 < Z))
                def _():
                    up_copy(piece(z - 1 - h, pos), h + 1, pos).start()

            @pl.when(z + 1 + h < Z)
            def _():
                dn_copy(piece(z + 1 + h, pos), h, pos).wait_recv()

            if h + 2 < Z:
                @pl.when((z + 1 + h < Z) & (z >= 1))
                def _():
                    dn_copy(piece(z + 1 + h, pos), h + 1, pos).start()

    def hop_sends_done():
        for h in range(Z - 1):
            for pos in range(A):
                @pl.when((z - h >= 0) & (z + 1 < Z))
                def _():
                    up_copy(piece(z - h, pos), h, pos).wait_send()

                @pl.when((z + h < Z) & (z >= 1))
                def _():
                    dn_copy(piece(z + h, pos), h, pos).wait_send()

    for d in order:
        sm_cp[d].wait_recv()
    ends = [smbuf[s, :hr, tok - 1 : tok] for s in range(A)]
    running = jnp.zeros((hr, 1), f32)
    for s in range(A):
        pre[s] = jnp.broadcast_to(running, (hr, tok))
        running = running + ends[s]
    total = running
    running = jnp.zeros((hr, 1), f32)
    for s in reversed(range(A)):
        aft[s] = jnp.broadcast_to(running, (hr, tok))
        running = running + ends[s]

    for d in relayed:
        qk_cp[d].wait_recv()
        there = qkbuf.at[flip(p, d)]
        qk_cp[d + 1] = start(remote(there, there, qk_s.at[d + 1], qk_r.at[d + 1], dev(z, flip(p, 1))))
    early, middle, late = list(range(A))[: A - 3], list(range(A))[A - 3 : A - 1], list(range(A))[A - 1 :]
    hop(0, early)

    causal = j_pos >= t_pos
    class_id = lax.broadcasted_iota(jnp.int32, (tab_ref.shape[1], tok), 0).astype(f32)
    pst[...] = jnp.zeros(pst.shape, f32)

    def state_pass(s):
        c = smbuf[s, :hr]
        mid = c[:, half - 1 : half]
        scaled[s] = (xbuf[s].astype(f32) * spread(jnp.exp(mid - c))).astype(bf16)
        end = dot_f32(qkbuf[s, 1], scaled[s]) * spread_row(jnp.exp(c[:, tok - 1 : tok] - mid))
        lev[0][s] = end.astype(bf16)
        pst[...] += end * spread_row(jnp.exp(aft[s, :, :1]))

    def local_pass(s):
        c = smbuf[s, :hr]
        onehot = jnp.where(smbuf[s, hr : hr + 1] == class_id, 1.0, 0.0).astype(f32)
        lw = dot_f32(table, onehot, precision=highest)
        lwbuf[s] = lw
        seg_row = jnp.broadcast_to(smbuf[s, hr + 1 : hr + 2], (tok, tok))
        same = seg_row == seg_row.T
        scores = dot_f32(qkbuf[s, 0], qkbuf[s, 1])
        s_same = jnp.where(causal & same, scores, 0.0).astype(bf16)
        s_diff = jnp.where(causal & jnp.logical_not(same), scores, 0.0).astype(bf16)
        big = dot_f32(jnp.concatenate([s_same, s_diff], axis=0), scaled[s])
        later = jnp.exp(c - c[:, half - 1 : half])
        acc[s] = (
            skip_wide * xbuf[s].astype(f32)
            + spread(later * lw[:hr]) * big[:tok]
            + spread(later * lw[hr : 2 * hr]) * big[tok:]
        )

    for d in range(A):
        if d == 0:
            own_x.wait()
        else:
            x_cp[d].wait_recv()
            if d not in relayed:
                qk_cp[d].wait_recv()
        state_pass(flip(p, d))

    split = pl.cdiv(cg // 128, 2) * 128
    sides = [pl.ds(0, split), pl.ds(split, cg - split)] if split < cg else [pl.ds(0, cg)]

    def z_copies(b, step, side):
        there = dev(z + step, p)
        copies = [
            remote(
                zsend.at[b, :, sides[side]], zrecv.at[b, :, sides[side]],
                zs_s.at[b, step, side], zs_r.at[b, side], there,
            )
        ]
        if side == 0:
            copies.insert(0, remote(tsend.at[b], trecv.at[b], zt_s.at[b, step], zt_r.at[b], there))
        return copies

    def is_last(b):
        return lax.rem(z, 2 ** (b + 1)) == 2**b - 1

    def z_send(b, side):
        for step in range(2**b, 0, -1):
            for copy in z_copies(b, step, side):
                copy.start()

    def z_sent(b):
        @pl.when(is_last(b))
        def _():
            for side in range(len(sides)):
                for step in range(2**b, 0, -1):
                    for copy in z_copies(b, step, side):
                        copy.wait_send()

    def z_wait(b, side):
        @pl.when(bit_of(z, b) == 1)
        def _():
            for copy in z_copies(b, 1, side):
                copy.wait_recv()

    total_wide = jnp.broadcast_to(total, (hr, tok))

    @pl.when(is_last(0))
    def _():
        zsend[0] = pst[...].astype(bf16)
        tsend[0] = total_wide
        for side in range(len(sides)):
            z_send(0, side)

    hop(0, middle)
    for s in range(A):
        local_pass(s)

    for b in range(a_bits - 1):
        for g in range(A >> (b + 1)):
            if g % 2 == 0:
                up_total = sum(ends[s] for s in range((2 * g + 1) << b, (2 * g + 2) << b))
                merged = lev[b][2 * g + 1].astype(f32) + spread_row(jnp.exp(up_total)) * lev[b][2 * g].astype(f32)
                lev[b + 1][g] = merged.astype(bf16)
            elif b + 2 < a_bits:
                up_total = sum(ends[s] for s in range((2 * g + 1) << b, (2 * g + 2) << b))
                merged = lev[b][2 * g + 1].astype(f32) + spread_row(jnp.exp(up_total)) * lev[b][2 * g].astype(f32)
                lev[b + 1][g] = merged.astype(bf16)
    for s in range(1, A):
        more = None
        for b in range(a_bits):
            if (s >> b) & 1:
                first = (s >> b) << b
                before = sum((ends[j] for j in range(first, s)), jnp.zeros((hr, 1), f32))
                scale = jnp.exp(smbuf[s, :hr] + before) * lwbuf[s, (2 + b) * hr : (3 + b) * hr]
                term = spread(scale) * dot_f32(qkbuf[s, 0], lev[b][(s >> b) - 1])
                more = term if more is None else more + term
        acc[s] += more

    for b in range(z_bits - 1):
        for side, where in enumerate(sides):
            z_wait(b, side)

            @pl.when(lax.rem(z, 2 ** (b + 1)) == 2 ** (b + 1) - 1)
            def _():
                mine = pst[:, where] if b == 0 else zsend[b, :, where].astype(f32)
                mine_total = total_wide if b == 0 else tsend[b]
                factor = spread_row(jnp.exp(mine_total[:, :1]))[:, where.start : where.start + where.size]
                zsend[b + 1, :, where] = (mine + factor * zrecv[b, :, where].astype(f32)).astype(bf16)
                if side == 0:
                    tsend[b + 1] = mine_total + trecv[b]

            @pl.when(is_last(b + 1))
            def _():
                z_send(b + 1, side)

    hop(0, late)
    if Z > 2:
        hop(1, early)

    z_prefix = jnp.zeros((hr, tok), f32)

    def z_pass(b, z_prefix):
        @pl.when(bit_of(z, b) == 1)
        def _():
            def body(s, carry):
                level = 2 + a_bits + b
                scale = jnp.exp(smbuf[s, :hr] + pre[s] + z_prefix) * lwbuf[s, level * hr : (level + 1) * hr]
                acc[s] += spread(scale) * dot_f32(qkbuf[s, 0], zrecv[b])
                return carry

            lax.fori_loop(0, A, body, 0, unroll=True)

    for b in range(z_bits):
        if b == z_bits - 1:
            for side in range(len(sides)):
                z_wait(b, side)
        z_pass(b, z_prefix)
        if b + 1 < z_bits:
            z_prefix = z_prefix + jnp.where(bit_of(z, b) == 1, trecv[b], 0.0)
        if b == 0 and Z > 2:
            hop(1, middle)

    def gate_pass(th):
        def body(s, carry):
            gate = gbuf[s, rows_of[th]].astype(f32)
            half_gate = 0.5 * gate
            gated = acc[s, rows_of[th]] * (half_gate + half_gate * jnp.tanh(half_gate))
            square = gated * gated
            folded = square[:, :128]
            for first in range(128, cg, 128):
                folded = folded + square[:, first : first + 128]
            folds[s, rows_of[th]] = folded
            hid[lax.div(s, 2), lax.rem(s, 2), rows_of[th]] = (gated * gain).astype(bf16)
            return carry

        if th == 0:
            own_g.wait()
        for d in order:
            g_cp[th, d].wait_recv()
        lax.fori_loop(0, A, body, 0, unroll=True)

    sq_cp = {}

    def send_squares():
        for s in range(A):
            sqsend[s] = dot_f32(jnp.ones((8, 128), f32), folds[s], NT, precision=highest)
        for d in order:
            t = flip(p, d)
            sq_cp[d] = start(remote(sqsend.at[t], sqrecv.at[p], sq_s.at[d], sq_r.at[d], dev(z, t)))
        sqrecv[p] = sqsend[p]

    bit0 = bit_of(p, 0)
    sequence = [list(range(a_bits)), [0] + list(range(1, a_bits))[::-1]]
    parts = projection_parts(sz)

    def block_of(k):
        out = 0
        for zz in range(Z):
            near = sorted(range(Z), key=lambda other: (abs(other - zz), other))
            out = jnp.where(z == zz, near[k], out)
        return out

    def path(i, th):
        return sequence[(i + th) % 2]

    def stage_copy(t, i, th):
        b = path(i, th)[t]
        return remote(
            snd[i][t].at[th], rcv[i][t].at[th], c_s.at[t, 2 * i + th], c_r.at[t, 2 * i + th],
            dev(z, flip(p, 1 << b)),
        )

    def multiply(i, th):
        k, first, width = parts[i]
        weights = wbuf[block_of(k), first : first + width]
        rows = A // 2 * half
        lhs = jnp.concatenate(
            [hid[:, bit, rows_of[th]].reshape(rows, cg) for bit in (1 - bit0, bit0)], axis=0
        )
        product = dot_f32(lhs, weights, NT)
        shape = snd[i][0].shape[1:]
        snd[i][0][th] = product[:rows].astype(bf16).reshape(shape)
        stage_copy(0, i, th).start()
        keep[i][0][th] = product[rows:].reshape(shape)

    def pick_half(ref, th, left, b, bit):
        axis = left.index(b)
        return ref[(th,) + (slice(None),) * axis + (bit,)]

    def fold(t, i, th):
        seq = path(i, th)
        left = [b for b in range(a_bits)[::-1] if b not in seq[: t + 1]]
        stage_copy(t, i, th).wait_recv()
        b = seq[t + 1]
        bit = bit_of(p, b)
        kept, got = keep[i][t], rcv[i][t]
        out = pick_half(kept, th, left, b, 1 - bit) + pick_half(got, th, left, b, 1 - bit).astype(f32)
        snd[i][t + 1][th] = out.astype(bf16)
        stage_copy(t + 1, i, th).start()
        keep[i][t + 1][th] = pick_half(kept, th, left, b, bit) + pick_half(got, th, left, b, bit).astype(f32)

    inverse = {}

    def finish(i, th):
        if not inverse:
            for d in order:
                sq_cp[d].wait_recv()
            gathered = jnp.concatenate([sqrecv[s, :1] for s in range(A)], axis=0)
            sums = dot_f32(gathered, jnp.ones((A, 128), f32), TN, precision=highest)
            inverse[0] = lax.rsqrt(sums / (A * cg) + epsilon)
        t = a_bits - 1
        k, first, width = parts[i]
        stage_copy(t, i, th).wait_recv()
        value = keep[i][t][th] + rcv[i][t][th].astype(f32)
        scale = jnp.concatenate([inverse[0][th * half : (th + 1) * half]] * (width // 128), axis=1)
        column = pl.multiple_of(block_of(k) * (A * oc) + first, 128)
        out_ref[rows_of[th], pl.ds(column, width)] = (value * scale).astype(out_ref.dtype)

    last = parts[-1][0]
    here = [i for i in range(len(parts)) if parts[i][0] < last]
    done = {}

    def run(i, th, upto):
        for stage in range(done.get((i, th), -1) + 1, upto + 1):
            if stage == 0:
                multiply(i, th)
            elif stage < a_bits:
                fold(stage - 1, i, th)
            else:
                finish(i, th)
            done[i, th] = stage

    own_w.wait()
    gate_pass(0)
    run(0, 0, 0)
    run(1, 0, 0)
    run(0, 0, 1)
    gate_pass(1)
    run(0, 1, 0)
    run(1, 0, 1)
    run(1, 1, 0)
    run(0, 1, 1)
    send_squares()
    if Z > 2:
        hop(1, late)
    fresh = [(1, 1)]
    for i in here[2:]:
        for th in range(2):
            run(i, th, 0)
            run(*fresh.pop(), 1)
            fresh.append((i, th))
    run(*fresh.pop(), 1)
    units = [(i, th) for i in here for th in range(2)]
    ending = [i for i in range(len(parts)) if i not in here]
    seen = 0

    def close(count):
        for stage in range(2, a_bits):
            for unit in units[:count]:
                if done[unit] < stage:
                    run(*unit, stage)

    for n, i in enumerate(ending):
        close(2 + 2 * n)
        need = pl.cdiv(parts[i][1] + parts[i][2], oc)
        hop(Z - 2, range(seen, need))
        seen = need
        run(i, 0, 0)
        run(i, 1, 0)
        run(i, 0, 1)
        run(i, 1, 1)
    units += [(i, th) for i in ending for th in range(2)]
    for stage in range(2, a_bits + 1):
        for unit in units:
            run(*unit, max(done[unit], stage))

    for copy in waits:
        copy.wait_send()
    hop_sends_done()
    for b in range(z_bits):
        z_sent(b)
    for i in range(len(parts)):
        for th in range(2):
            for t in range(a_bits):
                stage_copy(t, i, th).wait_send()


def projection_parts(sz):
    width = sz.A * sz.oc
    parts = [(k, 0, width) for k in range(sz.Z - 1)]
    first = pl.cdiv(width // 128, 2) * 128
    parts.append((sz.Z - 1, 0, first))
    if first < width:
        parts.append((sz.Z - 1, first, width - first))
    return parts


def mixer_call(sz, wt, values, gates, queries, keys, decay_t, lam, seg, table, skip, gain):
    A, Z, tok, cg, hr, oc = sz.A, sz.Z, sz.tok, sz.cg, sz.hr, sz.oc
    a_bits, z_bits, half, state = sz.a_bits, sz.z_bits, sz.half, sz.state
    hbm = pl.BlockSpec(memory_space=pl.ANY)
    vmem = pl.BlockSpec(memory_space=pltpu.VMEM)
    parts = projection_parts(sz)

    def stages(kind):
        return [
            [pltpu.VMEM((2,) + (2,) * (a_bits - 1 - t) + (half, width), kind) for t in range(a_bits)]
            for _, _, width in parts
        ]

    dma = pltpu.SemaphoreType.DMA
    smalls = [queries, keys, decay_t, lam, seg, table, skip, gain]
    scratch = [pltpu.VMEM(a.shape, a.dtype) for a in smalls] + [
        pltpu.VMEM((Z, A * oc, cg), bf16),
        pltpu.VMEM((A, tok, cg), bf16),
        pltpu.VMEM((A, tok, cg), bf16),
        pltpu.VMEM((A, 2, tok, state), bf16),
        pltpu.VMEM((A, hr + 8, tok), f32),
        pltpu.VMEM((A, hr + 8, tok), f32),
        pltpu.VMEM((A, hr, tok), f32),
        pltpu.VMEM((A, hr, tok), f32),
        pltpu.VMEM((A, sz.levels * hr, tok), f32),
        pltpu.VMEM((A, tok, cg), f32),
        [pltpu.VMEM((A >> b, state, cg), bf16) for b in range(a_bits)],
        pltpu.VMEM((state, cg), f32),
        pltpu.VMEM((z_bits, state, cg), bf16),
        pltpu.VMEM((z_bits, state, cg), bf16),
        pltpu.VMEM((z_bits, hr, tok), f32),
        pltpu.VMEM((z_bits, hr, tok), f32),
        pltpu.VMEM((A // 2, 2, tok, cg), bf16),
        pltpu.VMEM((A, 8, tok), f32),
        pltpu.VMEM((A, 8, tok), f32),
        pltpu.VMEM((A, tok, 128), f32),
        pltpu.VMEM((A, tok, cg), bf16),
        pltpu.VMEM((2 * hr, cg), bf16),
        stages(bf16),
        stages(bf16),
        stages(f32),
        dma((A,)), dma((A,)),
        dma((Z, A)), dma((Z, A)), dma((Z, A)), dma((Z, A)),
        dma((A,)), dma((A,)), dma((A,)), dma((A,)), dma((A,)), dma((A,)), dma((2, A)), dma((2, A)),
        dma((z_bits, Z, 2)), dma((z_bits, 2)), dma((z_bits, Z)), dma((z_bits,)),
        dma((A,)), dma((A,)),
        dma((a_bits, 2 * len(parts))), dma((a_bits, 2 * len(parts))),
        dma((len(smalls),)),
    ]
    return pl.pallas_call(
        lambda *refs: mixer_kernel(sz, *refs),
        out_shape=jax.ShapeDtypeStruct((tok, Z * A * oc), bf16),
        in_specs=[hbm] * 11,
        out_specs=vmem,
        scratch_shapes=scratch,
        name="mixer",
        cost_estimate=pl.CostEstimate(flops=1 << 32, bytes_accessed=32 << 20, transcendentals=1 << 21),
        compiler_params=pltpu.CompilerParams(
            collective_id=0, has_side_effects=True, vmem_limit_bytes=56 << 20
        ),
    )(wt, values, gates, queries, keys, decay_t, lam, seg, table, skip, gain)


def sizes_for(queries, values, log_decay, lam_table, out_proj):
    tok, state = queries.shape
    heads = log_decay.shape[1]
    count = lax.axis_size("seq")
    A = math.gcd(math.gcd(heads, 8), count)
    Z = count // A
    cg = values.shape[1] // A
    oc = out_proj.shape[1]
    fits = lax.axis_size("head") == 1 and A > 1 and Z > 1 and Z & (Z - 1) == 0
    fits = fits and cg % 128 == 0 and oc % 16 == 0 and (A * oc) % 128 == 0
    fits = fits and tok == 128 and state == 128 and -decay_floor * tok / 2 < 60
    if not fits:
        return None
    return Sizes(tok, state, cg, heads // A, oc, A, Z, lam_table.shape[1])


def split_device(
    queries,
    key_rows,
    values,
    gate_rows,
    log_decay,
    skip_gain,
    lam_index,
    segments,
    lam_table,
    norm_gain,
    out_proj,
):
    tok, state_dim = queries.shape
    head_count = log_decay.shape[1]
    cols = values.shape[1]
    head_dim = cols // head_count
    classes, level_count = lam_table.shape[:2]
    dev_count = lax.axis_size("seq")
    inner_total = cols * lax.axis_size("head")
    A = math.gcd(math.gcd(head_count, 8), dev_count)
    Z = dev_count // A
    a_bits = A.bit_length() - 1
    z_bits = Z.bit_length() - 1
    hg = head_count // A
    cg = hg * head_dim
    rows = A * tok
    out_cols = out_proj.shape[1]
    groups = [[z * A + i for i in range(A)] for z in range(Z)]
    me = lax.axis_index("seq")
    in_pos = lax.rem(me, A)
    z_pos = lax.div(me, A)

    def exchange(blocks):
        return lax.all_to_all(
            blocks, "seq", 0, 0, tiled=True, axis_index_groups=groups
        )

    def my_heads(array, width, axis):
        return lax.dynamic_slice_in_dim(array, in_pos * width, width, axis)

    w_blocks = out_proj.T.reshape(out_cols, A, cg).swapaxes(0, 1)
    w_block = exchange(w_blocks).reshape(A * out_cols, cg)

    packed = pack_call(
        queries,
        key_rows,
        values,
        log_decay,
        lam_index.astype(f32)[:, None],
        segments.astype(f32)[:, None],
        groups=A,
    )
    packed = exchange(packed)
    small = packed[:, :, 2 * state_dim + cg :].astype(f32)

    def shift(block, step):
        pairs = [(p, (p + step * A) % dev_count) for p in range(dev_count)]
        return lax.ppermute(block, "seq", pairs)

    w_ring = [(0, w_block)]
    above = below = w_block
    if Z > 1:
        above = shift(w_block, 1)
        w_ring.append((1, above))
    if Z > 2:
        below = shift(w_block, -1)
        w_ring.append((-1, below))

    cum = small[:, :, :hg] + small[:, :, hg : 2 * hg] + small[:, :, 2 * hg : 3 * hg]
    lam = small[:, :, 3 * hg].reshape(rows).astype(jnp.int32)
    seg = small[:, :, 3 * hg + 1]
    span = cum[:, -1, :]
    onehot = (lam[:, None] == jnp.arange(classes, dtype=jnp.int32)[None, :]).astype(f32)
    table = my_heads(lam_table, hg, 2).reshape(classes, level_count * hg)
    lw = jnp.dot(onehot, table, precision=highest).reshape(A, tok, level_count * hg)
    expand = (
        jnp.arange(hg, dtype=jnp.int32)[:, None]
        == jnp.arange(cg, dtype=jnp.int32)[None, :] // head_dim
    ).astype(bf16)

    total = span
    prefix = jnp.zeros((A, hg), f32)
    prefixes = []
    up_factors = []
    for b in range(a_bits):
        wide = 2**b
        low_total, up_total = total[0::2], total[1::2]
        is_up = (jnp.arange(A, dtype=jnp.int32) // wide % 2 == 1)[:, None]
        prefixes.append(jnp.where(is_up, prefix, -jnp.inf))
        up_factors.append(jnp.exp(up_total))
        prefix = prefix + jnp.where(is_up, jnp.repeat(low_total, 2 * wide, axis=0), 0.0)
        total = low_total + up_total
    total = total[0]

    def level_scale(before, level):
        weight = lw[:, :, (2 + level) * hg : (3 + level) * hg]
        return jnp.exp(cum + before[:, None, :]) * weight

    end_scale = jnp.exp(span[:, None, :] - cum)
    up_rows = jnp.concatenate(up_factors, axis=0)
    *level_states, state = state_call(
        packed, end_scale, up_rows, expand, state_dim=state_dim, bits=a_bits
    )
    gate_blocks = gate_rows.reshape(tok, A, cg).swapaxes(0, 1)
    gate_blocks, state, total = lax.optimization_barrier((gate_blocks, state, total))
    gates = exchange(gate_blocks)
    local_scales = [lw[:, :, : 2 * hg]]
    local_scales += [level_scale(before, b) for b, before in enumerate(prefixes)]
    local_scales = jnp.concatenate(local_scales, axis=2)

    others, other_scales = [], []
    for zb in range(z_bits):
        other = xor_permute(state, A << zb)
        other_total = xor_permute(total[None, :], A << zb)[0]
        is_up = jnp.bitwise_and(jnp.right_shift(z_pos, zb), 1) == 1
        others.append(other)
        before = jnp.where(is_up, prefix, -jnp.inf)
        other_scales.append(level_scale(before, a_bits + zb))
        if zb + 1 < z_bits:
            up_state = jnp.where(is_up, state, other).astype(f32)
            low_state = jnp.where(is_up, other, state).astype(f32)
            factor = widen(jnp.exp(jnp.where(is_up, total, other_total)), head_dim)
            state = (up_state + factor[None, :] * low_state).astype(bf16)
            prefix = prefix + jnp.where(is_up, other_total, 0.0)[None, :]
            total = total + other_total

    for distance in range(2, Z // 2 + 1):
        above, others = lax.optimization_barrier((above, others))
        above = shift(above, 1)
        w_ring.append((distance, above))
        if 2 * distance < Z:
            below = shift(below, -1)
            w_ring.append((-distance, below))

    skip = widen(my_heads(skip_gain, hg, 0), head_dim)[None, :]
    mixed = local_call(
        packed, cum, cum.swapaxes(1, 2), local_scales, seg, level_states, skip, expand,
        state_dim=state_dim, head_dim=head_dim,
    )
    gain = my_heads(norm_gain, cg, 0)[None, :]
    hidden, squares = gate_call(
        packed, mixed, others, other_scales, gates, gain, expand, state_dim=state_dim
    )

    def reduce_group(part, order, narrow):
        left = list(range(a_bits))[::-1]
        part = part.reshape((2,) * a_bits + part.shape[1:])
        for b in order:
            axis = left.index(b)
            left.remove(b)
            bit = jnp.bitwise_and(jnp.right_shift(in_pos, b), 1)
            mine = lax.dynamic_index_in_dim(part, bit, axis, keepdims=False)
            theirs = lax.dynamic_index_in_dim(part, 1 - bit, axis, keepdims=False)
            part = mine + xor_permute(theirs.astype(narrow), 2**b).astype(f32)
        return part

    bits = list(range(a_bits))
    flipped = bits[:1] + bits[1:][::-1]
    square_sum = reduce_group(squares.reshape(A, tok), bits, f32)
    square_sum = lax.psum(square_sum, "head")
    inv_rms = lax.rsqrt(square_sum / inner_total + epsilon)[:, None]
    block_cols = A * out_cols
    out = jnp.zeros((tok, Z * block_cols), bf16)
    for step, (distance, w_part) in enumerate(w_ring):
        part = lax.dot_general(
            hidden, w_part, (((1,), (1,)), ((), ())), preferred_element_type=f32
        )
        part = reduce_group(
            part.reshape(A, tok, block_cols), flipped if step % 2 else bits, bf16
        )
        block = lax.rem(z_pos - distance + Z, Z)
        out = lax.dynamic_update_slice_in_dim(
            out, (part * inv_rms).astype(bf16), block * block_cols, 1
        )
    return lax.psum_scatter(out, "head", scatter_dimension=0, tiled=True)


def per_device(
    queries,
    key_rows,
    values,
    gate_rows,
    log_decay,
    skip_gain,
    lam_index,
    segments,
    lam_table,
    norm_gain,
    out_proj,
):
    sz = sizes_for(queries, values, log_decay, lam_table, out_proj)
    if sz is None:
        return split_device(
            queries, key_rows, values, gate_rows, log_decay, skip_gain,
            lam_index, segments, lam_table, norm_gain, out_proj,
        )
    return mixer_call(
        sz,
        out_proj.T,
        values,
        gate_rows,
        queries,
        key_rows,
        log_decay.T,
        lam_index[None, :],
        segments[None, :],
        lam_table.transpose(1, 0, 2),
        skip_gain[None, :],
        norm_gain[None, :],
    )


def solution(mesh):
    return jax.shard_map(
        per_device,
        mesh=mesh,
        in_specs=(
            P("seq", None),
            P("seq", None),
            P("seq", "head"),
            P("seq", "head"),
            P("seq", "head"),
            P("head"),
            P("seq"),
            P("seq"),
            P(None, None, "head"),
            P("head"),
            P("head", "seq"),
        ),
        out_specs=P(("seq", "head"), None),
        check_vma=False,
    )
```

```python
import math

import jax
import jax.numpy as jnp
from jax import lax
from jax.experimental import pallas as pl
from jax.experimental.pallas import tpu as pltpu
from jax.sharding import PartitionSpec as P

epsilon = 1e-05
highest = lax.Precision.HIGHEST
f32 = jnp.float32
bf16 = jnp.bfloat16


def xor_permute(value, mask):
    pairs = [(source, source ^ mask) for source in range(lax.axis_size("seq"))]
    return lax.ppermute(value, "seq", pairs)


def widen(matrix, head_dim):
    return jnp.repeat(matrix, head_dim, axis=-1)


def pack_kernel(groups, q_ref, k_ref, x_ref, decay_ref, lam_ref, seg_ref, out_ref):
    tok, state_dim = q_ref.shape
    cg = x_ref.shape[1] // groups
    hg = decay_ref.shape[1] // groups
    t_pos = lax.broadcasted_iota(jnp.int32, (tok, tok), 0)
    j_pos = lax.broadcasted_iota(jnp.int32, (tok, tok), 1)
    ones = jnp.where(t_pos >= j_pos, 1.0, 0.0).astype(f32)
    cum = jnp.dot(ones, decay_ref[...], precision=highest, preferred_element_type=f32)
    first = cum.astype(bf16).astype(f32)
    second = (cum - first).astype(bf16).astype(f32)
    third = cum - first - second
    pad = out_ref.shape[2] - 2 * state_dim - cg - 3 * hg - 2
    tail = [lam_ref[...], seg_ref[...], jnp.zeros((tok, pad), f32)]
    for s in range(groups):
        out_ref[s, :, :state_dim] = q_ref[...]
        out_ref[s, :, state_dim : 2 * state_dim] = k_ref[...]
        out_ref[s, :, 2 * state_dim : 2 * state_dim + cg] = x_ref[:, s * cg : (s + 1) * cg]
        parts = [part[:, s * hg : (s + 1) * hg] for part in (first, second, third)]
        small = jnp.concatenate(parts + tail, axis=1)
        out_ref[s, :, 2 * state_dim + cg :] = small.astype(bf16)


def pack_call(queries, key_rows, values, log_decay, lam, seg, *, groups):
    tok, state_dim = queries.shape
    width = 2 * state_dim + values.shape[1] // groups + 3 * (log_decay.shape[1] // groups) + 2
    vmem = pl.BlockSpec(memory_space=pltpu.VMEM)
    return pl.pallas_call(
        lambda *refs: pack_kernel(groups, *refs),
        out_shape=jax.ShapeDtypeStruct((groups, tok, pl.cdiv(width + 1, 128) * 128), bf16),
        in_specs=[vmem] * 6,
        out_specs=vmem,
        name="pack",
        cost_estimate=pl.CostEstimate(
            flops=1 << 22, bytes_accessed=4 << 20, transcendentals=0
        ),
    )(queries, key_rows, values, log_decay, lam, seg)


def spread(scale, expand):
    high = scale.astype(bf16)
    low = (scale - high.astype(f32)).astype(bf16)
    return jnp.dot(high, expand, preferred_element_type=f32) + jnp.dot(
        low, expand, preferred_element_type=f32
    )


def state_kernel(bits, state_dim, packed_ref, scale_ref, up_ref, expand_ref, *outs):
    A = packed_ref.shape[0]
    expand = expand_ref[...]
    up_wide = spread(up_ref[...], expand)
    for s in range(A):
        decayed = packed_ref[s, :, 2 * state_dim : 2 * state_dim + expand.shape[1]].astype(f32) * spread(scale_ref[s], expand)
        keys = packed_ref[s, :, state_dim : 2 * state_dim]
        outs[0][s] = lax.dot_general(
            keys,
            decayed.astype(bf16),
            (((0,), (0,)), ((), ())),
            preferred_element_type=f32,
        ).astype(bf16)
    row = 0
    for b in range(bits):
        for g in range(A >> (b + 1)):
            low = outs[b][2 * g].astype(f32)
            high = outs[b][2 * g + 1].astype(f32)
            merged = (high + up_wide[row : row + 1] * low).astype(bf16)
            if b + 1 < bits:
                outs[b + 1][g] = merged
            else:
                outs[b + 1][...] = merged
            row += 1


def state_call(packed, end_scale, up_rows, expand, *, state_dim, bits):
    A = packed.shape[0]
    cg = expand.shape[1]
    shapes = [(A >> b, state_dim, cg) for b in range(bits)] + [(state_dim, cg)]
    vmem = pl.BlockSpec(memory_space=pltpu.VMEM)
    return pl.pallas_call(
        lambda *refs: state_kernel(bits, state_dim, *refs),
        out_shape=[jax.ShapeDtypeStruct(shape, bf16) for shape in shapes],
        in_specs=[vmem] * 4,
        out_specs=[vmem] * len(shapes),
        name="group_states",
        cost_estimate=pl.CostEstimate(
            flops=1 << 29, bytes_accessed=8 << 20, transcendentals=0
        ),
    )(packed, end_scale, up_rows, expand)


def local_kernel(
    state_dim, head_dim, bits, packed_ref, cum_ref, cum_t_ref, scale_ref, seg_ref,
    seg_t_ref, skip_ref, expand_ref, *rest
):
    states, out_ref = rest[:bits], rest[bits]
    tok, hg = cum_ref.shape[1:]
    cg = expand_ref.shape[1]
    q = packed_ref[0, :, :state_dim]
    keys = packed_ref[0, :, state_dim : 2 * state_dim]
    expand = expand_ref[...]
    scores = lax.dot_general(
        q, keys, (((1,), (1,)), ((), ())), preferred_element_type=f32
    )
    same = seg_ref[0] == seg_t_ref[0]
    t_pos = lax.broadcasted_iota(jnp.int32, (tok, tok), 0)
    j_pos = lax.broadcasted_iota(jnp.int32, (tok, tok), 1)
    causal = t_pos >= j_pos
    scales = scale_ref[0]
    cum = cum_ref[0]
    cum_t = cum_t_ref[0]
    x_wide = packed_ref[0, :, 2 * state_dim : 2 * state_dim + cg]
    acc = skip_ref[...] * x_wide.astype(f32)
    for b in range(bits):
        read = jnp.dot(q, states[b][0], preferred_element_type=f32)
        acc = acc + read * spread(scales[:, (2 + b) * hg : (3 + b) * hg], expand)
    out_ref[...] = acc

    def head_weights(h):
        gaps = jnp.where(causal, cum[:, h : h + 1] - cum_t[h : h + 1, :], -jnp.inf)
        level_w = jnp.where(same, scales[:, h : h + 1], scales[:, hg + h : hg + h + 1])
        return (scores * jnp.exp(gaps) * level_w).astype(bf16)

    per_tile = max(1, 128 // head_dim)
    for first in range(0, hg, per_tile):
        heads = range(first, min(first + per_tile, hg))
        low, high = first * head_dim, min((first + per_tile) * head_dim, cg)
        x_tile = x_wide[:, low:high]
        lane_head = lax.broadcasted_iota(jnp.int32, (tok, high - low), 1) // head_dim
        tile = None
        for h in heads:
            part = jnp.dot(head_weights(h), x_tile, preferred_element_type=f32)
            tile = part if tile is None else jnp.where(lane_head == h - first, part, tile)
        out_ref[:, low:high] += tile


def local_call(
    packed, cum, cum_t, scales, seg, level_states, skip, expand, *, state_dim, head_dim
):
    A, tok, width = packed.shape
    cg = expand.shape[1]
    hg = cum.shape[2]
    bits = len(level_states)

    def shard_spec(*dims):
        return pl.BlockSpec((1,) + dims, lambda s: (s, 0, 0))

    def sibling_spec(b):
        return pl.BlockSpec(
            (1, state_dim, cg), lambda s: (jnp.maximum(s // 2**b - 1, 0), 0, 0)
        )

    def whole_spec(shape):
        return pl.BlockSpec(shape, lambda s: (0, 0))

    return pl.pallas_call(
        lambda *refs: local_kernel(state_dim, head_dim, bits, *refs),
        grid=(A,),
        out_shape=jax.ShapeDtypeStruct((A * tok, cg), f32),
        in_specs=[
            shard_spec(tok, width),
            shard_spec(tok, hg),
            shard_spec(hg, tok),
            shard_spec(tok, scales.shape[2]),
            shard_spec(tok, 1),
            shard_spec(1, tok),
            whole_spec((1, cg)),
            whole_spec(expand.shape),
        ]
        + [sibling_spec(b) for b in range(bits)],
        out_specs=pl.BlockSpec((tok, cg), lambda s: (s, 0)),
        name="local_mix",
        cost_estimate=pl.CostEstimate(
            flops=1 << 32, bytes_accessed=12 << 20, transcendentals=1 << 21
        ),
    )(packed, cum, cum_t, scales, seg[:, :, None], seg[:, None, :], skip, expand, *level_states)


def gate_kernel(levels, packed_ref, mixed_ref, scale_ref, gates_ref, gain_ref, expand_ref, *rest):
    others, (hidden_ref, square_ref) = rest[:levels], rest[levels:]
    hg = expand_ref.shape[0]
    q = packed_ref[0]
    expand = expand_ref[...]
    scales = scale_ref[0]
    acc = mixed_ref[...]
    for level in range(levels):
        read = jnp.dot(q, others[level][...], preferred_element_type=f32)
        acc = acc + read * spread(scales[:, level * hg : (level + 1) * hg], expand)
    gate = gates_ref[0].astype(f32)
    gated = acc * (gate / (1.0 + jnp.exp(-gate)))
    square_ref[0] = jnp.sum(gated * gated, axis=1, keepdims=True)
    hidden_ref[...] = (gated * gain_ref[...]).astype(bf16)


def gate_call(packed, mixed, others, other_scales, gates, gain, expand, *, state_dim):
    A, tok, cg = gates.shape
    levels = len(others)
    scales = jnp.concatenate(other_scales, axis=2)

    def shard_spec(*dims):
        return pl.BlockSpec((1,) + dims, lambda s: (s, 0, 0))

    def whole_spec(shape):
        return pl.BlockSpec(shape, lambda s: (0, 0))

    rows_spec = pl.BlockSpec((tok, cg), lambda s: (s, 0))
    return pl.pallas_call(
        lambda *refs: gate_kernel(levels, *refs),
        grid=(A,),
        out_shape=[
            jax.ShapeDtypeStruct((A * tok, cg), bf16),
            jax.ShapeDtypeStruct((A, tok, 1), f32),
        ],
        in_specs=[
            shard_spec(tok, state_dim),
            rows_spec,
            shard_spec(tok, scales.shape[2]),
            shard_spec(tok, cg),
            whole_spec((1, cg)),
            whole_spec(expand.shape),
        ]
        + [whole_spec((state_dim, cg))] * levels,
        out_specs=[rows_spec, shard_spec(tok, 1)],
        name="gate_mix",
        cost_estimate=pl.CostEstimate(
            flops=1 << 30, bytes_accessed=8 << 20, transcendentals=1 << 20
        ),
    )(packed, mixed, scales, gates, gain, expand, *others)


MESH = pl.DeviceIdType.MESH
decay_floor = -0.69


def bit_of(pos, b):
    return lax.rem(lax.div(pos, 2**b), 2)


def flip(pos, mask):
    out = pos
    for b in range(mask.bit_length()):
        if (mask >> b) & 1:
            out = out + (1 - 2 * bit_of(pos, b)) * 2**b
    return out


def flip_traced(pos, step, bits):
    out = 0
    for b in range(bits):
        out = out + lax.rem(bit_of(pos, b) + bit_of(step, b), 2) * 2**b
    return out


def dot_f32(a, b, dims=(((1,), (0,)), ((), ())), precision=None):
    return lax.dot_general(a, b, dims, precision=precision, preferred_element_type=f32)


NT = (((1,), (1,)), ((), ()))
TN = (((0,), (0,)), ((), ()))


class Sizes:
    def __init__(self, tok, state, cg, hg, oc, A, Z, levels):
        self.tok, self.state, self.cg, self.hg, self.oc = tok, state, cg, hg, oc
        self.A, self.Z, self.levels = A, Z, levels
        self.a_bits = A.bit_length() - 1
        self.z_bits = Z.bit_length() - 1
        self.hr = pl.cdiv(hg, 16) * 16
        self.half = tok // 2
        self.head_dim = cg // hg


def plane_partners(Z):
    pairs = {(a, a + 1) for a in range(Z - 1)}
    for b in range(Z.bit_length() - 1):
        for last in range(2**b - 1, Z, 2 ** (b + 1)):
            pairs |= {(last, last + step) for step in range(1, 2**b + 1)}
    pairs |= {(b, a) for a, b in pairs}
    return [sorted(b for a, b in pairs if a == zz) for zz in range(Z)]


def mixer_kernel(
    sz, wt_ref, v_ref, g_ref, q_in, k_in, dec_in, lam_in, seg_in, tab_in, skip_in, gain_in,
    out_ref,
    q_ref, k_ref, dec_ref, lam_ref, seg_ref, tab_ref, skip_ref, gain_ref,
    wbuf, xbuf, gbuf, qkbuf, smsend, smbuf, pre, aft, lwbuf, acc, lev, pst, zsend, zrecv, tsend, trecv,
    hid, sqsend, sqrecv, folds, scaled, expand, snd, rcv, keep,
    w_s, w_r, up_s, up_r, dn_s, dn_r, qk_s, qk_r, sm_s, sm_r, x_s, x_r, g_s, g_r,
    zs_s, zs_r, zt_s, zt_r, sq_s, sq_r, c_s, c_r, in_r,
):
    A, Z, tok, cg, hg, hr, oc = sz.A, sz.Z, sz.tok, sz.cg, sz.hg, sz.hr, sz.oc
    state, a_bits, z_bits, half, levels = sz.state, sz.a_bits, sz.z_bits, sz.half, sz.levels
    me = lax.axis_index("seq")
    p = lax.rem(me, A)
    z = lax.div(me, A)
    waits = []

    def dev(zz, pp):
        return {"seq": zz * A + pp}

    def cols(pos):
        return pl.ds(pl.multiple_of(pos * cg, cg), cg)

    def remote(src, dst, send, recv, device):
        return pltpu.make_async_remote_copy(
            src_ref=src, dst_ref=dst, send_sem=send, recv_sem=recv,
            device_id=device, device_id_type=MESH,
        )

    barrier = pltpu.get_barrier_semaphore()
    for d in range(1, A):
        pl.semaphore_signal(barrier, inc=1, device_id=dev(z, flip(p, d)), device_id_type=MESH)
    meets = plane_partners(Z)
    for zz in range(Z):
        @pl.when(z == zz)
        def _():
            for other in meets[zz]:
                pl.semaphore_signal(barrier, inc=1, device_id=dev(other, p), device_id_type=MESH)


    def piece(zz, pos):
        return wbuf.at[zz, pl.ds(pl.multiple_of(pos * oc, 16), oc)]

    own_w = pltpu.make_async_copy(wt_ref.at[:, cols(p)], piece(z, p), w_r.at[0])
    own_x = pltpu.make_async_copy(v_ref.at[:, cols(p)], xbuf.at[p], x_r.at[0])
    own_g = pltpu.make_async_copy(g_ref.at[:, cols(p)], gbuf.at[p], g_r.at[0, 0])
    own_w.start()
    own_x.start()
    own_g.start()
    small_in = [
        pltpu.make_async_copy(src, dst, in_r.at[n])
        for n, (src, dst) in enumerate([
            (k_in, k_ref), (q_in, q_ref), (dec_in, dec_ref), (lam_in, lam_ref), (seg_in, seg_ref),
            (tab_in, tab_ref), (skip_in, skip_ref), (gain_in, gain_ref),
        ])
    ]
    for copy in small_in:
        copy.start()
    for copy in small_in[:2]:
        copy.wait()
    qkbuf[p, 0] = q_ref[...]
    qkbuf[p, 1] = k_ref[...].astype(f32).T.astype(bf16)
    expected = A - 1
    for zz in range(Z):
        expected = expected + jnp.where(z == zz, len(meets[zz]), 0)
    pl.semaphore_wait(barrier, expected)

    def start(copy):
        copy.start()
        waits.append(copy)
        return copy

    def up_copy(src, h, pos, dst=None):
        return remote(src, src if dst is None else dst, up_s.at[h, pos], up_r.at[h, pos], dev(z + 1, p))

    def dn_copy(src, h, pos, dst=None):
        return remote(src, src if dst is None else dst, dn_s.at[h, pos], dn_r.at[h, pos], dev(z - 1, p))

    def send_own(src, pos):
        @pl.when(z + 1 < Z)
        def _():
            up_copy(src, 0, pos, piece(z, pos)).start()

        @pl.when(z >= 1)
        def _():
            dn_copy(src, 0, pos, piece(z, pos)).start()

    order = list(range(1, A))
    relayed = [d for d in order if d % 2 == 0]
    direct = [1] + relayed
    w_cp, qk_cp, sm_cp, x_cp, g_cp = {}, {}, {}, {}, {}
    send_own(wt_ref.at[:, cols(p)], p)
    for d in order:
        t = flip(p, d)
        w_cp[d] = start(remote(wt_ref.at[:, cols(t)], piece(z, p), w_s.at[d], w_r.at[d], dev(z, t)))

    for copy in small_in[2:]:
        copy.wait()

    heads = dec_ref.shape[0]
    row_id = lax.broadcasted_iota(jnp.int32, (A * hr, heads), 0)
    head_id = lax.broadcasted_iota(jnp.int32, (A * hr, heads), 1)
    local_row = lax.rem(row_id, hr)
    place = (local_row < hg) & (lax.div(row_id, hr) * hg + local_row == head_id)
    placed = dot_f32(jnp.where(place, 1.0, 0.0).astype(f32), dec_ref[...], precision=highest)
    j_pos = lax.broadcasted_iota(jnp.int32, (tok, tok), 0)
    t_pos = lax.broadcasted_iota(jnp.int32, (tok, tok), 1)
    cum_all = dot_f32(placed, jnp.where(j_pos <= t_pos, 1.0, 0.0).astype(f32), precision=highest)
    for s in range(A):
        smsend[s, :hr] = cum_all[s * hr : (s + 1) * hr]
        smsend[s, hr : hr + 1] = lam_ref[...].astype(f32)
        smsend[s, hr + 1 : hr + 2] = seg_ref[...].astype(f32)
        smsend[s, hr + 2 : hr + 8] = jnp.zeros((6, tok), f32)
    smbuf[p] = smsend[p]
    for d in order:
        t = flip(p, d)
        sm_cp[d] = start(remote(smsend.at[t], smbuf.at[p], sm_s.at[d], sm_r.at[d], dev(z, t)))
    for d in direct:
        qk_cp[d] = start(remote(qkbuf.at[p], qkbuf.at[p], qk_s.at[d], qk_r.at[d], dev(z, flip(p, d))))
    for d in order:
        t = flip(p, d)
        x_cp[d] = start(remote(v_ref.at[:, cols(t)], xbuf.at[p], x_s.at[d], x_r.at[d], dev(z, t)))
    rows_of = [pl.ds(th * half, half) for th in range(2)]
    for th in range(2):
        for d in order:
            t = flip(p, d)
            g_cp[th, d] = start(
                remote(g_ref.at[rows_of[th], cols(t)], gbuf.at[p, rows_of[th]], g_s.at[th, d], g_r.at[th, d], dev(z, t))
            )

    pick_row = lax.broadcasted_iota(jnp.int32, (hr, heads), 0)
    pick_head = lax.broadcasted_iota(jnp.int32, (hr, heads), 1)
    pick = jnp.where((pick_row < hg) & (pick_row + p * hg == pick_head), 1.0, 0.0).astype(f32)
    table = jnp.concatenate(
        [dot_f32(pick, tab_ref[l], NT, precision=highest) for l in range(levels)], axis=0
    )
    e_row = lax.broadcasted_iota(jnp.int32, (2 * hr, cg), 0)
    e_col = lax.broadcasted_iota(jnp.int32, (2 * hr, cg), 1)
    expand[...] = jnp.where(lax.rem(e_row, hr) == lax.div(e_col, sz.head_dim), 1.0, 0.0).astype(bf16)

    def spread(rows):
        high = rows.astype(bf16)
        low = (rows - high.astype(f32)).astype(bf16)
        return dot_f32(jnp.concatenate([high, low], axis=0), expand[...], TN)

    def spread_row(column):
        return spread(jnp.broadcast_to(column, (hr, 8)))[:1]

    skip_rows = jnp.sum(pick * skip_ref[...], axis=1, keepdims=True)
    skip_wide = spread_row(skip_rows)
    gain = gain_ref[:, cols(p)]

    for d in order:
        w_cp[d].wait_recv()
        send_own(piece(z, flip(p, d)), flip(p, d))

    def hop(h, positions):
        for pos in positions:
            @pl.when(z - 1 - h >= 0)
            def _():
                up_copy(piece(z - 1 - h, pos), h, pos).wait_recv()

            if h + 2 < Z:
                @pl.when((z - 1 - h >= 0) & (z + 1 < Z))
                def _():
                    up_copy(piece(z - 1 - h, pos), h + 1, pos).start()

            @pl.when(z + 1 + h < Z)
            def _():
                dn_copy(piece(z + 1 + h, pos), h, pos).wait_recv()

            if h + 2 < Z:
                @pl.when((z + 1 + h < Z) & (z >= 1))
                def _():
                    dn_copy(piece(z + 1 + h, pos), h + 1, pos).start()

    def hop_sends_done():
        for h in range(Z - 1):
            for pos in range(A):
                @pl.when((z - h >= 0) & (z + 1 < Z))
                def _():
                    up_copy(piece(z - h, pos), h, pos).wait_send()

                @pl.when((z + h < Z) & (z >= 1))
                def _():
                    dn_copy(piece(z + h, pos), h, pos).wait_send()

    for d in order:
        sm_cp[d].wait_recv()
    ends = [smbuf[s, :hr, tok - 1 : tok] for s in range(A)]
    running = jnp.zeros((hr, 1), f32)
    for s in range(A):
        pre[s] = jnp.broadcast_to(running, (hr, tok))
        running = running + ends[s]
    total = running
    running = jnp.zeros((hr, 1), f32)
    for s in reversed(range(A)):
        aft[s] = jnp.broadcast_to(running, (hr, tok))
        running = running + ends[s]

    for d in relayed:
        qk_cp[d].wait_recv()
        there = qkbuf.at[flip(p, d)]
        qk_cp[d + 1] = start(remote(there, there, qk_s.at[d + 1], qk_r.at[d + 1], dev(z, flip(p, 1))))
    early, middle, late = list(range(A))[: A - 3], list(range(A))[A - 3 : A - 1], list(range(A))[A - 1 :]
    hop(0, early)

    causal = j_pos >= t_pos
    class_id = lax.broadcasted_iota(jnp.int32, (tab_ref.shape[1], tok), 0).astype(f32)
    pst[...] = jnp.zeros(pst.shape, f32)

    def state_pass(s):
        c = smbuf[s, :hr]
        mid = c[:, half - 1 : half]
        scaled[s] = (xbuf[s].astype(f32) * spread(jnp.exp(mid - c))).astype(bf16)
        end = dot_f32(qkbuf[s, 1], scaled[s]) * spread_row(jnp.exp(c[:, tok - 1 : tok] - mid))
        lev[0][s] = end.astype(bf16)
        pst[...] += end * spread_row(jnp.exp(aft[s, :, :1]))

    def local_pass(s):
        c = smbuf[s, :hr]
        onehot = jnp.where(smbuf[s, hr : hr + 1] == class_id, 1.0, 0.0).astype(f32)
        lw = dot_f32(table, onehot, precision=highest)
        lwbuf[s] = lw
        seg_row = jnp.broadcast_to(smbuf[s, hr + 1 : hr + 2], (tok, tok))
        same = seg_row == seg_row.T
        scores = dot_f32(qkbuf[s, 0], qkbuf[s, 1])
        s_same = jnp.where(causal & same, scores, 0.0).astype(bf16)
        s_diff = jnp.where(causal & jnp.logical_not(same), scores, 0.0).astype(bf16)
        big = dot_f32(jnp.concatenate([s_same, s_diff], axis=0), scaled[s])
        later = jnp.exp(c - c[:, half - 1 : half])
        acc[s] = (
            skip_wide * xbuf[s].astype(f32)
            + spread(later * lw[:hr]) * big[:tok]
            + spread(later * lw[hr : 2 * hr]) * big[tok:]
        )

    for d in range(A):
        if d == 0:
            own_x.wait()
        else:
            x_cp[d].wait_recv()
            if d not in relayed:
                qk_cp[d].wait_recv()
        state_pass(flip(p, d))

    split = pl.cdiv(cg // 128, 2) * 128
    sides = [pl.ds(0, split), pl.ds(split, cg - split)] if split < cg else [pl.ds(0, cg)]

    def z_copies(b, step, side):
        there = dev(z + step, p)
        copies = [
            remote(
                zsend.at[b, :, sides[side]], zrecv.at[b, :, sides[side]],
                zs_s.at[b, step, side], zs_r.at[b, side], there,
            )
        ]
        if side == 0:
            copies.insert(0, remote(tsend.at[b], trecv.at[b], zt_s.at[b, step], zt_r.at[b], there))
        return copies

    def is_last(b):
        return lax.rem(z, 2 ** (b + 1)) == 2**b - 1

    def z_send(b, side):
        for step in range(2**b, 0, -1):
            for copy in z_copies(b, step, side):
                copy.start()

    def z_sent(b):
        @pl.when(is_last(b))
        def _():
            for side in range(len(sides)):
                for step in range(2**b, 0, -1):
                    for copy in z_copies(b, step, side):
                        copy.wait_send()

    def z_wait(b, side):
        @pl.when(bit_of(z, b) == 1)
        def _():
            for copy in z_copies(b, 1, side):
                copy.wait_recv()

    total_wide = jnp.broadcast_to(total, (hr, tok))

    @pl.when(is_last(0))
    def _():
        zsend[0] = pst[...].astype(bf16)
        tsend[0] = total_wide
        for side in range(len(sides)):
            z_send(0, side)

    hop(0, middle)
    for s in range(A):
        local_pass(s)

    for b in range(a_bits - 1):
        for g in range(A >> (b + 1)):
            if g % 2 == 0:
                up_total = sum(ends[s] for s in range((2 * g + 1) << b, (2 * g + 2) << b))
                merged = lev[b][2 * g + 1].astype(f32) + spread_row(jnp.exp(up_total)) * lev[b][2 * g].astype(f32)
                lev[b + 1][g] = merged.astype(bf16)
            elif b + 2 < a_bits:
                up_total = sum(ends[s] for s in range((2 * g + 1) << b, (2 * g + 2) << b))
                merged = lev[b][2 * g + 1].astype(f32) + spread_row(jnp.exp(up_total)) * lev[b][2 * g].astype(f32)
                lev[b + 1][g] = merged.astype(bf16)
    for s in range(1, A):
        more = None
        for b in range(a_bits):
            if (s >> b) & 1:
                first = (s >> b) << b
                before = sum((ends[j] for j in range(first, s)), jnp.zeros((hr, 1), f32))
                scale = jnp.exp(smbuf[s, :hr] + before) * lwbuf[s, (2 + b) * hr : (3 + b) * hr]
                term = spread(scale) * dot_f32(qkbuf[s, 0], lev[b][(s >> b) - 1])
                more = term if more is None else more + term
        acc[s] += more

    for b in range(z_bits - 1):
        for side, where in enumerate(sides):
            z_wait(b, side)

            @pl.when(lax.rem(z, 2 ** (b + 1)) == 2 ** (b + 1) - 1)
            def _():
                mine = pst[:, where] if b == 0 else zsend[b, :, where].astype(f32)
                mine_total = total_wide if b == 0 else tsend[b]
                factor = spread_row(jnp.exp(mine_total[:, :1]))[:, where.start : where.start + where.size]
                zsend[b + 1, :, where] = (mine + factor * zrecv[b, :, where].astype(f32)).astype(bf16)
                if side == 0:
                    tsend[b + 1] = mine_total + trecv[b]

            @pl.when(is_last(b + 1))
            def _():
                z_send(b + 1, side)

    hop(0, late)
    if Z > 2:
        hop(1, early)

    z_prefix = jnp.zeros((hr, tok), f32)

    def z_pass(b, z_prefix):
        @pl.when(bit_of(z, b) == 1)
        def _():
            def body(s, carry):
                level = 2 + a_bits + b
                scale = jnp.exp(smbuf[s, :hr] + pre[s] + z_prefix) * lwbuf[s, level * hr : (level + 1) * hr]
                acc[s] += spread(scale) * dot_f32(qkbuf[s, 0], zrecv[b])
                return carry

            lax.fori_loop(0, A, body, 0, unroll=True)

    for b in range(z_bits):
        if b == z_bits - 1:
            for side in range(len(sides)):
                z_wait(b, side)
        z_pass(b, z_prefix)
        if b + 1 < z_bits:
            z_prefix = z_prefix + jnp.where(bit_of(z, b) == 1, trecv[b], 0.0)
        if b == 0 and Z > 2:
            hop(1, middle)

    def gate_pass(th):
        def body(s, carry):
            gate = gbuf[s, rows_of[th]].astype(f32)
            half_gate = 0.5 * gate
            gated = acc[s, rows_of[th]] * (half_gate + half_gate * jnp.tanh(half_gate))
            square = gated * gated
            folded = square[:, :128]
            for first in range(128, cg, 128):
                folded = folded + square[:, first : first + 128]
            folds[s, rows_of[th]] = folded
            hid[lax.div(s, 2), lax.rem(s, 2), rows_of[th]] = (gated * gain).astype(bf16)
            return carry

        if th == 0:
            own_g.wait()
        for d in order:
            g_cp[th, d].wait_recv()
        lax.fori_loop(0, A, body, 0, unroll=True)

    sq_cp = {}

    def send_squares():
        for s in range(A):
            sqsend[s] = dot_f32(jnp.ones((8, 128), f32), folds[s], NT, precision=highest)
        for d in order:
            t = flip(p, d)
            sq_cp[d] = start(remote(sqsend.at[t], sqrecv.at[p], sq_s.at[d], sq_r.at[d], dev(z, t)))
        sqrecv[p] = sqsend[p]

    bit0 = bit_of(p, 0)
    sequence = [list(range(a_bits)), [0] + list(range(1, a_bits))[::-1]]
    parts = projection_parts(sz)

    def block_of(k):
        out = 0
        for zz in range(Z):
            near = sorted(range(Z), key=lambda other: (abs(other - zz), other))
            out = jnp.where(z == zz, near[k], out)
        return out

    def path(i, th):
        return sequence[(i + th) % 2]

    def stage_copy(t, i, th):
        b = path(i, th)[t]
        return remote(
            snd[i][t].at[th], rcv[i][t].at[th], c_s.at[t, 2 * i + th], c_r.at[t, 2 * i + th],
            dev(z, flip(p, 1 << b)),
        )

    def multiply(i, th):
        k, first, width = parts[i]
        weights = wbuf[block_of(k), first : first + width]
        rows = A // 2 * half
        lhs = jnp.concatenate(
            [hid[:, bit, rows_of[th]].reshape(rows, cg) for bit in (1 - bit0, bit0)], axis=0
        )
        product = dot_f32(lhs, weights, NT)
        shape = snd[i][0].shape[1:]
        snd[i][0][th] = product[:rows].astype(bf16).reshape(shape)
        stage_copy(0, i, th).start()
        keep[i][0][th] = product[rows:].reshape(shape)

    def pick_half(ref, th, left, b, bit):
        axis = left.index(b)
        return ref[(th,) + (slice(None),) * axis + (bit,)]

    def fold(t, i, th):
        seq = path(i, th)
        left = [b for b in range(a_bits)[::-1] if b not in seq[: t + 1]]
        stage_copy(t, i, th).wait_recv()
        b = seq[t + 1]
        bit = bit_of(p, b)
        kept, got = keep[i][t], rcv[i][t]
        out = pick_half(kept, th, left, b, 1 - bit) + pick_half(got, th, left, b, 1 - bit).astype(f32)
        snd[i][t + 1][th] = out.astype(bf16)
        stage_copy(t + 1, i, th).start()
        keep[i][t + 1][th] = pick_half(kept, th, left, b, bit) + pick_half(got, th, left, b, bit).astype(f32)

    inverse = {}

    def finish(i, th):
        if not inverse:
            for d in order:
                sq_cp[d].wait_recv()
            gathered = jnp.concatenate([sqrecv[s, :1] for s in range(A)], axis=0)
            sums = dot_f32(gathered, jnp.ones((A, 128), f32), TN, precision=highest)
            inverse[0] = lax.rsqrt(sums / (A * cg) + epsilon)
        t = a_bits - 1
        k, first, width = parts[i]
        stage_copy(t, i, th).wait_recv()
        value = keep[i][t][th] + rcv[i][t][th].astype(f32)
        scale = jnp.concatenate([inverse[0][th * half : (th + 1) * half]] * (width // 128), axis=1)
        column = pl.multiple_of(block_of(k) * (A * oc) + first, 128)
        out_ref[rows_of[th], pl.ds(column, width)] = (value * scale).astype(out_ref.dtype)

    last = parts[-1][0]
    here = [i for i in range(len(parts)) if parts[i][0] < last]
    done = {}

    def run(i, th, upto):
        for stage in range(done.get((i, th), -1) + 1, upto + 1):
            if stage == 0:
                multiply(i, th)
            elif stage < a_bits:
                fold(stage - 1, i, th)
            else:
                finish(i, th)
            done[i, th] = stage

    own_w.wait()
    gate_pass(0)
    run(0, 0, 0)
    run(1, 0, 0)
    run(0, 0, 1)
    gate_pass(1)
    run(0, 1, 0)
    run(1, 0, 1)
    run(1, 1, 0)
    run(0, 1, 1)
    if Z > 2:
        hop(1, late)
    fresh = [(1, 1)]
    for i in here[2:]:
        for th in range(2):
            run(i, th, 0)
            run(*fresh.pop(), 1)
            fresh.append((i, th))
    run(*fresh.pop(), 1)
    send_squares()
    units = [(i, th) for i in here for th in range(2)]
    ending = [i for i in range(len(parts)) if i not in here]
    seen = 0

    def close(count):
        for stage in range(2, a_bits):
            for unit in units[:count]:
                if done[unit] < stage:
                    run(*unit, stage)

    for n, i in enumerate(ending):
        close(2 + 2 * n)
        need = pl.cdiv(parts[i][1] + parts[i][2], oc)
        hop(Z - 2, range(seen, need))
        seen = need
        run(i, 0, 0)
        run(i, 1, 0)
        run(i, 0, 1)
        run(i, 1, 1)
    units += [(i, th) for i in ending for th in range(2)]
    for stage in range(2, a_bits + 1):
        for unit in units:
            run(*unit, max(done[unit], stage))

    for copy in waits:
        copy.wait_send()
    hop_sends_done()
    for b in range(z_bits):
        z_sent(b)
    for i in range(len(parts)):
        for th in range(2):
            for t in range(a_bits):
                stage_copy(t, i, th).wait_send()


def projection_parts(sz):
    width = sz.A * sz.oc
    parts = [(k, 0, width) for k in range(sz.Z - 1)]
    first = pl.cdiv(width // 128, 2) * 128
    parts.append((sz.Z - 1, 0, first))
    if first < width:
        parts.append((sz.Z - 1, first, width - first))
    return parts


def mixer_call(sz, wt, values, gates, queries, keys, decay_t, lam, seg, table, skip, gain):
    A, Z, tok, cg, hr, oc = sz.A, sz.Z, sz.tok, sz.cg, sz.hr, sz.oc
    a_bits, z_bits, half, state = sz.a_bits, sz.z_bits, sz.half, sz.state
    hbm = pl.BlockSpec(memory_space=pl.ANY)
    vmem = pl.BlockSpec(memory_space=pltpu.VMEM)
    parts = projection_parts(sz)

    def stages(kind):
        return [
            [pltpu.VMEM((2,) + (2,) * (a_bits - 1 - t) + (half, width), kind) for t in range(a_bits)]
            for _, _, width in parts
        ]

    dma = pltpu.SemaphoreType.DMA
    smalls = [queries, keys, decay_t, lam, seg, table, skip, gain]
    scratch = [pltpu.VMEM(a.shape, a.dtype) for a in smalls] + [
        pltpu.VMEM((Z, A * oc, cg), bf16),
        pltpu.VMEM((A, tok, cg), bf16),
        pltpu.VMEM((A, tok, cg), bf16),
        pltpu.VMEM((A, 2, tok, state), bf16),
        pltpu.VMEM((A, hr + 8, tok), f32),
        pltpu.VMEM((A, hr + 8, tok), f32),
        pltpu.VMEM((A, hr, tok), f32),
        pltpu.VMEM((A, hr, tok), f32),
        pltpu.VMEM((A, sz.levels * hr, tok), f32),
        pltpu.VMEM((A, tok, cg), f32),
        [pltpu.VMEM((A >> b, state, cg), bf16) for b in range(a_bits)],
        pltpu.VMEM((state, cg), f32),
        pltpu.VMEM((z_bits, state, cg), bf16),
        pltpu.VMEM((z_bits, state, cg), bf16),
        pltpu.VMEM((z_bits, hr, tok), f32),
        pltpu.VMEM((z_bits, hr, tok), f32),
        pltpu.VMEM((A // 2, 2, tok, cg), bf16),
        pltpu.VMEM((A, 8, tok), f32),
        pltpu.VMEM((A, 8, tok), f32),
        pltpu.VMEM((A, tok, 128), f32),
        pltpu.VMEM((A, tok, cg), bf16),
        pltpu.VMEM((2 * hr, cg), bf16),
        stages(bf16),
        stages(bf16),
        stages(f32),
        dma((A,)), dma((A,)),
        dma((Z, A)), dma((Z, A)), dma((Z, A)), dma((Z, A)),
        dma((A,)), dma((A,)), dma((A,)), dma((A,)), dma((A,)), dma((A,)), dma((2, A)), dma((2, A)),
        dma((z_bits, Z, 2)), dma((z_bits, 2)), dma((z_bits, Z)), dma((z_bits,)),
        dma((A,)), dma((A,)),
        dma((a_bits, 2 * len(parts))), dma((a_bits, 2 * len(parts))),
        dma((len(smalls),)),
    ]
    return pl.pallas_call(
        lambda *refs: mixer_kernel(sz, *refs),
        out_shape=jax.ShapeDtypeStruct((tok, Z * A * oc), bf16),
        in_specs=[hbm] * 11,
        out_specs=vmem,
        scratch_shapes=scratch,
        name="mixer",
        cost_estimate=pl.CostEstimate(flops=1 << 32, bytes_accessed=32 << 20, transcendentals=1 << 21),
        compiler_params=pltpu.CompilerParams(
            collective_id=0, has_side_effects=True, vmem_limit_bytes=56 << 20
        ),
    )(wt, values, gates, queries, keys, decay_t, lam, seg, table, skip, gain)


def sizes_for(queries, values, log_decay, lam_table, out_proj):
    tok, state = queries.shape
    heads = log_decay.shape[1]
    count = lax.axis_size("seq")
    A = math.gcd(math.gcd(heads, 8), count)
    Z = count // A
    cg = values.shape[1] // A
    oc = out_proj.shape[1]
    fits = lax.axis_size("head") == 1 and A > 1 and Z > 1 and Z & (Z - 1) == 0
    fits = fits and cg % 128 == 0 and oc % 16 == 0 and (A * oc) % 128 == 0
    fits = fits and tok == 128 and state == 128 and -decay_floor * tok / 2 < 60
    if not fits:
        return None
    return Sizes(tok, state, cg, heads // A, oc, A, Z, lam_table.shape[1])


def split_device(
    queries,
    key_rows,
    values,
    gate_rows,
    log_decay,
    skip_gain,
    lam_index,
    segments,
    lam_table,
    norm_gain,
    out_proj,
):
    tok, state_dim = queries.shape
    head_count = log_decay.shape[1]
    cols = values.shape[1]
    head_dim = cols // head_count
    classes, level_count = lam_table.shape[:2]
    dev_count = lax.axis_size("seq")
    inner_total = cols * lax.axis_size("head")
    A = math.gcd(math.gcd(head_count, 8), dev_count)
    Z = dev_count // A
    a_bits = A.bit_length() - 1
    z_bits = Z.bit_length() - 1
    hg = head_count // A
    cg = hg * head_dim
    rows = A * tok
    out_cols = out_proj.shape[1]
    groups = [[z * A + i for i in range(A)] for z in range(Z)]
    me = lax.axis_index("seq")
    in_pos = lax.rem(me, A)
    z_pos = lax.div(me, A)

    def exchange(blocks):
        return lax.all_to_all(
            blocks, "seq", 0, 0, tiled=True, axis_index_groups=groups
        )

    def my_heads(array, width, axis):
        return lax.dynamic_slice_in_dim(array, in_pos * width, width, axis)

    w_blocks = out_proj.T.reshape(out_cols, A, cg).swapaxes(0, 1)
    w_block = exchange(w_blocks).reshape(A * out_cols, cg)

    packed = pack_call(
        queries,
        key_rows,
        values,
        log_decay,
        lam_index.astype(f32)[:, None],
        segments.astype(f32)[:, None],
        groups=A,
    )
    packed = exchange(packed)
    small = packed[:, :, 2 * state_dim + cg :].astype(f32)

    def shift(block, step):
        pairs = [(p, (p + step * A) % dev_count) for p in range(dev_count)]
        return lax.ppermute(block, "seq", pairs)

    w_ring = [(0, w_block)]
    above = below = w_block
    if Z > 1:
        above = shift(w_block, 1)
        w_ring.append((1, above))
    if Z > 2:
        below = shift(w_block, -1)
        w_ring.append((-1, below))

    cum = small[:, :, :hg] + small[:, :, hg : 2 * hg] + small[:, :, 2 * hg : 3 * hg]
    lam = small[:, :, 3 * hg].reshape(rows).astype(jnp.int32)
    seg = small[:, :, 3 * hg + 1]
    span = cum[:, -1, :]
    onehot = (lam[:, None] == jnp.arange(classes, dtype=jnp.int32)[None, :]).astype(f32)
    table = my_heads(lam_table, hg, 2).reshape(classes, level_count * hg)
    lw = jnp.dot(onehot, table, precision=highest).reshape(A, tok, level_count * hg)
    expand = (
        jnp.arange(hg, dtype=jnp.int32)[:, None]
        == jnp.arange(cg, dtype=jnp.int32)[None, :] // head_dim
    ).astype(bf16)

    total = span
    prefix = jnp.zeros((A, hg), f32)
    prefixes = []
    up_factors = []
    for b in range(a_bits):
        wide = 2**b
        low_total, up_total = total[0::2], total[1::2]
        is_up = (jnp.arange(A, dtype=jnp.int32) // wide % 2 == 1)[:, None]
        prefixes.append(jnp.where(is_up, prefix, -jnp.inf))
        up_factors.append(jnp.exp(up_total))
        prefix = prefix + jnp.where(is_up, jnp.repeat(low_total, 2 * wide, axis=0), 0.0)
        total = low_total + up_total
    total = total[0]

    def level_scale(before, level):
        weight = lw[:, :, (2 + level) * hg : (3 + level) * hg]
        return jnp.exp(cum + before[:, None, :]) * weight

    end_scale = jnp.exp(span[:, None, :] - cum)
    up_rows = jnp.concatenate(up_factors, axis=0)
    *level_states, state = state_call(
        packed, end_scale, up_rows, expand, state_dim=state_dim, bits=a_bits
    )
    gate_blocks = gate_rows.reshape(tok, A, cg).swapaxes(0, 1)
    gate_blocks, state, total = lax.optimization_barrier((gate_blocks, state, total))
    gates = exchange(gate_blocks)
    local_scales = [lw[:, :, : 2 * hg]]
    local_scales += [level_scale(before, b) for b, before in enumerate(prefixes)]
    local_scales = jnp.concatenate(local_scales, axis=2)

    others, other_scales = [], []
    for zb in range(z_bits):
        other = xor_permute(state, A << zb)
        other_total = xor_permute(total[None, :], A << zb)[0]
        is_up = jnp.bitwise_and(jnp.right_shift(z_pos, zb), 1) == 1
        others.append(other)
        before = jnp.where(is_up, prefix, -jnp.inf)
        other_scales.append(level_scale(before, a_bits + zb))
        if zb + 1 < z_bits:
            up_state = jnp.where(is_up, state, other).astype(f32)
            low_state = jnp.where(is_up, other, state).astype(f32)
            factor = widen(jnp.exp(jnp.where(is_up, total, other_total)), head_dim)
            state = (up_state + factor[None, :] * low_state).astype(bf16)
            prefix = prefix + jnp.where(is_up, other_total, 0.0)[None, :]
            total = total + other_total

    for distance in range(2, Z // 2 + 1):
        above, others = lax.optimization_barrier((above, others))
        above = shift(above, 1)
        w_ring.append((distance, above))
        if 2 * distance < Z:
            below = shift(below, -1)
            w_ring.append((-distance, below))

    skip = widen(my_heads(skip_gain, hg, 0), head_dim)[None, :]
    mixed = local_call(
        packed, cum, cum.swapaxes(1, 2), local_scales, seg, level_states, skip, expand,
        state_dim=state_dim, head_dim=head_dim,
    )
    gain = my_heads(norm_gain, cg, 0)[None, :]
    hidden, squares = gate_call(
        packed, mixed, others, other_scales, gates, gain, expand, state_dim=state_dim
    )

    def reduce_group(part, order, narrow):
        left = list(range(a_bits))[::-1]
        part = part.reshape((2,) * a_bits + part.shape[1:])
        for b in order:
            axis = left.index(b)
            left.remove(b)
            bit = jnp.bitwise_and(jnp.right_shift(in_pos, b), 1)
            mine = lax.dynamic_index_in_dim(part, bit, axis, keepdims=False)
            theirs = lax.dynamic_index_in_dim(part, 1 - bit, axis, keepdims=False)
            part = mine + xor_permute(theirs.astype(narrow), 2**b).astype(f32)
        return part

    bits = list(range(a_bits))
    flipped = bits[:1] + bits[1:][::-1]
    square_sum = reduce_group(squares.reshape(A, tok), bits, f32)
    square_sum = lax.psum(square_sum, "head")
    inv_rms = lax.rsqrt(square_sum / inner_total + epsilon)[:, None]
    block_cols = A * out_cols
    out = jnp.zeros((tok, Z * block_cols), bf16)
    for step, (distance, w_part) in enumerate(w_ring):
        part = lax.dot_general(
            hidden, w_part, (((1,), (1,)), ((), ())), preferred_element_type=f32
        )
        part = reduce_group(
            part.reshape(A, tok, block_cols), flipped if step % 2 else bits, bf16
        )
        block = lax.rem(z_pos - distance + Z, Z)
        out = lax.dynamic_update_slice_in_dim(
            out, (part * inv_rms).astype(bf16), block * block_cols, 1
        )
    return lax.psum_scatter(out, "head", scatter_dimension=0, tiled=True)


def per_device(
    queries,
    key_rows,
    values,
    gate_rows,
    log_decay,
    skip_gain,
    lam_index,
    segments,
    lam_table,
    norm_gain,
    out_proj,
):
    sz = sizes_for(queries, values, log_decay, lam_table, out_proj)
    if sz is None:
        return split_device(
            queries, key_rows, values, gate_rows, log_decay, skip_gain,
            lam_index, segments, lam_table, norm_gain, out_proj,
        )
    return mixer_call(
        sz,
        out_proj.T,
        values,
        gate_rows,
        queries,
        key_rows,
        log_decay.T,
        lam_index[None, :],
        segments[None, :],
        lam_table.transpose(1, 0, 2),
        skip_gain[None, :],
        norm_gain[None, :],
    )


def solution(mesh):
    return jax.shard_map(
        per_device,
        mesh=mesh,
        in_specs=(
            P("seq", None),
            P("seq", None),
            P("seq", "head"),
            P("seq", "head"),
            P("seq", "head"),
            P("head"),
            P("seq"),
            P("seq"),
            P(None, None, "head"),
            P("head"),
            P("head", "seq"),
        ),
        out_specs=P(("seq", "head"), None),
        check_vma=False,
    )
```
